32 devices in a mesh: fsdp: 8 (over z, x), ctx: 2 (over y), tp: 2 (over core).
Axes of the slice: x: 2, y: 2, z: 4, core: 2. Of those that a mesh axis runs over, the one named last changes fastest.
Arguments:
- tokens: bfloat16 [1024, 8, 1024], P('ctx', 'fsdp'), may hold values from -6 to 6
- segment_ids: int32 [8, 1024], P('fsdp', 'ctx'), may hold values from 0 to 31, never falling along the last dimension, each value on 1 to 768 neighbouring positions
- w_query: bfloat16 [1024, 1024], P('fsdp', 'tp'), may hold values from -0.1875 to 0.1875
- w_key: bfloat16 [1024, 1024], P('fsdp', 'tp'), may hold values from -0.1875 to 0.1875
- w_value: bfloat16 [1024, 1024], P('fsdp', 'tp'), may hold values from -0.1875 to 0.1875
- w_out: bfloat16 [1024, 1024], P('tp', 'fsdp'), may hold values from -0.75 to 0.75
- w_gate: bfloat16 [1024, 4096], P('fsdp', 'tp'), may hold values from -0.1875 to 0.1875
- w_up: bfloat16 [1024, 4096], P('fsdp', 'tp'), may hold values from -0.1875 to 0.1875
- w_down: bfloat16 [4096, 1024], P('tp', 'fsdp'), may hold values from -0.09375 to 0.09375
- gain_attn: bfloat16 [1024], P('fsdp'), may hold values from 0.25 to 1.75
- gain_ffn: bfloat16 [1024], P('fsdp'), may hold values from 0.25 to 1.75
- cotangent: bfloat16 [1024, 8, 1024], P('ctx', 'fsdp'), may hold values from -6 to 6
Outputs:
- output: bfloat16 [1024, 8, 1024], P('ctx', 'fsdp')
- grad_tokens: bfloat16 [1024, 8, 1024], P('ctx', 'fsdp')
- grad_query: float32 [1024, 1024], P('fsdp', 'tp')
- grad_key: float32 [1024, 1024], P('fsdp', 'tp')
- grad_value: float32 [1024, 1024], P('fsdp', 'tp')
- grad_out: float32 [1024, 1024], P('tp', 'fsdp')
- grad_gate: float32 [1024, 4096], P('fsdp', 'tp')
- grad_up: float32 [1024, 4096], P('fsdp', 'tp')
- grad_down: float32 [4096, 1024], P('tp', 'fsdp')
- grad_gain_attn: float32 [1024], P('fsdp')
- grad_gain_ffn: float32 [1024], P('fsdp')
The draws below stay inside these ranges and needn't reach their ends.
Inputs may be any that keep to these rules, and one draw needn't show every extreme that they name: `segment_ids`: within a sequence the segment id never falls from one position to the next; each document holds 1 to 768 positions and in each sequence one holds exactly that many.
All inputs are finite; a program needn't handle non-finite values.
Results may differ from the reference program's by a relative error of at most 0.017.
Values may be sent and summed in bfloat16 or wider, within the bound.
A program may use at most 192 MiB of HBM per device.

```python
import math
import jax
import jax.numpy as jnp
import numpy as np
from jax import lax

D = 1024
FF = 4096
HEADS = 16
HEAD_DIM = 64
SEQ_LEN = 1024
NSEQ = 8


def level_of(own_key, extent, cuts, low, high):
    factor_of = 1.0
    for position, shards_of in cuts:
        draws = jax.random.uniform(jax.random.fold_in(jax.random.fold_in(own_key, 6), position), (shards_of,), jnp.float32, low / len(cuts), high / len(cuts))
        factor_of = factor_of * jnp.repeat(jnp.exp(draws), extent[position] // shards_of).reshape((-1,) + (1,) * (len(extent) - 1 - position))
    return factor_of


def split_up(amount, total, limit, skew):
    loads = [(1 << 20) // math.isqrt(rank ** skew) + 1 for rank in range(2, amount + 1)]
    rest, given = total - limit - (amount - 1), [1] * (amount - 1)
    while rest > 0:
        movable = [i for i in range(amount - 1) if given[i] < limit]
        pool, left = sum([loads[i] for i in movable]), rest
        for i in movable:
            addition = min(limit - given[i], max(1, left * loads[i] // pool), rest)
            given[i] = given[i] + addition
            rest = rest - addition
    return np.array([limit] + given)


def uneven(stream_key, count, total, reach, lean):
    if count == 2:
        one = jax.random.randint(stream_key, (), max(1, total - reach), min(reach, total - 1) + 1)
        return jnp.stack([one, total - one])
    sizes = jnp.asarray(split_up(count, total, reach, lean), jnp.int32)
    couples = (count - 1) // 2
    giver, receiver = sizes[1:1 + 2 * couples:2], sizes[2:2 + 2 * couples:2]
    margin = jnp.minimum(giver - 1, reach - receiver)
    shifted = jax.random.randint(jax.random.fold_in(stream_key, 1), (couples,), 0, 1 << 20) % (margin + 1)
    sizes = sizes.at[1:1 + 2 * couples:2].set(giver - shifted).at[2:2 + 2 * couples:2].set(receiver + shifted)
    return sizes[jax.random.permutation(jax.random.fold_in(stream_key, 2), count)]


def normal_values(key, shape, deviation, reach, pieces=(), kind=jnp.bfloat16):
    array = deviation * jax.random.normal(key, shape, jnp.float32)
    if pieces:
        array = array * level_of(key, shape, pieces, -0.22, 0.18)
    return jnp.clip(array, -reach, reach).astype(kind)


def setup_inputs(seed: int = 0) -> dict:
    key_of = jax.random.split(jax.random.key(seed), 13)
    tokens = normal_values(key_of[0], (SEQ_LEN, NSEQ, D), 1.0, 6.0, ((0, 2), (1, 8)))
    segment_ids = jax.vmap(lambda own: jnp.searchsorted(jnp.cumsum(uneven(own, max(2, SEQ_LEN // 32), SEQ_LEN, 3 * SEQ_LEN // 4, 2)), jnp.arange(SEQ_LEN), side="right"))(jax.random.split(key_of[1], NSEQ)).reshape((NSEQ, SEQ_LEN)).astype(jnp.int32)
    w_query = normal_values(key_of[2], (D, D), D ** -0.5, 0.1875, ((0, 8), (1, 2)))
    w_key = normal_values(key_of[3], (D, D), D ** -0.5, 0.1875, ((0, 8), (1, 2)))
    w_value = normal_values(key_of[4], (D, D), D ** -0.5, 0.1875, ((0, 8), (1, 2)))
    w_out = normal_values(key_of[5], (D, D), (D // 16) ** -0.5, 0.75, ((0, 2), (1, 8)))
    w_gate = normal_values(key_of[6], (D, FF), D ** -0.5, 0.1875, ((0, 8), (1, 2)))
    w_up = normal_values(key_of[7], (D, FF), D ** -0.5, 0.1875, ((0, 8), (1, 2)))
    w_down = normal_values(key_of[8], (FF, D), FF ** -0.5, 0.09375, ((0, 2), (1, 8)))
    gain_attn = jnp.clip(1.0 + 0.15 * jax.random.normal(key_of[9], (D,), jnp.float32), 0.25, 1.75).astype(jnp.bfloat16)
    gain_ffn = jnp.clip(1.0 + 0.15 * jax.random.normal(key_of[10], (D,), jnp.float32), 0.25, 1.75).astype(jnp.bfloat16)
    cotangent = normal_values(key_of[11], (SEQ_LEN, NSEQ, D), 1.0, 6.0, ((0, 2), (1, 8)))
    return dict(tokens=tokens, segment_ids=segment_ids, w_query=w_query, w_key=w_key, w_value=w_value, w_out=w_out, w_gate=w_gate, w_up=w_up, w_down=w_down, gain_attn=gain_attn, gain_ffn=gain_ffn, cotangent=cotangent)


EPSILON = 1e-05
SCALE = 0.125
MASKED = -1e+30

@jax.custom_vjp
def low(v):
    return lax.optimization_barrier(v.astype(jnp.bfloat16)).astype(jnp.float32)

@jax.custom_vjp
def low_back(v):
    return v

def low_keep(v):
    return (low(v), None)

def low_pass(kept, grad):
    return (grad,)

def back_keep(v):
    return (v, None)

def back_low(kept, grad):
    return (low(grad),)
low.defvjp(low_keep, low_pass)
low_back.defvjp(back_keep, back_low)

def rms_norm(values, gain):
    return values * lax.rsqrt(lax.optimization_barrier(jnp.mean(values * values, axis=-1, keepdims=True)) + EPSILON) * gain

def project(values, weight):
    return jnp.einsum('lsd,de->lse', values, weight, precision=lax.Precision.HIGHEST)

def to_heads(values):
    length, group, width = values.shape
    return jnp.moveaxis(values.reshape(length, group, HEADS, HEAD_DIM), 2, 0)

def layer(seg, values, weights):
    w_query, w_key, w_value, w_out, w_gate, w_up, w_down, gain_attn, gain_ffn = weights
    length = values.shape[0]
    hidden_one = low(rms_norm(values, gain_attn))
    query = low(low_back(project(hidden_one, w_query)))
    keys = low(low_back(project(hidden_one, w_key)))
    vals = low(low_back(project(hidden_one, w_value)))
    where_pos = jnp.arange(length, dtype=jnp.int32)
    allowed = (where_pos[None, None, :] <= where_pos[None, :, None]) & (seg[:, :, None] == seg[:, None, :])

    def one_head(parts):
        q_head, k_head, v_head = parts
        scores = low_back(jnp.einsum('qsd,ksd->sqk', q_head, k_head, precision=lax.Precision.HIGHEST) * SCALE)
        scores = jnp.where(allowed, scores, MASKED)
        row_max = lax.optimization_barrier(jnp.max(scores, axis=-1, keepdims=True))
        expo = jnp.exp(scores - row_max)
        probs = low(expo / lax.optimization_barrier(jnp.sum(expo, axis=-1, keepdims=True)))
        return jnp.einsum('sqk,ksd->qsd', probs, v_head, precision=lax.Precision.HIGHEST)
    heads_out = lax.map(jax.checkpoint(one_head), (to_heads(query), to_heads(keys), to_heads(vals)))
    mixed = jnp.moveaxis(heads_out, 0, 2).reshape(values.shape)
    mixed = low(low_back(mixed))
    resid = values + low_back(project(mixed, w_out))
    hidden_two = low(rms_norm(resid, gain_ffn))
    gate = low_back(project(hidden_two, w_gate))
    upward = low_back(project(hidden_two, w_up))
    swish_up = low(gate * jax.nn.sigmoid(gate) * upward)
    return resid + low_back(project(swish_up, w_down))

def reference(tokens, segment_ids, w_query, w_key, w_value, w_out, w_gate, w_up, w_down, gain_attn, gain_ffn, cotangent):
    params = tuple((item.astype(jnp.float32) for item in (w_query, w_key, w_value, w_out, w_gate, w_up, w_down, gain_attn, gain_ffn)))
    group = 4 if NSEQ % 4 == 0 else 1
    blocks = NSEQ // group
    inputs = jnp.moveaxis(tokens.astype(jnp.float32).reshape(SEQ_LEN, blocks, group, D), 1, 0)
    seg_blocks = segment_ids.reshape(blocks, group, SEQ_LEN)
    cot_blocks = jnp.moveaxis(cotangent.astype(jnp.float32).reshape(SEQ_LEN, blocks, group, D), 1, 0)

    def step(totals, item):
        values, seg, cot = item

        def forward(inner_values, *weights):
            return layer(seg, inner_values, weights)
        result, pull = jax.vjp(forward, values, *params)
        grads = pull(cot)
        new_totals = tuple((total + grad for total, grad in zip(totals, grads[1:])))
        return (new_totals, (result.astype(jnp.bfloat16), grads[0].astype(jnp.bfloat16)))
    start = tuple((jnp.zeros_like(item) for item in params))
    totals, (outputs, input_grads) = lax.scan(step, start, (inputs, seg_blocks, cot_blocks))
    output = jnp.moveaxis(outputs, 0, 1).reshape(SEQ_LEN, NSEQ, D)
    grad_tokens = jnp.moveaxis(input_grads, 0, 1).reshape(SEQ_LEN, NSEQ, D)
    return (output, grad_tokens, totals[0], totals[1], totals[2], totals[3], totals[4], totals[5], totals[6], totals[7], totals[8])
```

```python
import functools

import jax
import jax.numpy as jnp
from jax import lax
from jax.experimental import pallas as pl
from jax.experimental.pallas import tpu as pltpu
from jax.sharding import PartitionSpec as P

HEAD_DIM = 64


EPSILON = 1e-05
SCALE = 0.125
MASKED = -1e30


def normalize(values):
    inverse = lax.rsqrt(jnp.mean(values * values, axis=-1, keepdims=True) + EPSILON)
    return (values * inverse, inverse)


def norm_back(grad_normed, normed, inverse):
    return inverse * (grad_normed - normed * jnp.mean(grad_normed * normed, axis=-1, keepdims=True))


def inner_rows(left, right):
    return lax.dot_general(
        left, right, (((0,), (0,)), ((), ())), preferred_element_type=jnp.float32
    )


def times_transposed(left, weight):
    return lax.dot_general(
        left, weight, (((1,), (1,)), ((), ())), preferred_element_type=jnp.float32
    )


def head_sum(partial_sum):
    return lax.psum(partial_sum, "tp")


def split_heads(values, head_size):
    length, sequences, width = values.shape
    return jnp.moveaxis(values.reshape(length, sequences, width // head_size, head_size), 2, 0)


def join_heads(values):
    heads, length, sequences, head_size = values.shape
    return jnp.moveaxis(values, 0, 2).reshape(length, sequences, heads * head_size)


def make_mask(query_pos, query_seg, key_pos, key_seg):
    before = key_pos[None, None, :] <= query_pos[None, :, None]
    same = query_seg.T[:, :, None] == key_seg.T[:, None, :]
    return before & same


def key_head_grads(parts, use_mask):
    q_head, k_head, v_head, d_head, log_total, delta = parts
    scores = jnp.einsum("qsd,ksd->sqk", q_head, k_head, preferred_element_type=jnp.float32) * SCALE
    probs = jnp.exp(jnp.where(use_mask, scores, MASKED) - log_total)
    grad_probs = jnp.einsum("qsd,ksd->sqk", d_head, v_head, preferred_element_type=jnp.float32)
    grad_scores = (probs * (grad_probs - delta)).astype(jnp.bfloat16)
    grad_v = jnp.einsum(
        "sqk,qsd->ksd", probs.astype(jnp.bfloat16), d_head, preferred_element_type=jnp.float32
    )
    grad_k = (
        jnp.einsum("sqk,qsd->ksd", grad_scores, q_head, preferred_element_type=jnp.float32) * SCALE
    )
    return (grad_k, grad_v)


def local(
    tokens,
    segment_ids,
    w_query,
    w_key,
    w_value,
    w_out,
    w_gate,
    w_up,
    w_down,
    gain_attn,
    gain_ffn,
    cotangent,
):
    local_len, sequences, width = tokens.shape
    rows = local_len * sequences
    (
        full_query,
        full_key,
        full_value,
        full_out,
        full_gate,
        full_up,
        full_down,
        full_gain_one,
        full_gain_two,
    ) = (
        lax.all_gather(w_query, "fsdp", axis=0, tiled=True),
        lax.all_gather(w_key, "fsdp", axis=0, tiled=True),
        lax.all_gather(w_value, "fsdp", axis=0, tiled=True),
        lax.all_gather(w_out, "fsdp", axis=1, tiled=True),
        lax.all_gather(w_gate, "fsdp", axis=0, tiled=True),
        lax.all_gather(w_up, "fsdp", axis=0, tiled=True),
        lax.all_gather(w_down, "fsdp", axis=1, tiled=True),
        lax.all_gather(gain_attn, "fsdp", axis=0, tiled=True),
        lax.all_gather(gain_ffn, "fsdp", axis=0, tiled=True),
    )
    gain_one = full_gain_one.astype(jnp.float32)
    gain_two = full_gain_two.astype(jnp.float32)
    head_width = full_query.shape[1]
    flat = tokens.astype(jnp.float32).reshape(rows, width)
    normed_one, inverse_one = normalize(flat)
    hidden_one = (normed_one * gain_one).astype(jnp.bfloat16)
    query = (
        jnp.dot(hidden_one, full_query, preferred_element_type=jnp.float32)
        .astype(jnp.bfloat16)
        .reshape(local_len, sequences, head_width)
    )
    keys = (
        jnp.dot(hidden_one, full_key, preferred_element_type=jnp.float32)
        .astype(jnp.bfloat16)
        .reshape(local_len, sequences, head_width)
    )
    vals = (
        jnp.dot(hidden_one, full_value, preferred_element_type=jnp.float32)
        .astype(jnp.bfloat16)
        .reshape(local_len, sequences, head_width)
    )
    pair = jnp.concatenate([keys, vals], axis=-1)
    seg_local = segment_ids.T
    pair_all, seg_all = (
        lax.all_gather(pair, "ctx", axis=0, tiled=True),
        lax.all_gather(seg_local, "ctx", axis=0, tiled=True),
    )
    length = pair_all.shape[0]
    query_pos = lax.axis_index("ctx") * local_len + jnp.arange(local_len, dtype=jnp.int32)
    all_pos = jnp.arange(length, dtype=jnp.int32)
    mask = make_mask(query_pos, seg_local, all_pos, seg_all)
    q_heads = split_heads(query, HEAD_DIM)
    k_heads = split_heads(pair_all[..., :head_width], HEAD_DIM)
    v_heads = split_heads(pair_all[..., head_width:], HEAD_DIM)

    def attend(parts):
        q_head, k_head, v_head = parts
        scores = (
            jnp.einsum("qsd,ksd->sqk", q_head, k_head, preferred_element_type=jnp.float32) * SCALE
        )
        scores = jnp.where(mask, scores, MASKED)
        row_max = jnp.max(scores, axis=-1, keepdims=True)
        log_total = row_max + jnp.log(jnp.sum(jnp.exp(scores - row_max), axis=-1, keepdims=True))
        probs = jnp.exp(scores - log_total).astype(jnp.bfloat16)
        return (
            jnp.einsum("sqk,ksd->qsd", probs, v_head, preferred_element_type=jnp.float32),
            log_total,
        )

    attended, log_totals = lax.map(attend, (q_heads, k_heads, v_heads))
    mixed = join_heads(attended).astype(jnp.bfloat16).reshape(rows, head_width)
    resid = flat + head_sum(jnp.dot(mixed, full_out, preferred_element_type=jnp.float32))
    normed_two, inverse_two = normalize(resid)
    hidden_two = (normed_two * gain_two).astype(jnp.bfloat16)
    gate = jnp.dot(hidden_two, full_gate, preferred_element_type=jnp.float32)
    upward = jnp.dot(hidden_two, full_up, preferred_element_type=jnp.float32)
    sigmoid_gate = jax.nn.sigmoid(gate)
    swish_up = (gate * sigmoid_gate * upward).astype(jnp.bfloat16)
    result = resid + head_sum(jnp.dot(swish_up, full_down, preferred_element_type=jnp.float32))
    output = result.astype(jnp.bfloat16).reshape(local_len, sequences, width)
    (
        full_query,
        full_key,
        full_value,
        full_out,
        full_gate,
        full_up,
        full_down,
        full_gain_one,
        full_gain_two,
    ) = (
        lax.all_gather(w_query, "fsdp", axis=0, tiled=True),
        lax.all_gather(w_key, "fsdp", axis=0, tiled=True),
        lax.all_gather(w_value, "fsdp", axis=0, tiled=True),
        lax.all_gather(w_out, "fsdp", axis=1, tiled=True),
        lax.all_gather(w_gate, "fsdp", axis=0, tiled=True),
        lax.all_gather(w_up, "fsdp", axis=0, tiled=True),
        lax.all_gather(w_down, "fsdp", axis=1, tiled=True),
        lax.all_gather(gain_attn, "fsdp", axis=0, tiled=True),
        lax.all_gather(gain_ffn, "fsdp", axis=0, tiled=True),
    )
    gain_one = full_gain_one.astype(jnp.float32)
    gain_two = full_gain_two.astype(jnp.float32)
    grad_result = cotangent.astype(jnp.float32).reshape(rows, width)
    grad_low = grad_result.astype(jnp.bfloat16)
    grad_wdown = inner_rows(swish_up, grad_low)
    grad_swish = times_transposed(grad_low, full_down)
    grad_gate_act = (
        grad_swish * upward * sigmoid_gate * (1.0 + gate * (1.0 - sigmoid_gate))
    ).astype(jnp.bfloat16)
    grad_upward = (grad_swish * gate * sigmoid_gate).astype(jnp.bfloat16)
    grad_wgate = inner_rows(hidden_two, grad_gate_act)
    grad_wup = inner_rows(hidden_two, grad_upward)
    grad_hidden_two = head_sum(
        times_transposed(grad_gate_act, full_gate) + times_transposed(grad_upward, full_up)
    )
    grad_gain_two = jnp.sum(grad_hidden_two * normed_two, axis=0)
    grad_resid = grad_result + norm_back(grad_hidden_two * gain_two, normed_two, inverse_two)
    grad_branch = grad_resid.astype(jnp.bfloat16)
    grad_wout = inner_rows(mixed, grad_branch)
    grad_mixed = (
        times_transposed(grad_branch, full_out)
        .astype(jnp.bfloat16)
        .reshape(local_len, sequences, head_width)
    )
    d_heads = split_heads(grad_mixed, HEAD_DIM)

    def query_side(parts):
        q_head, k_head, v_head, d_head, log_total = parts
        scores = (
            jnp.einsum("qsd,ksd->sqk", q_head, k_head, preferred_element_type=jnp.float32) * SCALE
        )
        probs = jnp.exp(jnp.where(mask, scores, MASKED) - log_total)
        grad_probs = jnp.einsum("qsd,ksd->sqk", d_head, v_head, preferred_element_type=jnp.float32)
        delta = jnp.sum(probs * grad_probs, axis=-1, keepdims=True)
        grad_scores = (probs * (grad_probs - delta)).astype(jnp.bfloat16)
        return (
            jnp.einsum("sqk,ksd->qsd", grad_scores, k_head, preferred_element_type=jnp.float32)
            * SCALE,
            delta,
        )

    grad_q_heads, deltas = lax.map(query_side, (q_heads, k_heads, v_heads, d_heads, log_totals))
    grad_query = join_heads(grad_q_heads).astype(jnp.bfloat16).reshape(rows, head_width)
    piece_mask = make_mask(
        query_pos, seg_local, jnp.arange(local_len * lax.axis_size("ctx"), dtype=jnp.int32), seg_all
    )
    k_piece = split_heads(pair_all[..., :head_width], HEAD_DIM)
    v_piece = split_heads(pair_all[..., head_width:], HEAD_DIM)

    def per_head(parts):
        return key_head_grads(parts, piece_mask)

    grad_k_heads, grad_v_heads = lax.map(
        per_head, (q_heads, k_piece, v_piece, d_heads, log_totals, deltas)
    )
    grad_pair = lax.psum_scatter(
        jnp.concatenate([join_heads(grad_k_heads), join_heads(grad_v_heads)], axis=-1).astype(
            jnp.bfloat16
        ),
        "ctx",
        scatter_dimension=0,
        tiled=True,
    ).astype(jnp.float32)
    grad_keys = grad_pair[..., :head_width].astype(jnp.bfloat16).reshape(rows, head_width)
    grad_vals = grad_pair[..., head_width:].astype(jnp.bfloat16).reshape(rows, head_width)
    grad_wquery = inner_rows(hidden_one, grad_query)
    grad_wkey = inner_rows(hidden_one, grad_keys)
    grad_wvalue = inner_rows(hidden_one, grad_vals)
    grad_hidden_one = head_sum(
        times_transposed(grad_query, full_query)
        + times_transposed(grad_keys, full_key)
        + times_transposed(grad_vals, full_value)
    )
    grad_gain_one = jnp.sum(grad_hidden_one * normed_one, axis=0)
    grad_input = grad_resid + norm_back(grad_hidden_one * gain_one, normed_one, inverse_one)
    grad_input = grad_input.astype(jnp.bfloat16).reshape(local_len, sequences, width)
    shares = (
        lax.psum_scatter(
            grad_wquery.astype(jnp.bfloat16), "fsdp", scatter_dimension=0, tiled=True
        ).astype(jnp.float32),
        lax.psum_scatter(
            grad_wkey.astype(jnp.bfloat16), "fsdp", scatter_dimension=0, tiled=True
        ).astype(jnp.float32),
        lax.psum_scatter(
            grad_wvalue.astype(jnp.bfloat16), "fsdp", scatter_dimension=0, tiled=True
        ).astype(jnp.float32),
        lax.psum_scatter(
            grad_wout.astype(jnp.bfloat16), "fsdp", scatter_dimension=1, tiled=True
        ).astype(jnp.float32),
        lax.psum_scatter(
            grad_wgate.astype(jnp.bfloat16), "fsdp", scatter_dimension=0, tiled=True
        ).astype(jnp.float32),
        lax.psum_scatter(
            grad_wup.astype(jnp.bfloat16), "fsdp", scatter_dimension=0, tiled=True
        ).astype(jnp.float32),
        lax.psum_scatter(
            grad_wdown.astype(jnp.bfloat16), "fsdp", scatter_dimension=1, tiled=True
        ).astype(jnp.float32),
        lax.psum_scatter(
            grad_gain_one.astype(jnp.bfloat16), "fsdp", scatter_dimension=0, tiled=True
        ).astype(jnp.float32),
        lax.psum_scatter(
            grad_gain_two.astype(jnp.bfloat16), "fsdp", scatter_dimension=0, tiled=True
        ).astype(jnp.float32),
    )
    shares = (
        lax.psum(shares[0].astype(jnp.bfloat16), "ctx").astype(jnp.float32),
        lax.psum(shares[1].astype(jnp.bfloat16), "ctx").astype(jnp.float32),
        lax.psum(shares[2].astype(jnp.bfloat16), "ctx").astype(jnp.float32),
        lax.psum(shares[3].astype(jnp.bfloat16), "ctx").astype(jnp.float32),
        lax.psum(shares[4].astype(jnp.bfloat16), "ctx").astype(jnp.float32),
        lax.psum(shares[5].astype(jnp.bfloat16), "ctx").astype(jnp.float32),
        lax.psum(shares[6].astype(jnp.bfloat16), "ctx").astype(jnp.float32),
        lax.psum(shares[7].astype(jnp.bfloat16), "ctx").astype(jnp.float32),
        lax.psum(shares[8].astype(jnp.bfloat16), "ctx").astype(jnp.float32),
    )
    return (
        output,
        grad_input,
        shares[0],
        shares[1],
        shares[2],
        shares[3],
        shares[4],
        shares[5],
        shares[6],
        shares[7],
        shares[8],
    )


BF = jnp.bfloat16
F32 = jnp.float32
I32 = jnp.int32
MESH = pl.DeviceIdType.MESH
BLOCK = 256
VMEM_BYTES = 67043328


def dot_nn(left, right):
    return jnp.dot(left, right, preferred_element_type=F32)


def dot_nt(left, right):
    return lax.dot_general(left, right, (((1,), (1,)), ((), ())), preferred_element_type=F32)


def dot_tn(left, right):
    return lax.dot_general(left, right, (((0,), (0,)), ((), ())), preferred_element_type=F32)


def loop(count, body):
    def step(index, carry):
        body(index)
        return carry

    lax.fori_loop(0, count, step, 0)


def tile(index, size):
    return pl.ds(pl.multiple_of(index * size, size), size)


def only_half(values, half):
    lane = lax.broadcasted_iota(I32, values.shape, 1)
    keep = (lane < HEAD_DIM) if half == 0 else (lane >= HEAD_DIM)
    return jnp.where(keep, values, jnp.zeros_like(values))


def write_bias(bias, seg_col, seg_row, block, length):
    lanes = tile(block, BLOCK)
    keys = seg_col[0:length, :]
    key_pos = lax.broadcasted_iota(I32, (length, BLOCK), 0)
    query_pos = lax.broadcasted_iota(I32, (length, BLOCK), 1) + block * BLOCK
    same = jnp.concatenate([keys, keys], axis=1) == seg_row[0:1, lanes]
    bias[0:length, :] = jnp.where(same & (key_pos <= query_pos), 0.0, MASKED)


def attend_block(block, length, pairs, query, keys, vals_t, bias, seg_col, seg_row, mixed, mixed_t, log_sum):
    write_bias(bias, seg_col, seg_row, block, length)
    rows = tile(block, BLOCK)

    def pair(index):
        cols = tile(index, 2 * HEAD_DIM)
        two = query[rows, cols]
        for half in (0, 1):
            scores = dot_nt(keys[0:length, cols], only_half(two, half)) + bias[0:length, :]
            top = jnp.max(scores, axis=0, keepdims=True)
            expo = jnp.exp(scores - top)
            total = jnp.sum(expo, axis=0, keepdims=True)
            log_sum[2 * index + half, :, rows] = jnp.broadcast_to(top + jnp.log(total), (8, BLOCK))
            probs = (expo * (1.0 / total)).astype(BF)
            head = tile(2 * index + half, HEAD_DIM)
            mixed_t[head, :] = dot_nn(vals_t[head, 0:length], probs)

    loop(pairs, pair)
    mixed[rows, :] = mixed_t[...].T.astype(BF)


def attend_back_block(
    block, length, pairs, query, keys, keys_t, vals, grad_mixed, bias, seg_col, seg_row, log_sum, grad_qkv, grad_q_t, grad_k, grad_v
):
    write_bias(bias, seg_col, seg_row, block, length)
    rows = tile(block, BLOCK)

    def pair(index):
        cols = tile(index, 2 * HEAD_DIM)
        two = query[rows, cols]
        grad_two = grad_mixed[rows, cols]
        for half in (0, 1):
            one = only_half(two, half)
            grad_one = only_half(grad_two, half)
            scores = dot_nt(keys[0:length, cols], one) + bias[0:length, :]
            probs = jnp.exp(scores - log_sum[2 * index + half, 0:1, rows])
            grad_probs = dot_nt(vals[0:length, cols], grad_one)
            delta = jnp.sum(probs * grad_probs, axis=0, keepdims=True)
            grad_scores = (probs * (grad_probs - delta)).astype(BF)
            grad_v[0:length, cols] += dot_nn(probs.astype(BF), grad_one)
            grad_k[0:length, cols] += dot_nn(grad_scores, one)
            head = tile(2 * index + half, HEAD_DIM)
            grad_q_t[head, :] = dot_nn(keys_t[head, 0:length], grad_scores)

    loop(pairs, pair)
    grad_qkv[rows, 0 : grad_q_t.shape[0]] = (grad_q_t[...].T * SCALE).astype(BF)


def layer_kernel(
    nz,
    tok, cot, seg, gains, w_q, w_k, w_v, w_o, w_g, w_u, w_d,
    out, g_tok, o_q, o_k, o_v, o_o, o_g, o_u, o_d, o_gain,
    xg, cg, seg_row, gain_all, wqkv, wo, wg, wu, wd,
    h1, h2, ab, query, keys, vals, keys_t, vals_t, mixed, grad_mixed, grad_qkv, grad_k, grad_v,
    act_g, act_u, act_m, y1, bias, mixed_t, log_sum, seg_col,
    part, pair_sum, from_core, from_y, final_rows,
    p_d, p_g, p_u, p_o, p_qkv, r_d, r_g, r_u, r_o, r_qkv, s_d, s_g, s_u, s_o, s_qkv, f_d, f_g, f_u, f_o, f_qkv,
    p_n, r_n, s_n, f_n, c_n, y_n,
    send_sems, recv_sems, local_sems,
):
    fs = lax.axis_index("fsdp")
    y = lax.axis_index("ctx")
    t = lax.axis_index("tp")
    z = fs // 2
    x = lax.rem(fs, 2)
    width = xg.shape[1]
    half_len = xg.shape[0] // 2
    quarter = half_len // 2
    heads_w = query.shape[1]
    hidden = act_m.shape[1]
    db = width // (2 * nz)

    def dev(fq, yq, tq):
        return {"fsdp": fq, "ctx": yq, "tp": tq}

    x_dev = dev(2 * z + (1 - x), y, t)
    y_dev = dev(fs, 1 - y, t)
    c_dev = dev(fs, y, 1 - t)

    def z_of(k):
        return lax.rem(z + k, nz)

    def z_from(k):
        return lax.rem(z + nz - k, nz)

    def z_dev(k):
        return dev(2 * z_of(k) + x, y, t)

    barrier = pltpu.get_barrier_semaphore()
    for peer in [x_dev, y_dev, c_dev] + [z_dev(k) for k in range(1, nz)]:
        pl.semaphore_signal(barrier, inc=1, device_id=peer, device_id_type=MESH)
    pl.semaphore_wait(barrier, nz + 2)

    count = {"send": 0, "recv": 0, "local": 0}
    sent = []

    def new(kind):
        count[kind] += 1
        return count[kind] - 1

    def send(src, dst, device, ridx):
        copy = pltpu.make_async_remote_copy(
            src, dst, send_sems.at[new("send")], recv_sems.at[ridx], device_id=device, device_id_type=MESH
        )
        copy.start()
        sent.append(copy)
        return copy

    def recv(dst, ridx):
        pltpu.make_async_remote_copy(
            dst, dst, send_sems.at[0], recv_sems.at[ridx], device_id=y_dev, device_id_type=MESH
        ).wait_recv()

    def local(src, dst):
        copy = pltpu.make_async_copy(src, dst, local_sems.at[new("local")])
        copy.start()
        return copy

    def many(number):
        return [new("recv") for _ in range(number)]

    def drain(copies):
        for copy in copies:
            copy.wait_send()
        gone = {id(copy) for copy in copies}
        sent[:] = [copy for copy in sent if id(copy) not in gone]

    hw = pl.ds(pl.multiple_of(y * heads_w, heads_w), heads_w)
    uw = pl.ds(pl.multiple_of(y * hidden, hidden), hidden)

    def rb(fq):
        return tile(fq, db)

    names = {
        "n": (gains, lambda fq: gain_all.at[fq]),
        "q": (w_q.at[:, hw], lambda fq: wqkv.at[rb(fq), 0:heads_w]),
        "k": (w_k.at[:, hw], lambda fq: wqkv.at[rb(fq), heads_w : 2 * heads_w]),
        "v": (w_v.at[:, hw], lambda fq: wqkv.at[rb(fq), 2 * heads_w : 3 * heads_w]),
        "o": (w_o.at[hw, :], lambda fq: wo.at[:, rb(fq)]),
        "g": (w_g.at[:, uw], lambda fq: wg.at[rb(fq), :]),
        "u": (w_u.at[:, uw], lambda fq: wu.at[rb(fq), :]),
        "d": (w_d.at[uw, :], lambda fq: wd.at[:, rb(fq)]),
    }
    z_recv = {name: [None] + many(nz - 1) for name in names}
    x_recv = {name: many(nz) for name in names}
    own_copy = {}

    def spread_z(name):
        src, place = names[name]
        own_copy[name] = local(src, place(fs))
        for k in range(1, nz):
            send(src, place(fs), z_dev(k), z_recv[name][k])

    def spread_x(name):
        src, place = names[name]
        send(src, place(fs), x_dev, x_recv[name][0])

    def hand_on(name, ks=None):
        place = names[name][1]
        for k in ks or range(1, nz):
            fq = 2 * z_from(k) + x
            recv(place(fq), z_recv[name][k])
            send(place(fq), place(fq), x_dev, x_recv[name][k])

    def arrived(name):
        place = names[name][1]
        own_copy[name].wait()
        for k in range(nz):
            recv(place(2 * z_from(k) + (1 - x)), x_recv[name][k])

    def rows_of(yq, tq):
        return pl.ds(pl.multiple_of(yq * half_len + tq * quarter, quarter), quarter)

    own_rows = rows_of(y, t)

    tok_y, tok_c, cot_y, cot_c, seg_y = many(5)
    spread_z("n")
    spread_x("n")
    seg_local = local(seg, seg_row.at[:, tile(y, half_len)])
    send(seg, seg_row.at[:, tile(y, half_len)], y_dev, seg_y)
    tok_local = local(tok, xg.at[tile(y, half_len), :])
    send(tok.at[tile(t, quarter), :], xg.at[own_rows, :], y_dev, tok_y)
    for name in ("q", "k", "v"):
        spread_z(name)
        spread_x(name)
    cot_local = local(cot, cg.at[tile(y, half_len), :])
    send(cot.at[tile(t, quarter), :], cg.at[own_rows, :], y_dev, cot_y)
    for name in ("o", "g"):
        spread_z(name)
        spread_x(name)
    spread_z("u")
    spread_z("d")

    far = rows_of(1 - y, t)
    far_other = rows_of(1 - y, 1 - t)

    def core_forward(ref, y_idx, c_idx):
        recv(ref.at[far, :], y_idx)
        return send(ref.at[far, :], ref.at[far, :], c_dev, c_idx)

    kinds = {"a": 0, "out": 1, "dh2": 2, "dh1": 3}
    ex_recv = {name: many(3) for name in kinds}
    ex_sent = []

    def exchange_far(name, compute):
        e = kinds[name]
        drain(ex_sent)
        ex_sent.clear()
        compute(far_other, part.at[0])
        ex_sent.append(send(part.at[0], from_core.at[e, 0], c_dev, ex_recv[name][0]))
        compute(far, part.at[1])
        recv(from_core.at[e, 0], ex_recv[name][0])

        def add(i):
            r = tile(i, 32)
            pair_sum[r, :] = (part[1, r, :].astype(F32) + from_core[e, 0, r, :].astype(F32)).astype(BF)

        loop(quarter // 32, add)
        ex_sent.append(send(pair_sum, from_y.at[e], y_dev, ex_recv[name][2]))

    def exchange_near(name, compute):
        e = kinds[name]
        compute(rows_of(y, 1 - t), part.at[2])
        ex_sent.append(send(part.at[2], from_core.at[e, 1], c_dev, ex_recv[name][1]))
        compute(own_rows, part.at[3])

    def exchange_end(name):
        e = kinds[name]
        recv(from_core.at[e, 1], ex_recv[name][1])
        recv(from_y.at[e], ex_recv[name][2])

    def total_of(name, r):
        e = kinds[name]
        return part[3, r, :].astype(F32) + from_core[e, 1, r, :].astype(F32) + from_y[e, r, :].astype(F32)

    def spread_rows(ref, idx):
        return [
            send(ref.at[own_rows, :], ref.at[own_rows, :], c_dev, idx[0]),
            send(ref.at[own_rows, :], ref.at[own_rows, :], y_dev, idx[1]),
        ]

    h2_idx = many(3)
    ab_idx = many(3)

    grads = {
        "d": (p_d, r_d, s_d, f_d),
        "g": (p_g, r_g, s_g, f_g),
        "u": (p_u, r_u, s_u, f_u),
        "o": (p_o, r_o, s_o, f_o),
        "qkv": (p_qkv, r_qkv, s_qkv, f_qkv),
        "n": (p_n, r_n, s_n, f_n),
    }
    gx = {name: many(nz) for name in grads}
    gz = {name: [None] + many(nz - 1) for name in grads}

    def grad_x(name):
        p, r = grads[name][:2]
        for k in list(range(1, nz)) + [0]:
            zq = z_of(k)
            send(p.at[1 - x, zq], r.at[zq], x_dev, gx[name][k])

    def add_rows(rows, body):
        step = 16 if rows % 16 == 0 else rows
        loop(rows // step, lambda i: body(tile(i, step)))

    def grad_z(name, ks=None):
        p, r, s = grads[name][:3]
        for k in ks or range(1, nz):
            zq = z_of(k)
            recv(r.at[zq], gx[name][k])

            def add(rr):
                p[x, zq, rr, :] = (p[x, zq, rr, :].astype(F32) + r[zq, rr, :].astype(F32)).astype(p.dtype)

            add_rows(p.shape[2], add)
            send(p.at[x, zq], s.at[k - 1], z_dev(k), gz[name][k])

    out_places = {
        "d": lambda f: [(f, o_d.at[uw, :])],
        "g": lambda f: [(f, o_g.at[:, uw])],
        "u": lambda f: [(f, o_u.at[:, uw])],
        "o": lambda f: [(f, o_o.at[hw, :])],
        "qkv": lambda f: [
            (f.at[:, i * heads_w : (i + 1) * heads_w], ref.at[:, hw]) for i, ref in enumerate((o_q, o_k, o_v))
        ],
    }
    out_idx = {"d": many(1), "g": many(1), "u": many(1), "o": many(1), "qkv": many(3)}
    last_local = []

    def grad_end(name):
        p, r, s, f = grads[name]
        recv(r.at[z], gx[name][0])
        for k in range(1, nz):
            recv(s.at[k - 1], gz[name][k])

        def add(rr):
            total = p[x, z, rr, :].astype(F32) + r[z, rr, :].astype(F32)
            for k in range(1, nz):
                total = total + s[k - 1, rr, :].astype(F32)
            f[rr, :] = total.astype(f.dtype)

        add_rows(p.shape[2], add)
        if name != "n":
            for (src, dst), idx in zip(out_places[name](f), out_idx[name]):
                last_local.append(local(src, dst))
                send(src, dst, y_dev, idx)

    def grad_done(name):
        other_h = pl.ds(pl.multiple_of((1 - y) * heads_w, heads_w), heads_w)
        other_u = pl.ds(pl.multiple_of((1 - y) * hidden, hidden), hidden)
        refs = {
            "d": [o_d.at[other_u, :]],
            "g": [o_g.at[:, other_u]],
            "u": [o_u.at[:, other_u]],
            "o": [o_o.at[other_h, :]],
            "qkv": [o_q.at[:, other_h], o_k.at[:, other_h], o_v.at[:, other_h]],
        }[name]
        for ref, idx in zip(refs, out_idx[name]):
            recv(ref, idx)

    hand_on("n")
    arrived("n")
    gain_one = jnp.concatenate([gain_all[i, 0:1, :] for i in range(2 * nz)], axis=1)
    gain_two = jnp.concatenate([gain_all[i, 1:2, :] for i in range(2 * nz)], axis=1)

    def norm_rows(start):
        def body(i):
            r = pl.ds(pl.multiple_of(start + i * 32, 32), 32)
            values = xg[r, :].astype(F32)
            inverse = lax.rsqrt(jnp.mean(values * values, axis=-1, keepdims=True) + EPSILON)
            h1[r, :] = (values * inverse * gain_one).astype(BF)

        loop(half_len // 32, body)

    tok_local.wait()
    norm_rows(y * half_len)
    core_forward(xg, tok_y, tok_c)
    seg_local.wait()
    recv(seg_row.at[:, tile(1 - y, half_len)], seg_y)
    seg_col[...] = jnp.broadcast_to(seg_row[0:1, :], (128, 2 * half_len)).T
    recv(xg.at[far_other, :], tok_c)
    norm_rows((1 - y) * half_len)
    for name in ("q", "k", "v"):
        hand_on(name)
    hand_on("o")
    spread_x("u")
    for name in ("q", "k", "v"):
        arrived(name)

    def project(i):
        r = tile(i, 512)
        rows = h1[r, :]
        query[r, :] = (dot_nn(rows, wqkv[:, 0:heads_w]).astype(BF).astype(F32) * SCALE).astype(BF)
        keys[r, :] = dot_nn(rows, wqkv[:, heads_w : 2 * heads_w]).astype(BF)
        vals[r, :] = dot_nn(rows, wqkv[:, 2 * heads_w : 3 * heads_w]).astype(BF)

    loop(xg.shape[0] // 512, project)
    keys_t[...] = keys[...].T
    vals_t[...] = vals[...].T
    core_forward(cg, cot_y, cot_c)

    blocks = half_len // BLOCK
    pairs = heads_w // (2 * HEAD_DIM)

    def attend_half(which):
        def body(i):
            block = which * blocks + i
            args = (pairs, query, keys, vals_t, bias, seg_col, seg_row, mixed, mixed_t, log_sum)

            @pl.when(which == 0)
            def _():
                attend_block(block, half_len, *args)

            @pl.when(which == 1)
            def _():
                attend_block(block, 2 * half_len, *args)

        loop(blocks, body)

    attend_half(1 - y)
    hand_on("g", [1])
    arrived("o")

    def out_rows(r, dst):
        dst[...] = dot_nn(mixed[r, :], wo[...]).astype(BF)

    exchange_far("a", out_rows)
    attend_half(y)
    exchange_near("a", out_rows)
    hand_on("g", [2])
    exchange_end("a")

    def first_residual(i):
        r = tile(i, 32)
        rr = pl.ds(pl.multiple_of(y * half_len + t * quarter + i * 32, 32), 32)
        values = xg[rr, :].astype(F32) + total_of("a", r)
        y1[r, :] = values
        inverse = lax.rsqrt(jnp.mean(values * values, axis=-1, keepdims=True) + EPSILON)
        h2[rr, :] = (values * inverse * gain_two).astype(BF)

    loop(quarter // 32, first_residual)
    row_sends = spread_rows(h2, h2_idx)
    hand_on("g", [3])
    spread_x("d")
    row_sends.append(core_forward(h2, h2_idx[1], h2_idx[2]))
    recv(h2.at[rows_of(y, 1 - t), :], h2_idx[0])
    recv(h2.at[far_other, :], h2_idx[2])
    hand_on("u")
    arrived("g")
    arrived("u")

    def gate_rows(i):
        r = tile(i, 256)
        rows = h2[r, :]

        def cols(j):
            c = tile(j, 256)
            g = dot_nn(rows, wg[:, c])
            u = dot_nn(rows, wu[:, c])
            sg = 1.0 / (1.0 + jnp.exp(-g))
            gs = g * sg
            act_u[r, c] = gs.astype(BF)
            act_g[r, c] = (u * sg * (1.0 + g * (1.0 - sg))).astype(BF)
            act_m[r, c] = (gs * u).astype(BF)

        loop(hidden // 256, cols)

    n_rows = xg.shape[0] // 256
    loop(n_rows // 2, gate_rows)
    hand_on("d", [1])
    loop(n_rows // 2, lambda i: gate_rows(i + n_rows // 2))
    hand_on("d", [2])
    cot_local.wait()
    recv(cg.at[far_other, :], cot_c)

    def grad_cols(left, right, p, rows, index):
        c = tile(index, 2 * db)
        for i in range(rows // 256):
            r = slice(i * 256, (i + 1) * 256)
            both = dot_tn(left[:, r], right[:, c]).astype(BF)
            p[0, index, r, :] = both[:, 0:db]
            p[1, index, r, :] = both[:, db : 2 * db]

    def grad_rows(left, right, p, index):
        c = tile(index, 2 * db)
        both = dot_tn(left[:, c], right[...]).astype(BF)
        p[0, index] = both[0:db, :]
        p[1, index] = both[db : 2 * db, :]

    loop(nz, lambda i: grad_cols(act_m, cg, p_d, hidden, i))
    hand_on("d", [3])
    grad_x("d")
    arrived("d")

    def hidden_back(r, dst):
        rows = cg[r, :]

        def cols(j):
            c = tile(j, 256)
            dm = dot_nt(rows, wd[c, :])
            act_g[r, c] = (dm * act_g[r, c].astype(F32)).astype(BF)
            act_u[r, c] = (dm * act_u[r, c].astype(F32)).astype(BF)

        loop(hidden // 256, cols)

        def back(j):
            c = tile(j, 512)
            dst[:, c] = (dot_nt(act_g[r, :], wg[c, :]) + dot_nt(act_u[r, :], wu[c, :])).astype(BF)

        loop(width // 512, back)

    exchange_far("dh2", hidden_back)
    exchange_near("dh2", hidden_back)
    loop(nz, lambda i: grad_rows(h2, act_g, p_g, i))
    grad_x("g")
    loop(nz, lambda i: grad_rows(h2, act_u, p_u, i))
    grad_x("u")
    grad_z("d", [1])
    exchange_end("dh2")

    def second_residual(i, carry):
        r = tile(i, 32)
        rr = pl.ds(pl.multiple_of(y * half_len + t * quarter + i * 32, 32), 32)
        values = y1[r, :]
        inverse = lax.rsqrt(jnp.mean(values * values, axis=-1, keepdims=True) + EPSILON)
        normed = values * inverse
        grad = total_of("dh2", r)
        scaled = grad * gain_two
        mean = jnp.mean(scaled * normed, axis=-1, keepdims=True)
        full = cg[rr, :].astype(F32) + inverse * (scaled - normed * mean)
        final_rows[r, :] = full
        ab[rr, :] = full.astype(BF)
        return carry + jnp.sum(grad * normed, axis=0, keepdims=True)

    gain_two_grad = lax.fori_loop(0, quarter // 32, second_residual, jnp.zeros((1, width), F32))
    row_sends += spread_rows(ab, ab_idx)

    def down_rows(r, dst):
        def cols(j):
            c = tile(j, 512)
            dst[:, c] = dot_nn(act_m[r, :], wd[:, c]).astype(BF)

        loop(width // 512, cols)

    exchange_far("out", down_rows)
    exchange_near("out", down_rows)
    grad_z("d", [2, 3])
    row_sends.append(core_forward(ab, ab_idx[1], ab_idx[2]))
    recv(ab.at[rows_of(y, 1 - t), :], ab_idx[0])
    recv(ab.at[far_other, :], ab_idx[2])

    def mixed_back(i):
        r = tile(i, 512)
        grad_mixed[r, :] = dot_nt(ab[r, :], wo[...]).astype(BF)

    loop(xg.shape[0] // 512, mixed_back)
    loop(nz, lambda i: grad_cols(mixed, ab, p_o, heads_w, i))
    grad_x("o")
    grad_k[...] = jnp.zeros_like(grad_k)
    grad_v[...] = jnp.zeros_like(grad_v)

    def attend_back_half(which):
        def body(i):
            block = which * blocks + i
            args = (
                pairs, query, keys, keys_t, vals, grad_mixed, bias, seg_col, seg_row, log_sum, grad_qkv, mixed_t, grad_k, grad_v,
            )
            attend_back_block(block, (which + 1) * half_len, *args)

        loop(blocks, body)

    attend_back_half(0)
    grad_z("g", [1, 2])
    attend_back_half(1)
    grad_qkv[:, heads_w : 2 * heads_w] = grad_k[...].astype(BF)
    grad_qkv[:, 2 * heads_w : 3 * heads_w] = grad_v[...].astype(BF)
    loop(nz, lambda i: grad_rows(h1, grad_qkv, p_qkv, i))
    grad_x("qkv")

    def hidden_one_back(r, dst):
        def cols(j):
            c = tile(j, 512)
            dst[:, c] = dot_nt(grad_qkv[r, :], wqkv[c, :]).astype(BF)

        loop(width // 512, cols)

    exchange_end("out")
    out_c, gtok_c = many(2)
    my_rows = tile(t, quarter)
    other_rows = tile(1 - t, quarter)

    def finish_out(i):
        r = tile(i, 32)
        ab[r, :] = (y1[r, :] + total_of("out", r)).astype(BF)

    grad_z("g", [3])
    drain(row_sends)
    loop(quarter // 32, finish_out)
    last_local.append(local(ab.at[0:quarter, :], out.at[my_rows, :]))
    send(ab.at[0:quarter, :], out.at[my_rows, :], c_dev, out_c)
    exchange_far("dh1", hidden_one_back)
    exchange_near("dh1", hidden_one_back)
    grad_end("d")
    grad_z("u")
    grad_end("g")
    exchange_end("dh1")

    def last(i, carry):
        r = tile(i, 32)
        rr = pl.ds(pl.multiple_of(y * half_len + t * quarter + i * 32, 32), 32)
        values = xg[rr, :].astype(F32)
        inverse = lax.rsqrt(jnp.mean(values * values, axis=-1, keepdims=True) + EPSILON)
        normed = values * inverse
        grad = total_of("dh1", r)
        scaled = grad * gain_one
        mean = jnp.mean(scaled * normed, axis=-1, keepdims=True)
        full = final_rows[r, :] + inverse * (scaled - normed * mean)
        h2[r, :] = full.astype(BF)
        return carry + jnp.sum(grad * normed, axis=0, keepdims=True)

    gain_one_grad = lax.fori_loop(0, quarter // 32, last, jnp.zeros((1, width), F32))
    for i in range(2 * nz):
        c = slice(i * db, (i + 1) * db)
        p_n[i % 2, i // 2] = jnp.concatenate(
            [gain_one_grad[:, c], gain_two_grad[:, c], jnp.zeros((6, db), F32)], axis=0
        )
    grad_x("n")
    last_local.append(local(h2.at[0:quarter, :], g_tok.at[my_rows, :]))
    send(h2.at[0:quarter, :], g_tok.at[my_rows, :], c_dev, gtok_c)
    grad_z("n")
    grad_z("o")
    grad_end("u")
    grad_z("qkv")
    grad_end("n")
    n_c, n_y = many(2)
    send(f_n, c_n, c_dev, n_c)
    grad_end("o")
    recv(c_n, n_c)
    y_n[0] = f_n[...] + c_n[...]
    send(y_n.at[0], y_n.at[1], y_dev, n_y)
    grad_end("qkv")
    recv(y_n.at[1], n_y)
    o_gain[...] = y_n[0] + y_n[1]
    for name in ("d", "g", "u", "o", "qkv"):
        grad_done(name)
    recv(out.at[other_rows, :], out_c)
    recv(g_tok.at[other_rows, :], gtok_c)
    for copy in last_local:
        copy.wait()
    drain(list(sent))


def fused(nz, tokens, segment_ids, w_query, w_key, w_value, w_out, w_gate, w_up, w_down, gain_attn, gain_ffn, cotangent):
    half_len, _, width = tokens.shape
    length = 2 * half_len
    quarter = half_len // 2
    heads_w = w_query.shape[1] // 2
    hidden = w_gate.shape[1] // 2
    db = w_query.shape[0]
    heads = heads_w // HEAD_DIM
    gains = jnp.concatenate(
        [gain_attn.astype(F32)[None], gain_ffn.astype(F32)[None], jnp.zeros((6, db), F32)], axis=0
    )
    seg = jnp.broadcast_to(segment_ids, (8, half_len))

    def vm(*shape, dtype=BF):
        return pltpu.VMEM(shape, dtype)

    shape_d, shape_g, shape_o, shape_qkv = (hidden, db), (db, hidden), (heads_w, db), (db, 3 * heads_w)
    shapes = (shape_d, shape_g, shape_g, shape_o, shape_qkv)
    scratch = [
        vm(length, width), vm(length, width), vm(8, length, dtype=I32), vm(2 * nz, 8, db, dtype=F32),
        vm(width, 3 * heads_w), vm(heads_w, width), vm(width, hidden), vm(width, hidden), vm(hidden, width),
        vm(length, width), vm(length, width), vm(length, width),
        vm(length, heads_w), vm(length, heads_w), vm(length, heads_w), vm(heads_w, length), vm(heads_w, length),
        vm(length, heads_w), vm(length, heads_w), vm(length, 3 * heads_w),
        vm(length, heads_w, dtype=F32), vm(length, heads_w, dtype=F32),
        vm(length, hidden), vm(length, hidden), vm(length, hidden),
        vm(quarter, width, dtype=F32), vm(length, BLOCK, dtype=F32), vm(heads_w, BLOCK, dtype=F32),
        vm(heads, 8, length, dtype=F32), vm(length, 128, dtype=I32),
        vm(4, quarter, width), vm(quarter, width), vm(4, 2, quarter, width), vm(4, quarter, width),
        vm(quarter, width, dtype=F32),
    ]
    scratch += [vm(2, nz, *shape) for shape in shapes]
    scratch += [vm(nz, *shape) for shape in shapes]
    scratch += [vm(nz - 1, *shape) for shape in shapes]
    scratch += [vm(*shape) for shape in shapes]
    scratch += [
        vm(2, nz, 8, db, dtype=F32), vm(nz, 8, db, dtype=F32), vm(nz - 1, 8, db, dtype=F32), vm(8, db, dtype=F32),
        vm(8, db, dtype=F32), vm(2, 8, db, dtype=F32),
    ]
    scratch += [pltpu.SemaphoreType.DMA((160,)), pltpu.SemaphoreType.DMA((160,)), pltpu.SemaphoreType.DMA((32,))]
    anywhere = pl.BlockSpec(memory_space=pl.ANY)
    weights = (w_query, w_key, w_value, w_out, w_gate, w_up, w_down)
    results = pl.pallas_call(
        functools.partial(layer_kernel, nz),
        out_shape=[jax.ShapeDtypeStruct((half_len, width), BF)] * 2
        + [jax.ShapeDtypeStruct(item.shape, BF) for item in weights]
        + [jax.ShapeDtypeStruct((8, db), F32)],
        in_specs=[anywhere] * 11,
        out_specs=[anywhere] * 9 + [pl.BlockSpec(memory_space=pltpu.VMEM)],
        scratch_shapes=scratch,
        compiler_params=pltpu.CompilerParams(
            collective_id=0, has_side_effects=True, vmem_limit_bytes=VMEM_BYTES
        ),
        name="layer",
    )(tokens.reshape(half_len, width), cotangent.reshape(half_len, width), seg, gains, *weights)
    shape = tokens.shape
    return (
        results[0].reshape(shape),
        results[1].reshape(shape),
        *[item.astype(F32) for item in results[2:9]],
        results[9][0],
        results[9][1],
    )


def fits(mesh, tokens_shape):
    return mesh.shape["fsdp"] == 8 and mesh.shape["ctx"] == 2 and mesh.shape["tp"] == 2 and tokens_shape[1] == 1


def solution(mesh):
    def step(tokens, *rest):
        if fits(mesh, tokens.shape):
            return fused(mesh.shape["fsdp"] // 2, tokens, *rest)
        return local(tokens, *rest)

    return jax.shard_map(
        step,
        mesh=mesh,
        in_specs=(
            P("ctx", "fsdp", None),
            P("fsdp", "ctx"),
            P("fsdp", "tp"),
            P("fsdp", "tp"),
            P("fsdp", "tp"),
            P("tp", "fsdp"),
            P("fsdp", "tp"),
            P("fsdp", "tp"),
            P("tp", "fsdp"),
            P("fsdp"),
            P("fsdp"),
            P("ctx", "fsdp", None),
        ),
        out_specs=(
            P("ctx", "fsdp", None),
            P("ctx", "fsdp", None),
            P("fsdp", "tp"),
            P("fsdp", "tp"),
            P("fsdp", "tp"),
            P("tp", "fsdp"),
            P("fsdp", "tp"),
            P("fsdp", "tp"),
            P("tp", "fsdp"),
            P("fsdp"),
            P("fsdp"),
        ),
        check_vma=False,
    )
```

```python
import functools

import jax
import jax.numpy as jnp
from jax import lax
from jax.experimental import pallas as pl
from jax.experimental.pallas import tpu as pltpu
from jax.sharding import PartitionSpec as P

HEAD_DIM = 64


EPSILON = 1e-05
SCALE = 0.125
MASKED = -1e30


def normalize(values):
    inverse = lax.rsqrt(jnp.mean(values * values, axis=-1, keepdims=True) + EPSILON)
    return (values * inverse, inverse)


def norm_back(grad_normed, normed, inverse):
    return inverse * (grad_normed - normed * jnp.mean(grad_normed * normed, axis=-1, keepdims=True))


def inner_rows(left, right):
    return lax.dot_general(
        left, right, (((0,), (0,)), ((), ())), preferred_element_type=jnp.float32
    )


def times_transposed(left, weight):
    return lax.dot_general(
        left, weight, (((1,), (1,)), ((), ())), preferred_element_type=jnp.float32
    )


def head_sum(partial_sum):
    return lax.psum(partial_sum, "tp")


def split_heads(values, head_size):
    length, sequences, width = values.shape
    return jnp.moveaxis(values.reshape(length, sequences, width // head_size, head_size), 2, 0)


def join_heads(values):
    heads, length, sequences, head_size = values.shape
    return jnp.moveaxis(values, 0, 2).reshape(length, sequences, heads * head_size)


def make_mask(query_pos, query_seg, key_pos, key_seg):
    before = key_pos[None, None, :] <= query_pos[None, :, None]
    same = query_seg.T[:, :, None] == key_seg.T[:, None, :]
    return before & same


def key_head_grads(parts, use_mask):
    q_head, k_head, v_head, d_head, log_total, delta = parts
    scores = jnp.einsum("qsd,ksd->sqk", q_head, k_head, preferred_element_type=jnp.float32) * SCALE
    probs = jnp.exp(jnp.where(use_mask, scores, MASKED) - log_total)
    grad_probs = jnp.einsum("qsd,ksd->sqk", d_head, v_head, preferred_element_type=jnp.float32)
    grad_scores = (probs * (grad_probs - delta)).astype(jnp.bfloat16)
    grad_v = jnp.einsum(
        "sqk,qsd->ksd", probs.astype(jnp.bfloat16), d_head, preferred_element_type=jnp.float32
    )
    grad_k = (
        jnp.einsum("sqk,qsd->ksd", grad_scores, q_head, preferred_element_type=jnp.float32) * SCALE
    )
    return (grad_k, grad_v)


def local(
    tokens,
    segment_ids,
    w_query,
    w_key,
    w_value,
    w_out,
    w_gate,
    w_up,
    w_down,
    gain_attn,
    gain_ffn,
    cotangent,
):
    local_len, sequences, width = tokens.shape
    rows = local_len * sequences
    (
        full_query,
        full_key,
        full_value,
        full_out,
        full_gate,
        full_up,
        full_down,
        full_gain_one,
        full_gain_two,
    ) = (
        lax.all_gather(w_query, "fsdp", axis=0, tiled=True),
        lax.all_gather(w_key, "fsdp", axis=0, tiled=True),
        lax.all_gather(w_value, "fsdp", axis=0, tiled=True),
        lax.all_gather(w_out, "fsdp", axis=1, tiled=True),
        lax.all_gather(w_gate, "fsdp", axis=0, tiled=True),
        lax.all_gather(w_up, "fsdp", axis=0, tiled=True),
        lax.all_gather(w_down, "fsdp", axis=1, tiled=True),
        lax.all_gather(gain_attn, "fsdp", axis=0, tiled=True),
        lax.all_gather(gain_ffn, "fsdp", axis=0, tiled=True),
    )
    gain_one = full_gain_one.astype(jnp.float32)
    gain_two = full_gain_two.astype(jnp.float32)
    head_width = full_query.shape[1]
    flat = tokens.astype(jnp.float32).reshape(rows, width)
    normed_one, inverse_one = normalize(flat)
    hidden_one = (normed_one * gain_one).astype(jnp.bfloat16)
    query = (
        jnp.dot(hidden_one, full_query, preferred_element_type=jnp.float32)
        .astype(jnp.bfloat16)
        .reshape(local_len, sequences, head_width)
    )
    keys = (
        jnp.dot(hidden_one, full_key, preferred_element_type=jnp.float32)
        .astype(jnp.bfloat16)
        .reshape(local_len, sequences, head_width)
    )
    vals = (
        jnp.dot(hidden_one, full_value, preferred_element_type=jnp.float32)
        .astype(jnp.bfloat16)
        .reshape(local_len, sequences, head_width)
    )
    pair = jnp.concatenate([keys, vals], axis=-1)
    seg_local = segment_ids.T
    pair_all, seg_all = (
        lax.all_gather(pair, "ctx", axis=0, tiled=True),
        lax.all_gather(seg_local, "ctx", axis=0, tiled=True),
    )
    length = pair_all.shape[0]
    query_pos = lax.axis_index("ctx") * local_len + jnp.arange(local_len, dtype=jnp.int32)
    all_pos = jnp.arange(length, dtype=jnp.int32)
    mask = make_mask(query_pos, seg_local, all_pos, seg_all)
    q_heads = split_heads(query, HEAD_DIM)
    k_heads = split_heads(pair_all[..., :head_width], HEAD_DIM)
    v_heads = split_heads(pair_all[..., head_width:], HEAD_DIM)

    def attend(parts):
        q_head, k_head, v_head = parts
        scores = (
            jnp.einsum("qsd,ksd->sqk", q_head, k_head, preferred_element_type=jnp.float32) * SCALE
        )
        scores = jnp.where(mask, scores, MASKED)
        row_max = jnp.max(scores, axis=-1, keepdims=True)
        log_total = row_max + jnp.log(jnp.sum(jnp.exp(scores - row_max), axis=-1, keepdims=True))
        probs = jnp.exp(scores - log_total).astype(jnp.bfloat16)
        return (
            jnp.einsum("sqk,ksd->qsd", probs, v_head, preferred_element_type=jnp.float32),
            log_total,
        )

    attended, log_totals = lax.map(attend, (q_heads, k_heads, v_heads))
    mixed = join_heads(attended).astype(jnp.bfloat16).reshape(rows, head_width)
    resid = flat + head_sum(jnp.dot(mixed, full_out, preferred_element_type=jnp.float32))
    normed_two, inverse_two = normalize(resid)
    hidden_two = (normed_two * gain_two).astype(jnp.bfloat16)
    gate = jnp.dot(hidden_two, full_gate, preferred_element_type=jnp.float32)
    upward = jnp.dot(hidden_two, full_up, preferred_element_type=jnp.float32)
    sigmoid_gate = jax.nn.sigmoid(gate)
    swish_up = (gate * sigmoid_gate * upward).astype(jnp.bfloat16)
    result = resid + head_sum(jnp.dot(swish_up, full_down, preferred_element_type=jnp.float32))
    output = result.astype(jnp.bfloat16).reshape(local_len, sequences, width)
    (
        full_query,
        full_key,
        full_value,
        full_out,
        full_gate,
        full_up,
        full_down,
        full_gain_one,
        full_gain_two,
    ) = (
        lax.all_gather(w_query, "fsdp", axis=0, tiled=True),
        lax.all_gather(w_key, "fsdp", axis=0, tiled=True),
        lax.all_gather(w_value, "fsdp", axis=0, tiled=True),
        lax.all_gather(w_out, "fsdp", axis=1, tiled=True),
        lax.all_gather(w_gate, "fsdp", axis=0, tiled=True),
        lax.all_gather(w_up, "fsdp", axis=0, tiled=True),
        lax.all_gather(w_down, "fsdp", axis=1, tiled=True),
        lax.all_gather(gain_attn, "fsdp", axis=0, tiled=True),
        lax.all_gather(gain_ffn, "fsdp", axis=0, tiled=True),
    )
    gain_one = full_gain_one.astype(jnp.float32)
    gain_two = full_gain_two.astype(jnp.float32)
    grad_result = cotangent.astype(jnp.float32).reshape(rows, width)
    grad_low = grad_result.astype(jnp.bfloat16)
    grad_wdown = inner_rows(swish_up, grad_low)
    grad_swish = times_transposed(grad_low, full_down)
    grad_gate_act = (
        grad_swish * upward * sigmoid_gate * (1.0 + gate * (1.0 - sigmoid_gate))
    ).astype(jnp.bfloat16)
    grad_upward = (grad_swish * gate * sigmoid_gate).astype(jnp.bfloat16)
    grad_wgate = inner_rows(hidden_two, grad_gate_act)
    grad_wup = inner_rows(hidden_two, grad_upward)
    grad_hidden_two = head_sum(
        times_transposed(grad_gate_act, full_gate) + times_transposed(grad_upward, full_up)
    )
    grad_gain_two = jnp.sum(grad_hidden_two * normed_two, axis=0)
    grad_resid = grad_result + norm_back(grad_hidden_two * gain_two, normed_two, inverse_two)
    grad_branch = grad_resid.astype(jnp.bfloat16)
    grad_wout = inner_rows(mixed, grad_branch)
    grad_mixed = (
        times_transposed(grad_branch, full_out)
        .astype(jnp.bfloat16)
        .reshape(local_len, sequences, head_width)
    )
    d_heads = split_heads(grad_mixed, HEAD_DIM)

    def query_side(parts):
        q_head, k_head, v_head, d_head, log_total = parts
        scores = (
            jnp.einsum("qsd,ksd->sqk", q_head, k_head, preferred_element_type=jnp.float32) * SCALE
        )
        probs = jnp.exp(jnp.where(mask, scores, MASKED) - log_total)
        grad_probs = jnp.einsum("qsd,ksd->sqk", d_head, v_head, preferred_element_type=jnp.float32)
        delta = jnp.sum(probs * grad_probs, axis=-1, keepdims=True)
        grad_scores = (probs * (grad_probs - delta)).astype(jnp.bfloat16)
        return (
            jnp.einsum("sqk,ksd->qsd", grad_scores, k_head, preferred_element_type=jnp.float32)
            * SCALE,
            delta,
        )

    grad_q_heads, deltas = lax.map(query_side, (q_heads, k_heads, v_heads, d_heads, log_totals))
    grad_query = join_heads(grad_q_heads).astype(jnp.bfloat16).reshape(rows, head_width)
    piece_mask = make_mask(
        query_pos, seg_local, jnp.arange(local_len * lax.axis_size("ctx"), dtype=jnp.int32), seg_all
    )
    k_piece = split_heads(pair_all[..., :head_width], HEAD_DIM)
    v_piece = split_heads(pair_all[..., head_width:], HEAD_DIM)

    def per_head(parts):
        return key_head_grads(parts, piece_mask)

    grad_k_heads, grad_v_heads = lax.map(
        per_head, (q_heads, k_piece, v_piece, d_heads, log_totals, deltas)
    )
    grad_pair = lax.psum_scatter(
        jnp.concatenate([join_heads(grad_k_heads), join_heads(grad_v_heads)], axis=-1).astype(
            jnp.bfloat16
        ),
        "ctx",
        scatter_dimension=0,
        tiled=True,
    ).astype(jnp.float32)
    grad_keys = grad_pair[..., :head_width].astype(jnp.bfloat16).reshape(rows, head_width)
    grad_vals = grad_pair[..., head_width:].astype(jnp.bfloat16).reshape(rows, head_width)
    grad_wquery = inner_rows(hidden_one, grad_query)
    grad_wkey = inner_rows(hidden_one, grad_keys)
    grad_wvalue = inner_rows(hidden_one, grad_vals)
    grad_hidden_one = head_sum(
        times_transposed(grad_query, full_query)
        + times_transposed(grad_keys, full_key)
        + times_transposed(grad_vals, full_value)
    )
    grad_gain_one = jnp.sum(grad_hidden_one * normed_one, axis=0)
    grad_input = grad_resid + norm_back(grad_hidden_one * gain_one, normed_one, inverse_one)
    grad_input = grad_input.astype(jnp.bfloat16).reshape(local_len, sequences, width)
    shares = (
        lax.psum_scatter(
            grad_wquery.astype(jnp.bfloat16), "fsdp", scatter_dimension=0, tiled=True
        ).astype(jnp.float32),
        lax.psum_scatter(
            grad_wkey.astype(jnp.bfloat16), "fsdp", scatter_dimension=0, tiled=True
        ).astype(jnp.float32),
        lax.psum_scatter(
            grad_wvalue.astype(jnp.bfloat16), "fsdp", scatter_dimension=0, tiled=True
        ).astype(jnp.float32),
        lax.psum_scatter(
            grad_wout.astype(jnp.bfloat16), "fsdp", scatter_dimension=1, tiled=True
        ).astype(jnp.float32),
        lax.psum_scatter(
            grad_wgate.astype(jnp.bfloat16), "fsdp", scatter_dimension=0, tiled=True
        ).astype(jnp.float32),
        lax.psum_scatter(
            grad_wup.astype(jnp.bfloat16), "fsdp", scatter_dimension=0, tiled=True
        ).astype(jnp.float32),
        lax.psum_scatter(
            grad_wdown.astype(jnp.bfloat16), "fsdp", scatter_dimension=1, tiled=True
        ).astype(jnp.float32),
        lax.psum_scatter(
            grad_gain_one.astype(jnp.bfloat16), "fsdp", scatter_dimension=0, tiled=True
        ).astype(jnp.float32),
        lax.psum_scatter(
            grad_gain_two.astype(jnp.bfloat16), "fsdp", scatter_dimension=0, tiled=True
        ).astype(jnp.float32),
    )
    shares = (
        lax.psum(shares[0].astype(jnp.bfloat16), "ctx").astype(jnp.float32),
        lax.psum(shares[1].astype(jnp.bfloat16), "ctx").astype(jnp.float32),
        lax.psum(shares[2].astype(jnp.bfloat16), "ctx").astype(jnp.float32),
        lax.psum(shares[3].astype(jnp.bfloat16), "ctx").astype(jnp.float32),
        lax.psum(shares[4].astype(jnp.bfloat16), "ctx").astype(jnp.float32),
        lax.psum(shares[5].astype(jnp.bfloat16), "ctx").astype(jnp.float32),
        lax.psum(shares[6].astype(jnp.bfloat16), "ctx").astype(jnp.float32),
        lax.psum(shares[7].astype(jnp.bfloat16), "ctx").astype(jnp.float32),
        lax.psum(shares[8].astype(jnp.bfloat16), "ctx").astype(jnp.float32),
    )
    return (
        output,
        grad_input,
        shares[0],
        shares[1],
        shares[2],
        shares[3],
        shares[4],
        shares[5],
        shares[6],
        shares[7],
        shares[8],
    )


BF = jnp.bfloat16
F32 = jnp.float32
I32 = jnp.int32
MESH = pl.DeviceIdType.MESH
BLOCK = 256
VMEM_BYTES = 67043328
ORDER = (
    "gain", "z:qkv", "x:o", "tok", "ro:o:0", "z:o", "x:qkv", "cot", "r:qkv:1", "x:g",
    "r:o:1", "a:o", "z:g", "r:qkv:2", "seg", "x:u0", "z:u0", "cotf", "ro:o:1", "tokf",
    "n0", "r:qkv:3", "z:u1", "r:o:2", "r:u0:1", "x:d", "x:u1", "n1", "r:u1:1", "a:qkv",
    "ro:o:2", "r:g:1", "proj", "z:d", "r:o:3", "ro:u0:0", "at0", "ro:o:3", "xa0", "r:u1:2",
    "xa1", "xa2", "r:g:2", "at1", "a:u0", "xa3", "xa4", "r:u0:2", "ro:u0:1", "r:d:1",
    "r:u1:3", "xa5", "r:g:3", "ro:u0:2", "r:u0:3", "cotr", "h2f", "r:d:2", "a:u1", "a:g",
    "ro:u0:3", "gt0", "gt3", "gt2", "r:d:3", "gt1", "gd0", "gd1", "sx:d1:1", "sx:d0:1",
    "a:d", "xh0", "sx:d0:2", "sx:d1:3", "sx:d1:2", "xh1", "s:d0:2", "s:d1:1", "xh2", "xh3",
    "sx:d1:4", "xh4", "s:d0:12", "gg0", "s:d1:2", "s:d0:3", "gu0", "gg1", "xh5", "xo0",
    "s:g:1", "xo1", "s:d0:13", "s:d1:3", "mb0", "bk0", "s:g:2", "abf", "xo2", "s:d0:4",
    "xo3", "xo4", "s:u:1", "mb1", "go", "bk1", "s:u:2", "cvt", "xo5", "s:g:3",
    "gq0", "xt0", "s:d0:14", "s:d1:4", "e:d1", "gu1", "xt1", "xt2", "s:qkv:1", "s:g:4",
    "xt3", "s:o:12", "e:d0", "e:g", "gq1", "s:qkv:2", "xt4", "s:u:3", "xt5", "s:o:2",
    "s:qkv:3", "s:u:4", "e:u", "s:o:3", "nc", "ny", "s:qkv:4", "e:qkv", "s:o:13", "s:o:4",
    "s:o:14", "e:o", "ne", "end",
)


def dot_nn(left, right):
    return jnp.dot(left, right, preferred_element_type=F32)


def dot_nt(left, right):
    return lax.dot_general(left, right, (((1,), (1,)), ((), ())), preferred_element_type=F32)


def dot_tn(left, right):
    return lax.dot_general(left, right, (((0,), (0,)), ((), ())), preferred_element_type=F32)


def loop(count, body):
    def step(index, carry):
        body(index)
        return carry

    lax.fori_loop(0, count, step, 0)


def tile(index, size):
    return pl.ds(pl.multiple_of(index * size, size), size)


def only_half(values, half):
    lane = lax.broadcasted_iota(I32, values.shape, 1)
    keep = (lane < HEAD_DIM) if half == 0 else (lane >= HEAD_DIM)
    return jnp.where(keep, values, jnp.zeros_like(values))


def write_bias(bias, seg_col, seg_row, block, length):
    lanes = tile(block, BLOCK)
    keys = seg_col[0:length, :]
    key_pos = lax.broadcasted_iota(I32, (length, BLOCK), 0)
    query_pos = lax.broadcasted_iota(I32, (length, BLOCK), 1) + block * BLOCK
    same = jnp.concatenate([keys, keys], axis=1) == seg_row[0:1, lanes]
    bias[0:length, :] = jnp.where(same & (key_pos <= query_pos), 0.0, MASKED)


def attend_block(block, length, pairs, query, keys, vals_t, bias, seg_col, seg_row, mixed, mixed_t, log_sum):
    write_bias(bias, seg_col, seg_row, block, length)
    rows = tile(block, BLOCK)

    def pair(index):
        cols = tile(index, 2 * HEAD_DIM)
        two = query[rows, cols]
        for half in (0, 1):
            scores = dot_nt(keys[0:length, cols], only_half(two, half)) + bias[0:length, :]
            top = jnp.max(scores, axis=0, keepdims=True)
            expo = jnp.exp(scores - top)
            total = jnp.sum(expo, axis=0, keepdims=True)
            log_sum[2 * index + half, :, rows] = jnp.broadcast_to(top + jnp.log(total), (8, BLOCK))
            probs = (expo * (1.0 / total)).astype(BF)
            head = tile(2 * index + half, HEAD_DIM)
            mixed_t[head, :] = dot_nn(vals_t[head, 0:length], probs)

    loop(pairs, pair)
    mixed[rows, :] = mixed_t[...].T.astype(BF)


def attend_back_block(
    block, length, pairs, query, keys, keys_t, vals, grad_mixed, bias, seg_col, seg_row, log_sum, grad_qkv, grad_q_t, grad_k, grad_v
):
    write_bias(bias, seg_col, seg_row, block, length)
    rows = tile(block, BLOCK)

    def pair(index):
        cols = tile(index, 2 * HEAD_DIM)
        two = query[rows, cols]
        grad_two = grad_mixed[rows, cols]
        for half in (0, 1):
            one = only_half(two, half)
            grad_one = only_half(grad_two, half)
            scores = dot_nt(keys[0:length, cols], one) + bias[0:length, :]
            probs = jnp.exp(scores - log_sum[2 * index + half, 0:1, rows])
            grad_probs = dot_nt(vals[0:length, cols], grad_one)
            delta = jnp.sum(probs * grad_probs, axis=0, keepdims=True)
            grad_scores = (probs * (grad_probs - delta)).astype(BF)
            grad_v[0:length, cols] += dot_nn(probs.astype(BF), grad_one)
            grad_k[0:length, cols] += dot_nn(grad_scores, one)
            head = tile(2 * index + half, HEAD_DIM)
            grad_q_t[head, :] = dot_nn(keys_t[head, 0:length], grad_scores)

    loop(pairs, pair)
    grad_qkv[rows, 0 : grad_q_t.shape[0]] = (grad_q_t[...].T * SCALE).astype(BF)


def layer_kernel(
    nz,
    tok, cot, seg, gains, w_q, w_k, w_v, w_o, w_g, w_u, w_d,
    out, g_tok, o_q, o_k, o_v, o_o, o_g, o_u, o_d, o_gain,
    xg, cg, seg_row, gain_all, wqkv, wo, wg, wu, wd,
    h1, h2, ab, query, keys, vals, keys_t, vals_t, mixed, grad_mixed, grad_qkv, grad_k, grad_v,
    act_g, act_u, act_m, y1, bias, mixed_t, log_sum, seg_col,
    part, pair_sum, from_core, from_y, final_rows,
    p_d0, p_d1, p_g, p_u, p_o, p_qkv, r_d0, r_d1, r_g, r_u, r_o, r_qkv,
    s_d0, s_d1, s_g, s_u, s_o, s_qkv, f_d0, f_d1, f_g, f_u, f_o, f_qkv,
    p_n, s_n, f_n, c_n, y_n,
    send_sems, recv_sems, local_sems,
):
    fs = lax.axis_index("fsdp")
    y = lax.axis_index("ctx")
    t = lax.axis_index("tp")
    z = fs // 2
    x = lax.rem(fs, 2)
    width = xg.shape[1]
    half_len = xg.shape[0] // 2
    quarter = half_len // 2
    heads_w = query.shape[1]
    hidden = act_m.shape[1]
    db = width // (2 * nz)

    def dev(fq, yq, tq):
        return {"fsdp": fq, "ctx": yq, "tp": tq}

    x_dev = dev(2 * z + (1 - x), y, t)
    y_dev = dev(fs, 1 - y, t)
    c_dev = dev(fs, y, 1 - t)

    def z_from(k):
        return lax.rem(z + nz - k, nz)

    z_next = dev(2 * lax.rem(z + 1, nz) + x, y, t)

    barrier = pltpu.get_barrier_semaphore()
    plane = [(k, c) for k in range(nz) for c in (0, 1) if k or c]

    def plane_dev(k, c):
        return dev(2 * lax.rem(z + k, nz) + lax.rem(x + c, 2), y, t)

    for peer in [y_dev, c_dev] + [plane_dev(k, c) for k, c in plane]:
        pl.semaphore_signal(barrier, inc=1, device_id=peer, device_id_type=MESH)
    pl.semaphore_wait(barrier, 2 * nz + 1)

    count = {"send": 0, "recv": 0, "local": 0}
    sent = []

    def new(kind):
        count[kind] += 1
        return count[kind] - 1

    def send(src, dst, device, ridx):
        copy = pltpu.make_async_remote_copy(
            src, dst, send_sems.at[new("send")], recv_sems.at[ridx], device_id=device, device_id_type=MESH
        )
        copy.start()
        sent.append(copy)
        return copy

    def recv(dst, ridx):
        pltpu.make_async_remote_copy(
            dst, dst, send_sems.at[0], recv_sems.at[ridx], device_id=y_dev, device_id_type=MESH
        ).wait_recv()

    def local(src, dst):
        copy = pltpu.make_async_copy(src, dst, local_sems.at[new("local")])
        copy.start()
        return copy

    def many(number):
        return [new("recv") for _ in range(number)]

    def drain(copies):
        for copy in copies:
            copy.wait_send()
        gone = {id(copy) for copy in copies}
        sent[:] = [copy for copy in sent if id(copy) not in gone]

    hw = pl.ds(pl.multiple_of(y * heads_w, heads_w), heads_w)
    uw = pl.ds(pl.multiple_of(y * hidden, hidden), hidden)

    def rb(fq):
        return tile(fq, db)

    ub = db // 2

    def ub_rows(fq, part_of):
        return pl.ds(pl.multiple_of(fq * db + part_of * ub, ub), ub)

    names = {
        "qkv": (
            [w_q.at[:, hw], w_k.at[:, hw], w_v.at[:, hw]],
            lambda fq: [wqkv.at[rb(fq), i * heads_w : (i + 1) * heads_w] for i in range(3)],
            lambda fq: wqkv.at[rb(fq), :],
            False,
        ),
        "o": ([w_o.at[hw, :]], lambda fq: [wo.at[:, rb(fq)]], lambda fq: wo.at[:, rb(fq)], True),
        "g": ([w_g.at[:, uw]], lambda fq: [wg.at[rb(fq), :]], lambda fq: wg.at[rb(fq), :], False),
        "u0": (
            [w_u.at[0:ub, uw]], lambda fq: [wu.at[ub_rows(fq, 0), :]], lambda fq: wu.at[ub_rows(fq, 0), :], True,
        ),
        "u1": (
            [w_u.at[ub:db, uw]], lambda fq: [wu.at[ub_rows(fq, 1), :]], lambda fq: wu.at[ub_rows(fq, 1), :], False,
        ),
        "d": ([w_d.at[uw, :]], lambda fq: [wd.at[:, rb(fq)]], lambda fq: wd.at[:, rb(fq)], False),
    }
    first_z = {name: many(len(item[0])) for name, item in names.items()}
    first_x = {name: many(len(item[0])) for name, item in names.items()}
    ring_own = {name: [None, None] + many(nz - 2) for name in names}
    ring_other = {name: [None] + many(nz - 1) for name in names if names[name][3]}
    over_x = {name: [None] + many(nz - 1) for name in names if not names[name][3]}
    own_copy = {}

    def start_z(name):
        srcs, places = names[name][:2]
        own_copy[name] = [local(src, dst) for src, dst in zip(srcs, places(fs))]
        for src, dst, idx in zip(srcs, places(fs), first_z[name]):
            send(src, dst, z_next, idx)

    def start_x(name):
        srcs, places = names[name][:2]
        for src, dst, idx in zip(srcs, places(fs), first_x[name]):
            send(src, dst, x_dev, idx)

    def relay(name, k):
        places, place, pair_first = names[name][1:]
        fq = 2 * z_from(k) + x
        if k == 1:
            for dst, idx in zip(places(fq), first_z[name]):
                recv(dst, idx)
        else:
            recv(place(fq), ring_own[name][k])
        if k < nz - 1:
            send(place(fq), place(fq), z_next, ring_own[name][k + 1])
        if not pair_first:
            send(place(fq), place(fq), x_dev, over_x[name][k])

    def relay_other(name, k):
        places, place = names[name][1:3]
        fq = 2 * z_from(k) + (1 - x)
        if k == 0:
            for dst, idx in zip(places(fq), first_x[name]):
                recv(dst, idx)
        else:
            recv(place(fq), ring_other[name][k])
        if k < nz - 1:
            send(place(fq), place(fq), z_next, ring_other[name][k + 1])

    def relay_both(name, k):
        relay(name, k)
        relay_other(name, k)

    def arrived(name):
        places, place, pair_first = names[name][1:]
        for copy in own_copy[name]:
            copy.wait()
        if not pair_first:
            for dst, idx in zip(places(2 * z + (1 - x)), first_x[name]):
                recv(dst, idx)
            for k in range(1, nz):
                recv(place(2 * z_from(k) + (1 - x)), over_x[name][k])

    def rows_of(yq, tq):
        return pl.ds(pl.multiple_of(yq * half_len + tq * quarter, quarter), quarter)

    own_rows = rows_of(y, t)

    tok_y, tok_c, cot_y, cot_c, seg_y = many(5)
    n_idx = many(len(plane))
    n_local = local(gains, gain_all.at[fs])
    for (k, c), idx in zip(plane, n_idx):
        send(gains, gain_all.at[fs], plane_dev(k, c), idx)
    seg_local = local(seg, seg_row.at[:, tile(y, half_len)])
    send(seg, seg_row.at[:, tile(y, half_len)], y_dev, seg_y)
    tok_local = local(tok, xg.at[tile(y, half_len), :])
    cot_local = local(cot, cg.at[tile(y, half_len), :])

    far = rows_of(1 - y, t)
    far_other = rows_of(1 - y, 1 - t)

    def core_forward(ref, y_idx, c_idx):
        recv(ref.at[far, :], y_idx)
        return send(ref.at[far, :], ref.at[far, :], c_dev, c_idx)

    kinds = {"a": 0, "out": 1, "dh2": 2, "dh1": 3}
    ex_recv = {name: many(3) for name in kinds}
    ex_sent = []

    def exchange(name, compute, stage):
        e = kinds[name]
        if stage == 0:
            drain(ex_sent)
            ex_sent.clear()
            compute(far_other, part.at[0])
            ex_sent.append(send(part.at[0], from_core.at[e, 0], c_dev, ex_recv[name][0]))
        elif stage == 1:
            compute(far, part.at[1])
        elif stage == 2:
            recv(from_core.at[e, 0], ex_recv[name][0])

            def add(i):
                r = tile(i, 32)
                pair_sum[r, :] = (part[1, r, :].astype(F32) + from_core[e, 0, r, :].astype(F32)).astype(BF)

            loop(quarter // 32, add)
            ex_sent.append(send(pair_sum, from_y.at[e], y_dev, ex_recv[name][2]))
        elif stage == 3:
            compute(rows_of(y, 1 - t), part.at[2])
            ex_sent.append(send(part.at[2], from_core.at[e, 1], c_dev, ex_recv[name][1]))
        elif stage == 4:
            compute(own_rows, part.at[3])
        else:
            recv(from_core.at[e, 1], ex_recv[name][1])
            recv(from_y.at[e], ex_recv[name][2])

    def total_of(name, r):
        e = kinds[name]
        return part[3, r, :].astype(F32) + from_core[e, 1, r, :].astype(F32) + from_y[e, r, :].astype(F32)

    def spread_rows(ref, idx):
        return [
            send(ref.at[own_rows, :], ref.at[own_rows, :], c_dev, idx[0]),
            send(ref.at[own_rows, :], ref.at[own_rows, :], y_dev, idx[1]),
        ]

    h2_idx = many(3)
    ab_idx = many(3)

    grads = {
        "d0": (p_d0, r_d0, s_d0, f_d0, True),
        "d1": (p_d1, r_d1, s_d1, f_d1, False),
        "g": (p_g, r_g, s_g, f_g, False),
        "u": (p_u, r_u, s_u, f_u, False),
        "o": (p_o, r_o, s_o, f_o, True),
        "qkv": (p_qkv, r_qkv, s_qkv, f_qkv, False),
    }
    gx = {name: [None] + many(1 if item[4] else nz) for name, item in grads.items()}
    gz = {name: [[None] + many(nz - 1) for _ in range(2 if item[4] else 1)] for name, item in grads.items()}

    def add_rows(rows, cols, body):
        step = min(rows, 16 if cols > 512 else 128)
        loop(rows // step, lambda i: body(tile(i, step)))

    def grad_send(name, k):
        p, r, s, _, ring_first = grads[name]
        if ring_first:
            send(p.at[lax.rem(x + k, 2), z_from(1)], s.at[k - 1, 0], z_next, gz[name][k - 1][1])
        else:
            send(p.at[1 - x, z_from(k)], r.at[k - 1], x_dev, gx[name][k])

    def grad_step(name, k):
        p, r, s, f, ring_first = grads[name]
        if ring_first:
            c, k = divmod(k, 10)
            xq = lax.rem(x + 1 + c, 2)
            recv(s.at[c, k - 2], gz[name][c][k - 1])
            last_own = k == nz and c == 1
            if last_own:
                recv(r.at[0], gx[name][1])

            def add_ring(rr):
                total = p[xq, z_from(k), rr, :].astype(F32) + s[c, k - 2, rr, :].astype(F32)
                if last_own:
                    f[rr, :] = (total + r[0, rr, :].astype(F32)).astype(f.dtype)
                else:
                    p[xq, z_from(k), rr, :] = total.astype(p.dtype)

            add_rows(*p.shape[2:], add_ring)
            if k < nz:
                send(p.at[xq, z_from(k)], s.at[c, k - 1], z_next, gz[name][c][k])
            elif c == 0:
                send(p.at[xq, z_from(k)], r.at[0], x_dev, gx[name][1])
            return
        zq = z_from(k)
        recv(r.at[k - 1], gx[name][k])
        if k > 1:
            recv(s.at[0, k - 2], gz[name][0][k - 1])

        def add(rr):
            total = p[x, zq, rr, :].astype(F32) + r[k - 1, rr, :].astype(F32)
            if k > 1:
                total = total + s[0, k - 2, rr, :].astype(F32)
            if k < nz:
                p[x, zq, rr, :] = total.astype(p.dtype)
            else:
                f[rr, :] = total.astype(f.dtype)

        add_rows(*p.shape[2:], add)
        if k < nz:
            send(p.at[x, zq], s.at[0, k - 1], z_next, gz[name][0][k])

    part_h = hidden // 2

    def places_of(name, yq):
        h = pl.ds(pl.multiple_of(yq * heads_w, heads_w), heads_w)
        u = pl.ds(pl.multiple_of(yq * hidden, hidden), hidden)
        if name in ("d0", "d1"):
            return [o_d.at[pl.ds(pl.multiple_of(yq * hidden + (name == "d1") * part_h, part_h), part_h), :]]
        if name == "qkv":
            return [ref.at[:, h] for ref in (o_q, o_k, o_v)]
        return [{"g": o_g.at[:, u], "u": o_u.at[:, u], "o": o_o.at[h, :]}[name]]

    out_idx = {name: many(3 if name == "qkv" else 1) for name in grads}
    last_local = []

    def grad_end(name):
        f = grads[name][3]
        srcs = [f.at[:, i * heads_w : (i + 1) * heads_w] for i in range(3)] if name == "qkv" else [f]
        for src, dst, idx in zip(srcs, places_of(name, y), out_idx[name]):
            last_local.append(local(src, dst))
            send(src, dst, y_dev, idx)

    def grad_done(name):
        for ref, idx in zip(places_of(name, 1 - y), out_idx[name]):
            recv(ref, idx)

    value = {}
    blocks = half_len // BLOCK
    pairs = heads_w // (2 * HEAD_DIM)
    out_c, gtok_c = many(2)
    ng_idx = many(len(plane))
    n_c, n_y = many(2)
    my_rows = tile(t, quarter)
    other_rows = tile(1 - t, quarter)
    row_sends = []

    def send_tok():
        send(tok.at[tile(t, quarter), :], xg.at[own_rows, :], y_dev, tok_y)

    def send_cot():
        send(cot.at[tile(t, quarter), :], cg.at[own_rows, :], y_dev, cot_y)

    def gather_gains():
        n_local.wait()
        for (k, c), idx in zip(plane, n_idx):
            recv(gain_all.at[2 * z_from(k) + lax.rem(x + c, 2)], idx)
        value["one"] = jnp.concatenate([gain_all[i, 0:1, :] for i in range(2 * nz)], axis=1)
        value["two"] = jnp.concatenate([gain_all[i, 1:2, :] for i in range(2 * nz)], axis=1)

    def norm_rows(start):
        gain_one = value["one"]

        def body(i):
            r = pl.ds(pl.multiple_of(start + i * 32, 32), 32)
            values = xg[r, :].astype(F32)
            inverse = lax.rsqrt(jnp.mean(values * values, axis=-1, keepdims=True) + EPSILON)
            h1[r, :] = (values * inverse * gain_one).astype(BF)

        loop(half_len // 32, body)

    def norm_own():
        tok_local.wait()
        norm_rows(y * half_len)

    def norm_far():
        recv(xg.at[far_other, :], tok_c)
        norm_rows((1 - y) * half_len)

    def segments():
        seg_local.wait()
        recv(seg_row.at[:, tile(1 - y, half_len)], seg_y)
        seg_col[...] = jnp.broadcast_to(seg_row[0:1, :], (128, 2 * half_len)).T

    def project():
        def body(i):
            r = tile(i, 512)
            rows = h1[r, :]
            query[r, :] = (dot_nn(rows, wqkv[:, 0:heads_w]).astype(BF).astype(F32) * SCALE).astype(BF)
            keys[r, :] = dot_nn(rows, wqkv[:, heads_w : 2 * heads_w]).astype(BF)
            vals[r, :] = dot_nn(rows, wqkv[:, 2 * heads_w : 3 * heads_w]).astype(BF)

        loop(xg.shape[0] // 512, body)
        keys_t[...] = keys[...].T
        vals_t[...] = vals[...].T

    def either(half, body):
        @pl.when(half == 0)
        def _():
            body(half_len)

        @pl.when(half == 1)
        def _():
            body(2 * half_len)

    def attend(half):
        def block(i):
            args = (pairs, query, keys, vals_t, bias, seg_col, seg_row, mixed, mixed_t, log_sum)
            either(half, lambda length: attend_block(half * blocks + i, length, *args))

        loop(blocks, block)

    def out_rows(r, dst):
        dst[...] = dot_nn(mixed[r, :], wo[...]).astype(BF)

    def first_residual():
        exchange("a", None, 5)
        gain_two = value["two"]

        def body(i):
            r = tile(i, 32)
            rr = pl.ds(pl.multiple_of(y * half_len + t * quarter + i * 32, 32), 32)
            values = xg[rr, :].astype(F32) + total_of("a", r)
            y1[r, :] = values
            inverse = lax.rsqrt(jnp.mean(values * values, axis=-1, keepdims=True) + EPSILON)
            h2[rr, :] = (values * inverse * gain_two).astype(BF)

        loop(quarter // 32, body)
        row_sends.extend(spread_rows(h2, h2_idx))

    def gate(start):
        r = pl.ds(start, quarter)
        rows = h2[r, :]

        def cols(j):
            c = tile(j, 256)
            g = dot_nn(rows, wg[:, c])
            u = dot_nn(rows, wu[:, c])
            sg = 1.0 / (1.0 + jnp.exp(-g))
            gs = g * sg
            act_u[r, c] = gs.astype(BF)
            act_g[r, c] = (u * sg * (1.0 + g * (1.0 - sg))).astype(BF)
            act_m[r, c] = (gs * u).astype(BF)

        loop(hidden // 256, cols)

    def grad_cols(left, start, right, p, index):
        c = tile(index, 2 * db)
        for i in range(p.shape[2] // 256):
            r = slice(start + i * 256, start + (i + 1) * 256)
            both = dot_tn(left[:, r], right[:, c]).astype(BF)
            rows = slice(i * 256, (i + 1) * 256)
            p[0, index, rows, :] = both[:, 0:db]
            p[1, index, rows, :] = both[:, db : 2 * db]

    def grad_rows(left, right, p, index):
        c = tile(index, 2 * db)
        both = dot_tn(left[:, c], right[...]).astype(BF)
        p[0, index] = both[0:db, :]
        p[1, index] = both[db : 2 * db, :]

    def grad_down(part_of, p):
        loop(nz, lambda i: grad_cols(act_m, part_of * part_h, cg, p, i))

    def some_blocks(name, left, right, ks):
        p = grads[name][0]
        loop(len(ks), lambda i: grad_rows(left, right, p, z_from(ks[0] + i)))
        for k in ks:
            grad_send(name, k)

    def hidden_back(r, dst):
        rows = cg[r, :]

        def cols(j):
            c = tile(j, 256)
            dm = dot_nt(rows, wd[c, :])
            act_g[r, c] = (dm * act_g[r, c].astype(F32)).astype(BF)
            act_u[r, c] = (dm * act_u[r, c].astype(F32)).astype(BF)

        loop(hidden // 256, cols)

        def back(j):
            c = tile(j, 512)
            dst[:, c] = (dot_nt(act_g[r, :], wg[c, :]) + dot_nt(act_u[r, :], wu[c, :])).astype(BF)

        loop(width // 512, back)

    def second_residual():
        exchange("dh2", None, 5)
        gain_two = value["two"]

        def body(i, carry):
            r = tile(i, 32)
            rr = pl.ds(pl.multiple_of(y * half_len + t * quarter + i * 32, 32), 32)
            values = y1[r, :]
            inverse = lax.rsqrt(jnp.mean(values * values, axis=-1, keepdims=True) + EPSILON)
            normed = values * inverse
            grad = total_of("dh2", r)
            scaled = grad * gain_two
            mean = jnp.mean(scaled * normed, axis=-1, keepdims=True)
            full = cg[rr, :].astype(F32) + inverse * (scaled - normed * mean)
            final_rows[r, :] = full
            ab[rr, :] = full.astype(BF)
            return carry + jnp.sum(grad * normed, axis=0, keepdims=True)

        value["grad_two"] = lax.fori_loop(0, quarter // 32, body, jnp.zeros((1, width), F32))
        row_sends.extend(spread_rows(ab, ab_idx))

    def down_rows(r, dst):
        def cols(j):
            c = tile(j, 512)
            dst[:, c] = dot_nn(act_m[r, :], wd[:, c]).astype(BF)

        loop(width // 512, cols)

    def mixed_back(half):
        r = tile(half, half_len)
        grad_mixed[r, :] = dot_nt(ab[r, :], wo[...]).astype(BF)

    def clear_sums():
        grad_k[...] = jnp.zeros_like(grad_k)
        grad_v[...] = jnp.zeros_like(grad_v)

    def attend_back(half):
        def block(i):
            args = (
                pairs, query, keys, keys_t, vals, grad_mixed, bias, seg_col, seg_row, log_sum, grad_qkv, mixed_t, grad_k, grad_v,
            )
            either(half, lambda length: attend_back_block(half * blocks + i, length, *args))

        loop(blocks, block)

    def own_back():
        recv(ab.at[rows_of(y, 1 - t), :], ab_idx[0])
        clear_sums()
        mixed_back(y)

    def far_back():
        recv(ab.at[far_other, :], ab_idx[2])
        mixed_back(1 - y)

    def grad_out_all():
        loop(nz, lambda i: grad_cols(mixed, 0, ab, p_o, i))
        grad_send("o", 1)
        grad_send("o", 2)

    def sums_to_bf16():
        grad_qkv[:, heads_w : 2 * heads_w] = grad_k[...].astype(BF)
        grad_qkv[:, 2 * heads_w : 3 * heads_w] = grad_v[...].astype(BF)

    def hidden_one_back(r, dst):
        def cols(j):
            c = tile(j, 512)
            dst[:, c] = dot_nt(grad_qkv[r, :], wqkv[c, :]).astype(BF)

        loop(width // 512, cols)

    def finish_out():
        exchange("out", None, 5)

        def body(i):
            r = tile(i, 32)
            act_m[r, 0:width] = (y1[r, :] + total_of("out", r)).astype(BF)

        loop(quarter // 32, body)
        last_local.append(local(act_m.at[0:quarter, 0:width], out.at[my_rows, :]))
        send(act_m.at[0:quarter, 0:width], out.at[my_rows, :], c_dev, out_c)

    def finish_tokens():
        exchange("dh1", None, 5)
        drain(row_sends)
        gain_one = value["one"]

        def body(i, carry):
            r = tile(i, 32)
            rr = pl.ds(pl.multiple_of(y * half_len + t * quarter + i * 32, 32), 32)
            values = xg[rr, :].astype(F32)
            inverse = lax.rsqrt(jnp.mean(values * values, axis=-1, keepdims=True) + EPSILON)
            normed = values * inverse
            grad = total_of("dh1", r)
            scaled = grad * gain_one
            mean = jnp.mean(scaled * normed, axis=-1, keepdims=True)
            full = final_rows[r, :] + inverse * (scaled - normed * mean)
            h2[r, :] = full.astype(BF)
            return carry + jnp.sum(grad * normed, axis=0, keepdims=True)

        gain_one_grad = lax.fori_loop(0, quarter // 32, body, jnp.zeros((1, width), F32))
        for i in range(2 * nz):
            c = slice(i * db, (i + 1) * db)
            p_n[i % 2, i // 2] = jnp.concatenate(
                [gain_one_grad[:, c], value["grad_two"][:, c], jnp.zeros((6, db), F32)], axis=0
            )
        for i, (k, c) in enumerate(plane):
            send(p_n.at[lax.rem(x + c, 2), lax.rem(z + k, nz)], s_n.at[i], plane_dev(k, c), ng_idx[i])
        last_local.append(local(h2.at[0:quarter, :], g_tok.at[my_rows, :]))
        send(h2.at[0:quarter, :], g_tok.at[my_rows, :], c_dev, gtok_c)

    def gains_core():
        total = p_n[x, z]
        for i in range(len(plane)):
            recv(s_n.at[i], ng_idx[i])
            total = total + s_n[i]
        f_n[...] = total
        send(f_n, c_n, c_dev, n_c)

    def gains_y():
        recv(c_n, n_c)
        y_n[0] = f_n[...] + c_n[...]
        send(y_n.at[0], y_n.at[1], y_dev, n_y)

    def gains_end():
        recv(y_n.at[1], n_y)
        o_gain[...] = y_n[0] + y_n[1]

    def finish():
        for name in grads:
            grad_done(name)
        recv(out.at[other_rows, :], out_c)
        recv(g_tok.at[other_rows, :], gtok_c)
        for copy in last_local:
            copy.wait()
        drain(list(sent))

    tasks = {
        "tok": send_tok,
        "cot": send_cot,
        "gain": gather_gains,
        "tokf": lambda: core_forward(xg, tok_y, tok_c),
        "cotf": lambda: core_forward(cg, cot_y, cot_c),
        "cotr": lambda: (cot_local.wait(), recv(cg.at[far_other, :], cot_c)),
        "seg": segments,
        "n0": norm_own,
        "n1": norm_far,
        "proj": project,
        "at0": lambda: attend(1 - y),
        "at1": lambda: attend(y),
        "h2f": lambda: row_sends.append(core_forward(h2, h2_idx[1], h2_idx[2])),
        "xa5": first_residual,
        "gt0": lambda: gate(y * half_len + t * quarter),
        "gt1": lambda: (recv(h2.at[rows_of(y, 1 - t), :], h2_idx[0]), gate(y * half_len + (1 - t) * quarter)),
        "gt2": lambda: gate((1 - y) * half_len + t * quarter),
        "gt3": lambda: (recv(h2.at[far_other, :], h2_idx[2]), gate((1 - y) * half_len + (1 - t) * quarter)),
        "gd0": lambda: grad_down(0, p_d0),
        "gd1": lambda: grad_down(1, p_d1),
        "xh5": second_residual,
        "abf": lambda: row_sends.append(core_forward(ab, ab_idx[1], ab_idx[2])),
        "mb0": own_back,
        "mb1": far_back,
        "bk0": lambda: attend_back(y),
        "bk1": lambda: attend_back(1 - y),
        "go": grad_out_all,
        "cvt": sums_to_bf16,
        "xo5": finish_out,
        "xt5": finish_tokens,
        "nc": gains_core,
        "ny": gains_y,
        "ne": gains_end,
        "end": finish,
    }
    for i in range(5):
        tasks[f"xa{i}"] = functools.partial(exchange, "a", out_rows, i)
        tasks[f"xh{i}"] = functools.partial(exchange, "dh2", hidden_back, i)
        tasks[f"xo{i}"] = functools.partial(exchange, "out", down_rows, i)
        tasks[f"xt{i}"] = functools.partial(exchange, "dh1", hidden_one_back, i)
    for name in names:
        tasks["z:" + name] = functools.partial(start_z, name)
        tasks["x:" + name] = functools.partial(start_x, name)
        tasks["a:" + name] = functools.partial(arrived, name)
        for k in range(1, nz):
            tasks[f"r:{name}:{k}"] = functools.partial(relay, name, k)
        if names[name][3]:
            for k in range(nz):
                tasks[f"ro:{name}:{k}"] = functools.partial(relay_other, name, k)
    for name in grads:
        tasks["e:" + name] = functools.partial(grad_end, name)
        if grads[name][4]:
            for c in (0, 1):
                for k in range(2, nz + 1):
                    tasks[f"s:{name}:{10 * c + k}"] = functools.partial(grad_step, name, 10 * c + k)
        else:
            for k in range(1, nz + 1):
                tasks[f"s:{name}:{k}"] = functools.partial(grad_step, name, k)
    for name in ("d0", "d1"):
        for k in (1, 2) if grads[name][4] else range(1, nz + 1):
            tasks[f"sx:{name}:{k}"] = functools.partial(grad_send, name, k)
    for i, ks in enumerate(((1, 2), (3, 4))):
        tasks[f"gg{i}"] = functools.partial(some_blocks, "g", h2, act_g, ks)
        tasks[f"gu{i}"] = functools.partial(some_blocks, "u", h2, act_u, ks)
        tasks[f"gq{i}"] = functools.partial(some_blocks, "qkv", h1, grad_qkv, ks)
    for name in ORDER:
        tasks.pop(name)()
    assert not tasks


def fused(nz, tokens, segment_ids, w_query, w_key, w_value, w_out, w_gate, w_up, w_down, gain_attn, gain_ffn, cotangent):
    half_len, _, width = tokens.shape
    length = 2 * half_len
    quarter = half_len // 2
    heads_w = w_query.shape[1] // 2
    hidden = w_gate.shape[1] // 2
    db = w_query.shape[0]
    heads = heads_w // HEAD_DIM
    gains = jnp.concatenate(
        [gain_attn.astype(F32)[None], gain_ffn.astype(F32)[None], jnp.zeros((6, db), F32)], axis=0
    )
    seg = jnp.broadcast_to(segment_ids, (8, half_len))

    def vm(*shape, dtype=BF):
        return pltpu.VMEM(shape, dtype)

    shape_d, shape_g, shape_o, shape_qkv = (hidden // 2, db), (db, hidden), (heads_w, db), (db, 3 * heads_w)
    shapes = (shape_d, shape_d, shape_g, shape_g, shape_o, shape_qkv)
    ring_first = (True, False, False, False, True, False)
    scratch = [
        vm(length, width), vm(length, width), vm(8, length, dtype=I32), vm(2 * nz, 8, db, dtype=F32),
        vm(width, 3 * heads_w), vm(heads_w, width), vm(width, hidden), vm(width, hidden), vm(hidden, width),
        vm(length, width), vm(length, width), vm(length, width),
        vm(length, heads_w), vm(length, heads_w), vm(length, heads_w), vm(heads_w, length), vm(heads_w, length),
        vm(length, heads_w), vm(length, heads_w), vm(length, 3 * heads_w),
        vm(length, heads_w, dtype=F32), vm(length, heads_w, dtype=F32),
        vm(length, hidden), vm(length, hidden), vm(length, hidden),
        vm(quarter, width, dtype=F32), vm(length, BLOCK, dtype=F32), vm(heads_w, BLOCK, dtype=F32),
        vm(heads, 8, length, dtype=F32), vm(length, 128, dtype=I32),
        vm(4, quarter, width), vm(quarter, width), vm(4, 2, quarter, width), vm(4, quarter, width),
        vm(quarter, width, dtype=F32),
    ]
    scratch += [vm(2, nz, *shape) for shape in shapes]
    scratch += [vm(1 if first else nz, *shape) for shape, first in zip(shapes, ring_first)]
    scratch += [vm(2 if first else 1, nz - 1, *shape) for shape, first in zip(shapes, ring_first)]
    scratch += [vm(*shape) for shape in shapes]
    scratch += [
        vm(2, nz, 8, db, dtype=F32), vm(2 * nz - 1, 8, db, dtype=F32), vm(8, db, dtype=F32),
        vm(8, db, dtype=F32), vm(2, 8, db, dtype=F32),
    ]
    scratch += [pltpu.SemaphoreType.DMA((192,)), pltpu.SemaphoreType.DMA((192,)), pltpu.SemaphoreType.DMA((48,))]
    anywhere = pl.BlockSpec(memory_space=pl.ANY)
    weights = (w_query, w_key, w_value, w_out, w_gate, w_up, w_down)
    results = pl.pallas_call(
        functools.partial(layer_kernel, nz),
        out_shape=[jax.ShapeDtypeStruct((half_len, width), BF)] * 2
        + [jax.ShapeDtypeStruct(item.shape, BF) for item in weights]
        + [jax.ShapeDtypeStruct((8, db), F32)],
        in_specs=[anywhere] * 11,
        out_specs=[anywhere] * 9 + [pl.BlockSpec(memory_space=pltpu.VMEM)],
        scratch_shapes=scratch,
        compiler_params=pltpu.CompilerParams(
            collective_id=0, has_side_effects=True, vmem_limit_bytes=VMEM_BYTES
        ),
        name="layer",
    )(tokens.reshape(half_len, width), cotangent.reshape(half_len, width), seg, gains, *weights)
    shape = tokens.shape
    return (
        results[0].reshape(shape),
        results[1].reshape(shape),
        *[item.astype(F32) for item in results[2:9]],
        results[9][0],
        results[9][1],
    )


def fits(mesh, tokens_shape):
    return mesh.shape["fsdp"] == 8 and mesh.shape["ctx"] == 2 and mesh.shape["tp"] == 2 and tokens_shape[1:] == (1, 1024)


def solution(mesh):
    def step(tokens, *rest):
        if fits(mesh, tokens.shape):
            return fused(mesh.shape["fsdp"] // 2, tokens, *rest)
        return local(tokens, *rest)

    return jax.shard_map(
        step,
        mesh=mesh,
        in_specs=(
            P("ctx", "fsdp", None),
            P("fsdp", "ctx"),
            P("fsdp", "tp"),
            P("fsdp", "tp"),
            P("fsdp", "tp"),
            P("tp", "fsdp"),
            P("fsdp", "tp"),
            P("fsdp", "tp"),
            P("tp", "fsdp"),
            P("fsdp"),
            P("fsdp"),
            P("ctx", "fsdp", None),
        ),
        out_specs=(
            P("ctx", "fsdp", None),
            P("ctx", "fsdp", None),
            P("fsdp", "tp"),
            P("fsdp", "tp"),
            P("fsdp", "tp"),
            P("tp", "fsdp"),
            P("fsdp", "tp"),
            P("fsdp", "tp"),
            P("tp", "fsdp"),
            P("fsdp"),
            P("fsdp"),
        ),
        check_vma=False,
    )
```

```python
import functools

import jax
import jax.numpy as jnp
from jax import lax
from jax.experimental import pallas as pl
from jax.experimental.pallas import tpu as pltpu
from jax.sharding import PartitionSpec as P

HEAD_DIM = 64


EPSILON = 1e-05
SCALE = 0.125
MASKED = -1e30


def normalize(values):
    inverse = lax.rsqrt(jnp.mean(values * values, axis=-1, keepdims=True) + EPSILON)
    return (values * inverse, inverse)


def norm_back(grad_normed, normed, inverse):
    return inverse * (grad_normed - normed * jnp.mean(grad_normed * normed, axis=-1, keepdims=True))


def inner_rows(left, right):
    return lax.dot_general(
        left, right, (((0,), (0,)), ((), ())), preferred_element_type=jnp.float32
    )


def times_transposed(left, weight):
    return lax.dot_general(
        left, weight, (((1,), (1,)), ((), ())), preferred_element_type=jnp.float32
    )


def head_sum(partial_sum):
    return lax.psum(partial_sum, "tp")


def split_heads(values, head_size):
    length, sequences, width = values.shape
    return jnp.moveaxis(values.reshape(length, sequences, width // head_size, head_size), 2, 0)


def join_heads(values):
    heads, length, sequences, head_size = values.shape
    return jnp.moveaxis(values, 0, 2).reshape(length, sequences, heads * head_size)


def make_mask(query_pos, query_seg, key_pos, key_seg):
    before = key_pos[None, None, :] <= query_pos[None, :, None]
    same = query_seg.T[:, :, None] == key_seg.T[:, None, :]
    return before & same


def key_head_grads(parts, use_mask):
    q_head, k_head, v_head, d_head, log_total, delta = parts
    scores = jnp.einsum("qsd,ksd->sqk", q_head, k_head, preferred_element_type=jnp.float32) * SCALE
    probs = jnp.exp(jnp.where(use_mask, scores, MASKED) - log_total)
    grad_probs = jnp.einsum("qsd,ksd->sqk", d_head, v_head, preferred_element_type=jnp.float32)
    grad_scores = (probs * (grad_probs - delta)).astype(jnp.bfloat16)
    grad_v = jnp.einsum(
        "sqk,qsd->ksd", probs.astype(jnp.bfloat16), d_head, preferred_element_type=jnp.float32
    )
    grad_k = (
        jnp.einsum("sqk,qsd->ksd", grad_scores, q_head, preferred_element_type=jnp.float32) * SCALE
    )
    return (grad_k, grad_v)


def local(
    tokens,
    segment_ids,
    w_query,
    w_key,
    w_value,
    w_out,
    w_gate,
    w_up,
    w_down,
    gain_attn,
    gain_ffn,
    cotangent,
):
    local_len, sequences, width = tokens.shape
    rows = local_len * sequences
    (
        full_query,
        full_key,
        full_value,
        full_out,
        full_gate,
        full_up,
        full_down,
        full_gain_one,
        full_gain_two,
    ) = (
        lax.all_gather(w_query, "fsdp", axis=0, tiled=True),
        lax.all_gather(w_key, "fsdp", axis=0, tiled=True),
        lax.all_gather(w_value, "fsdp", axis=0, tiled=True),
        lax.all_gather(w_out, "fsdp", axis=1, tiled=True),
        lax.all_gather(w_gate, "fsdp", axis=0, tiled=True),
        lax.all_gather(w_up, "fsdp", axis=0, tiled=True),
        lax.all_gather(w_down, "fsdp", axis=1, tiled=True),
        lax.all_gather(gain_attn, "fsdp", axis=0, tiled=True),
        lax.all_gather(gain_ffn, "fsdp", axis=0, tiled=True),
    )
    gain_one = full_gain_one.astype(jnp.float32)
    gain_two = full_gain_two.astype(jnp.float32)
    head_width = full_query.shape[1]
    flat = tokens.astype(jnp.float32).reshape(rows, width)
    normed_one, inverse_one = normalize(flat)
    hidden_one = (normed_one * gain_one).astype(jnp.bfloat16)
    query = (
        jnp.dot(hidden_one, full_query, preferred_element_type=jnp.float32)
        .astype(jnp.bfloat16)
        .reshape(local_len, sequences, head_width)
    )
    keys = (
        jnp.dot(hidden_one, full_key, preferred_element_type=jnp.float32)
        .astype(jnp.bfloat16)
        .reshape(local_len, sequences, head_width)
    )
    vals = (
        jnp.dot(hidden_one, full_value, preferred_element_type=jnp.float32)
        .astype(jnp.bfloat16)
        .reshape(local_len, sequences, head_width)
    )
    pair = jnp.concatenate([keys, vals], axis=-1)
    seg_local = segment_ids.T
    pair_all, seg_all = (
        lax.all_gather(pair, "ctx", axis=0, tiled=True),
        lax.all_gather(seg_local, "ctx", axis=0, tiled=True),
    )
    length = pair_all.shape[0]
    query_pos = lax.axis_index("ctx") * local_len + jnp.arange(local_len, dtype=jnp.int32)
    all_pos = jnp.arange(length, dtype=jnp.int32)
    mask = make_mask(query_pos, seg_local, all_pos, seg_all)
    q_heads = split_heads(query, HEAD_DIM)
    k_heads = split_heads(pair_all[..., :head_width], HEAD_DIM)
    v_heads = split_heads(pair_all[..., head_width:], HEAD_DIM)

    def attend(parts):
        q_head, k_head, v_head = parts
        scores = (
            jnp.einsum("qsd,ksd->sqk", q_head, k_head, preferred_element_type=jnp.float32) * SCALE
        )
        scores = jnp.where(mask, scores, MASKED)
        row_max = jnp.max(scores, axis=-1, keepdims=True)
        log_total = row_max + jnp.log(jnp.sum(jnp.exp(scores - row_max), axis=-1, keepdims=True))
        probs = jnp.exp(scores - log_total).astype(jnp.bfloat16)
        return (
            jnp.einsum("sqk,ksd->qsd", probs, v_head, preferred_element_type=jnp.float32),
            log_total,
        )

    attended, log_totals = lax.map(attend, (q_heads, k_heads, v_heads))
    mixed = join_heads(attended).astype(jnp.bfloat16).reshape(rows, head_width)
    resid = flat + head_sum(jnp.dot(mixed, full_out, preferred_element_type=jnp.float32))
    normed_two, inverse_two = normalize(resid)
    hidden_two = (normed_two * gain_two).astype(jnp.bfloat16)
    gate = jnp.dot(hidden_two, full_gate, preferred_element_type=jnp.float32)
    upward = jnp.dot(hidden_two, full_up, preferred_element_type=jnp.float32)
    sigmoid_gate = jax.nn.sigmoid(gate)
    swish_up = (gate * sigmoid_gate * upward).astype(jnp.bfloat16)
    result = resid + head_sum(jnp.dot(swish_up, full_down, preferred_element_type=jnp.float32))
    output = result.astype(jnp.bfloat16).reshape(local_len, sequences, width)
    (
        full_query,
        full_key,
        full_value,
        full_out,
        full_gate,
        full_up,
        full_down,
        full_gain_one,
        full_gain_two,
    ) = (
        lax.all_gather(w_query, "fsdp", axis=0, tiled=True),
        lax.all_gather(w_key, "fsdp", axis=0, tiled=True),
        lax.all_gather(w_value, "fsdp", axis=0, tiled=True),
        lax.all_gather(w_out, "fsdp", axis=1, tiled=True),
        lax.all_gather(w_gate, "fsdp", axis=0, tiled=True),
        lax.all_gather(w_up, "fsdp", axis=0, tiled=True),
        lax.all_gather(w_down, "fsdp", axis=1, tiled=True),
        lax.all_gather(gain_attn, "fsdp", axis=0, tiled=True),
        lax.all_gather(gain_ffn, "fsdp", axis=0, tiled=True),
    )
    gain_one = full_gain_one.astype(jnp.float32)
    gain_two = full_gain_two.astype(jnp.float32)
    grad_result = cotangent.astype(jnp.float32).reshape(rows, width)
    grad_low = grad_result.astype(jnp.bfloat16)
    grad_wdown = inner_rows(swish_up, grad_low)
    grad_swish = times_transposed(grad_low, full_down)
    grad_gate_act = (
        grad_swish * upward * sigmoid_gate * (1.0 + gate * (1.0 - sigmoid_gate))
    ).astype(jnp.bfloat16)
    grad_upward = (grad_swish * gate * sigmoid_gate).astype(jnp.bfloat16)
    grad_wgate = inner_rows(hidden_two, grad_gate_act)
    grad_wup = inner_rows(hidden_two, grad_upward)
    grad_hidden_two = head_sum(
        times_transposed(grad_gate_act, full_gate) + times_transposed(grad_upward, full_up)
    )
    grad_gain_two = jnp.sum(grad_hidden_two * normed_two, axis=0)
    grad_resid = grad_result + norm_back(grad_hidden_two * gain_two, normed_two, inverse_two)
    grad_branch = grad_resid.astype(jnp.bfloat16)
    grad_wout = inner_rows(mixed, grad_branch)
    grad_mixed = (
        times_transposed(grad_branch, full_out)
        .astype(jnp.bfloat16)
        .reshape(local_len, sequences, head_width)
    )
    d_heads = split_heads(grad_mixed, HEAD_DIM)

    def query_side(parts):
        q_head, k_head, v_head, d_head, log_total = parts
        scores = (
            jnp.einsum("qsd,ksd->sqk", q_head, k_head, preferred_element_type=jnp.float32) * SCALE
        )
        probs = jnp.exp(jnp.where(mask, scores, MASKED) - log_total)
        grad_probs = jnp.einsum("qsd,ksd->sqk", d_head, v_head, preferred_element_type=jnp.float32)
        delta = jnp.sum(probs * grad_probs, axis=-1, keepdims=True)
        grad_scores = (probs * (grad_probs - delta)).astype(jnp.bfloat16)
        return (
            jnp.einsum("sqk,ksd->qsd", grad_scores, k_head, preferred_element_type=jnp.float32)
            * SCALE,
            delta,
        )

    grad_q_heads, deltas = lax.map(query_side, (q_heads, k_heads, v_heads, d_heads, log_totals))
    grad_query = join_heads(grad_q_heads).astype(jnp.bfloat16).reshape(rows, head_width)
    piece_mask = make_mask(
        query_pos, seg_local, jnp.arange(local_len * lax.axis_size("ctx"), dtype=jnp.int32), seg_all
    )
    k_piece = split_heads(pair_all[..., :head_width], HEAD_DIM)
    v_piece = split_heads(pair_all[..., head_width:], HEAD_DIM)

    def per_head(parts):
        return key_head_grads(parts, piece_mask)

    grad_k_heads, grad_v_heads = lax.map(
        per_head, (q_heads, k_piece, v_piece, d_heads, log_totals, deltas)
    )
    grad_pair = lax.psum_scatter(
        jnp.concatenate([join_heads(grad_k_heads), join_heads(grad_v_heads)], axis=-1).astype(
            jnp.bfloat16
        ),
        "ctx",
        scatter_dimension=0,
        tiled=True,
    ).astype(jnp.float32)
    grad_keys = grad_pair[..., :head_width].astype(jnp.bfloat16).reshape(rows, head_width)
    grad_vals = grad_pair[..., head_width:].astype(jnp.bfloat16).reshape(rows, head_width)
    grad_wquery = inner_rows(hidden_one, grad_query)
    grad_wkey = inner_rows(hidden_one, grad_keys)
    grad_wvalue = inner_rows(hidden_one, grad_vals)
    grad_hidden_one = head_sum(
        times_transposed(grad_query, full_query)
        + times_transposed(grad_keys, full_key)
        + times_transposed(grad_vals, full_value)
    )
    grad_gain_one = jnp.sum(grad_hidden_one * normed_one, axis=0)
    grad_input = grad_resid + norm_back(grad_hidden_one * gain_one, normed_one, inverse_one)
    grad_input = grad_input.astype(jnp.bfloat16).reshape(local_len, sequences, width)
    shares = (
        lax.psum_scatter(
            grad_wquery.astype(jnp.bfloat16), "fsdp", scatter_dimension=0, tiled=True
        ).astype(jnp.float32),
        lax.psum_scatter(
            grad_wkey.astype(jnp.bfloat16), "fsdp", scatter_dimension=0, tiled=True
        ).astype(jnp.float32),
        lax.psum_scatter(
            grad_wvalue.astype(jnp.bfloat16), "fsdp", scatter_dimension=0, tiled=True
        ).astype(jnp.float32),
        lax.psum_scatter(
            grad_wout.astype(jnp.bfloat16), "fsdp", scatter_dimension=1, tiled=True
        ).astype(jnp.float32),
        lax.psum_scatter(
            grad_wgate.astype(jnp.bfloat16), "fsdp", scatter_dimension=0, tiled=True
        ).astype(jnp.float32),
        lax.psum_scatter(
            grad_wup.astype(jnp.bfloat16), "fsdp", scatter_dimension=0, tiled=True
        ).astype(jnp.float32),
        lax.psum_scatter(
            grad_wdown.astype(jnp.bfloat16), "fsdp", scatter_dimension=1, tiled=True
        ).astype(jnp.float32),
        lax.psum_scatter(
            grad_gain_one.astype(jnp.bfloat16), "fsdp", scatter_dimension=0, tiled=True
        ).astype(jnp.float32),
        lax.psum_scatter(
            grad_gain_two.astype(jnp.bfloat16), "fsdp", scatter_dimension=0, tiled=True
        ).astype(jnp.float32),
    )
    shares = (
        lax.psum(shares[0].astype(jnp.bfloat16), "ctx").astype(jnp.float32),
        lax.psum(shares[1].astype(jnp.bfloat16), "ctx").astype(jnp.float32),
        lax.psum(shares[2].astype(jnp.bfloat16), "ctx").astype(jnp.float32),
        lax.psum(shares[3].astype(jnp.bfloat16), "ctx").astype(jnp.float32),
        lax.psum(shares[4].astype(jnp.bfloat16), "ctx").astype(jnp.float32),
        lax.psum(shares[5].astype(jnp.bfloat16), "ctx").astype(jnp.float32),
        lax.psum(shares[6].astype(jnp.bfloat16), "ctx").astype(jnp.float32),
        lax.psum(shares[7].astype(jnp.bfloat16), "ctx").astype(jnp.float32),
        lax.psum(shares[8].astype(jnp.bfloat16), "ctx").astype(jnp.float32),
    )
    return (
        output,
        grad_input,
        shares[0],
        shares[1],
        shares[2],
        shares[3],
        shares[4],
        shares[5],
        shares[6],
        shares[7],
        shares[8],
    )


BF = jnp.bfloat16
F32 = jnp.float32
I32 = jnp.int32
MESH = pl.DeviceIdType.MESH
BLOCK = 256
VMEM_BYTES = 67043328
ORDER = (
    72, 101, 61, 117, 60, 1, 110, 66, 63, 78, 67, 84, 69, 6, 106, 87, 70, 0, 81, 85, 75, 71, 73, 64,
    88, 82, 65, 79, 4, 76, 90, 94, 83, 3, 91, 100, 62, 86, 77, 2, 7, 8, 74, 80, 113, 68, 89, 9,
    92, 97, 95, 10, 93, 116, 103, 107, 40, 41, 114, 42, 111, 98, 102, 11, 43, 44, 104, 119, 115, 108, 12, 105,
    99, 112, 13, 120, 5, 96, 109, 14, 15, 17, 121, 16, 18, 166, 19, 168, 170, 169, 167, 118, 50, 171, 51, 126,
    130, 123, 52, 53, 54, 34, 131, 124, 127, 36, 20, 135, 125, 45, 37, 22, 132, 35, 46, 140, 136, 47, 21, 24,
    23, 26, 48, 141, 133, 129, 25, 49, 28, 145, 27, 148, 55, 38, 142, 128, 122, 172, 39, 146, 177, 180, 56, 176,
    57, 137, 58, 147, 59, 143, 162, 181, 149, 173, 174, 182, 152, 139, 29, 138, 175, 150, 157, 153, 144, 134, 163, 178,
    30, 158, 154, 183, 164, 31, 179, 159, 155, 151, 165, 161, 32, 160, 156, 33,
)
SEMS = (48, 161, 22)


def dot_nn(left, right):
    return jnp.dot(left, right, preferred_element_type=F32)


def dot_nt(left, right):
    return lax.dot_general(left, right, (((1,), (1,)), ((), ())), preferred_element_type=F32)


def dot_tn(left, right):
    return lax.dot_general(left, right, (((0,), (0,)), ((), ())), preferred_element_type=F32)


def loop(count, body):
    def step(index, carry):
        body(index)
        return carry

    lax.fori_loop(0, count, step, 0)


def tile(index, size):
    return pl.ds(pl.multiple_of(index * size, size), size)


def only_half(values, half):
    lane = lax.broadcasted_iota(I32, values.shape, 1)
    keep = (lane < HEAD_DIM) if half == 0 else (lane >= HEAD_DIM)
    return jnp.where(keep, values, jnp.zeros_like(values))


def write_bias(bias, seg_col, seg_row, block, length):
    lanes = tile(block, BLOCK)
    keys = seg_col[0:length, :]
    key_pos = lax.broadcasted_iota(I32, (length, BLOCK), 0)
    query_pos = lax.broadcasted_iota(I32, (length, BLOCK), 1) + block * BLOCK
    same = jnp.concatenate([keys, keys], axis=1) == seg_row[0:1, lanes]
    bias[0:length, :] = jnp.where(same & (key_pos <= query_pos), 0.0, MASKED)


def attend_block(block, length, pairs, query, keys, vals_t, bias, seg_col, seg_row, mixed, mixed_t, log_sum):
    write_bias(bias, seg_col, seg_row, block, length)
    rows = tile(block, BLOCK)

    def pair(index):
        cols = tile(index, 2 * HEAD_DIM)
        two = query[rows, cols]
        for half in (0, 1):
            scores = dot_nt(keys[0:length, cols], only_half(two, half)) + bias[0:length, :]
            top = jnp.max(scores, axis=0, keepdims=True)
            expo = jnp.exp(scores - top)
            total = jnp.sum(expo, axis=0, keepdims=True)
            log_sum[2 * index + half, :, rows] = jnp.broadcast_to(top + jnp.log(total), (8, BLOCK))
            probs = (expo * (1.0 / total)).astype(BF)
            head = tile(2 * index + half, HEAD_DIM)
            mixed_t[head, :] = dot_nn(vals_t[head, 0:length], probs)

    loop(pairs, pair)
    mixed[rows, :] = mixed_t[...].T.astype(BF)


def attend_back_block(
    block, length, pairs, query, keys, keys_t, vals, grad_mixed, bias, seg_col, seg_row, log_sum, grad_qkv, grad_q_t, grad_k, grad_v
):
    write_bias(bias, seg_col, seg_row, block, length)
    rows = tile(block, BLOCK)

    def pair(index):
        cols = tile(index, 2 * HEAD_DIM)
        two = query[rows, cols]
        grad_two = grad_mixed[rows, cols]
        for half in (0, 1):
            one = only_half(two, half)
            grad_one = only_half(grad_two, half)
            scores = dot_nt(keys[0:length, cols], one) + bias[0:length, :]
            probs = jnp.exp(scores - log_sum[2 * index + half, 0:1, rows])
            grad_probs = dot_nt(vals[0:length, cols], grad_one)
            delta = jnp.sum(probs * grad_probs, axis=0, keepdims=True)
            grad_scores = (probs * (grad_probs - delta)).astype(BF)
            grad_v[0:length, cols] += dot_nn(probs.astype(BF), grad_one)
            grad_k[0:length, cols] += dot_nn(grad_scores, one)
            head = tile(2 * index + half, HEAD_DIM)
            grad_q_t[head, :] = dot_nn(keys_t[head, 0:length], grad_scores)

    loop(pairs, pair)
    grad_qkv[rows, 0 : grad_q_t.shape[0]] = (grad_q_t[...].T * SCALE).astype(BF)


def layer_kernel(
    nz,
    tok, cot, seg, gains, w_q, w_k, w_v, w_o, w_g, w_u, w_d,
    out, g_tok, o_q, o_k, o_v, o_o, o_g, o_u, o_d, o_gain,
    xg, cg, seg_row, gain_all, wqkv, wo, wg, wu, wd,
    h1, h2, ab, query, keys, vals, keys_t, vals_t, mixed, grad_mixed, grad_qkv, grad_k, grad_v,
    act_g, act_u, act_m, y1, bias, mixed_t, log_sum, seg_col,
    part, pair_sum, from_core, from_y, final_rows,
    p_d0, p_d1, p_g, p_u, p_o, p_q, p_k, p_v, r_d0, r_d1, r_g, r_u, r_o, r_q, r_k, r_v,
    s_d0, s_d1, s_g, s_u, s_o, s_q, s_k, s_v, f_d0, f_d1, f_g, f_u, f_o, f_q, f_k, f_v,
    p_n, s_n, f_n, c_n, y_n,
    send_sems, recv_sems, local_sems,
):
    fs = lax.axis_index("fsdp")
    y = lax.axis_index("ctx")
    t = lax.axis_index("tp")
    z = fs // 2
    x = lax.rem(fs, 2)
    width = xg.shape[1]
    half_len = xg.shape[0] // 2
    quarter = half_len // 2
    heads_w = query.shape[1]
    hidden = act_m.shape[1]
    db = width // (2 * nz)

    def dev(fq, yq, tq):
        return {"fsdp": fq, "ctx": yq, "tp": tq}

    x_dev = dev(2 * z + (1 - x), y, t)
    y_dev = dev(fs, 1 - y, t)
    c_dev = dev(fs, y, 1 - t)

    def z_from(k):
        return lax.rem(z + nz - k, nz)

    z_next = dev(2 * lax.rem(z + 1, nz) + x, y, t)

    barrier = pltpu.get_barrier_semaphore()
    plane = [(k, c) for k in range(nz) for c in (0, 1) if k or c]

    def plane_dev(k, c):
        return dev(2 * lax.rem(z + k, nz) + lax.rem(x + c, 2), y, t)

    for peer in [y_dev, c_dev] + [plane_dev(k, c) for k, c in plane]:
        pl.semaphore_signal(barrier, inc=1, device_id=peer, device_id_type=MESH)
    pl.semaphore_wait(barrier, 2 * nz + 1)

    count = {"send": 0, "recv": 0, "local": 0}
    sent = []

    def new(kind):
        count[kind] += 1
        return count[kind] - 1

    slots = [None] * SEMS[0]

    def send(src, dst, device, ridx):
        slot = new("send") % SEMS[0]
        if slots[slot] is not None:
            drain([copy for copy in sent if copy is slots[slot]])
        copy = pltpu.make_async_remote_copy(
            src, dst, send_sems.at[slot], recv_sems.at[ridx], device_id=device, device_id_type=MESH
        )
        slots[slot] = copy
        copy.start()
        sent.append(copy)
        return copy

    def recv(dst, ridx):
        pltpu.make_async_remote_copy(
            dst, dst, send_sems.at[0], recv_sems.at[ridx], device_id=y_dev, device_id_type=MESH
        ).wait_recv()

    def local(src, dst):
        copy = pltpu.make_async_copy(src, dst, local_sems.at[new("local")])
        copy.start()
        return copy

    def many(number):
        return [new("recv") for _ in range(number)]

    def drain(copies):
        left = [copy for copy in sent if any(copy is other for other in copies)]
        for copy in left:
            copy.wait_send()
        sent[:] = [copy for copy in sent if not any(copy is other for other in left)]

    hw = pl.ds(pl.multiple_of(y * heads_w, heads_w), heads_w)
    uw = pl.ds(pl.multiple_of(y * hidden, hidden), hidden)

    def rb(fq):
        return tile(fq, db)

    ub = db // 2

    def ub_rows(fq, part_of):
        return pl.ds(pl.multiple_of(fq * db + part_of * ub, ub), ub)

    names = {
        "n": (gains, lambda fq: gain_all.at[fq], False),
        "q": (w_q.at[:, hw], lambda fq: wqkv.at[rb(fq), 0:heads_w], False),
        "k": (w_k.at[:, hw], lambda fq: wqkv.at[rb(fq), heads_w : 2 * heads_w], False),
        "v": (w_v.at[:, hw], lambda fq: wqkv.at[rb(fq), 2 * heads_w : 3 * heads_w], False),
        "o": (w_o.at[hw, :], lambda fq: wo.at[:, rb(fq)], True),
        "g": (w_g.at[:, uw], lambda fq: wg.at[rb(fq), :], False),
        "u0": (w_u.at[0:ub, uw], lambda fq: wu.at[ub_rows(fq, 0), :], True),
        "u1": (w_u.at[ub:db, uw], lambda fq: wu.at[ub_rows(fq, 1), :], False),
        "d": (w_d.at[uw, :], lambda fq: wd.at[:, rb(fq)], False),
    }
    ring_own = {name: [None] + many(nz - 1) for name in names}
    ring_other = {name: [None] + many(nz - 1) for name in names if names[name][2]}
    over_x = {name: many(1 if names[name][2] else nz) for name in names}
    own_copy = {}

    def start_z(name):
        src, place, _ = names[name]
        own_copy[name] = local(src, place(fs))
        send(src, place(fs), z_next, ring_own[name][1])

    def start_x(name):
        src, place, _ = names[name]
        send(src, place(fs), x_dev, over_x[name][0])

    def relay(name, k):
        place, pair_first = names[name][1:]
        block = place(2 * z_from(k) + x)
        recv(block, ring_own[name][k])
        if k < nz - 1:
            send(block, block, z_next, ring_own[name][k + 1])
        if not pair_first:
            send(block, block, x_dev, over_x[name][k])

    def relay_other(name, k):
        block = names[name][1](2 * z_from(k) + (1 - x))
        recv(block, over_x[name][0] if k == 0 else ring_other[name][k])
        if k < nz - 1:
            send(block, block, z_next, ring_other[name][k + 1])

    def arrived(name):
        place, pair_first = names[name][1:]
        own_copy[name].wait()
        if not pair_first:
            for k in range(nz):
                recv(place(2 * z_from(k) + (1 - x)), over_x[name][k])

    def rows_of(yq, tq):
        return pl.ds(pl.multiple_of(yq * half_len + tq * quarter, quarter), quarter)

    own_rows = rows_of(y, t)

    tok_y, tok_c, cot_y, cot_c, seg_y = many(5)
    seg_local = local(seg, seg_row.at[:, tile(y, half_len)])
    send(seg, seg_row.at[:, tile(y, half_len)], y_dev, seg_y)
    tok_local = local(tok, xg.at[tile(y, half_len), :])
    cot_local = local(cot, cg.at[tile(y, half_len), :])

    far = rows_of(1 - y, t)
    far_other = rows_of(1 - y, 1 - t)

    def core_forward(ref, y_idx, c_idx):
        recv(ref.at[far, :], y_idx)
        return send(ref.at[far, :], ref.at[far, :], c_dev, c_idx)

    kinds = {"a": 0, "out": 1, "dh2": 2, "dh1": 3}
    ex_recv = {name: many(3) for name in kinds}
    ex_sent = []

    def exchange(name, compute, stage):
        e = kinds[name]
        if stage == 0:
            drain(ex_sent)
            ex_sent.clear()
            compute(far_other, part.at[0])
            ex_sent.append(send(part.at[0], from_core.at[e, 0], c_dev, ex_recv[name][0]))
        elif stage == 1:
            compute(far, part.at[1])
        elif stage == 2:
            recv(from_core.at[e, 0], ex_recv[name][0])

            def add(i):
                r = tile(i, 32)
                pair_sum[r, :] = (part[1, r, :].astype(F32) + from_core[e, 0, r, :].astype(F32)).astype(BF)

            loop(quarter // 32, add)
            ex_sent.append(send(pair_sum, from_y.at[e], y_dev, ex_recv[name][2]))
        elif stage == 3:
            compute(rows_of(y, 1 - t), part.at[2])
            ex_sent.append(send(part.at[2], from_core.at[e, 1], c_dev, ex_recv[name][1]))
        elif stage == 4:
            compute(own_rows, part.at[3])
        else:
            recv(from_core.at[e, 1], ex_recv[name][1])
            recv(from_y.at[e], ex_recv[name][2])

    def total_of(name, r):
        e = kinds[name]
        return part[3, r, :].astype(F32) + from_core[e, 1, r, :].astype(F32) + from_y[e, r, :].astype(F32)

    def spread_rows(ref, idx):
        return [
            send(ref.at[own_rows, :], ref.at[own_rows, :], c_dev, idx[0]),
            send(ref.at[own_rows, :], ref.at[own_rows, :], y_dev, idx[1]),
        ]

    h2_idx = many(3)
    ab_idx = many(3)

    grads = {
        "d0": (p_d0, r_d0, s_d0, f_d0, True),
        "d1": (p_d1, r_d1, s_d1, f_d1, False),
        "g": (p_g, r_g, s_g, f_g, False),
        "u": (p_u, r_u, s_u, f_u, False),
        "o": (p_o, r_o, s_o, f_o, True),
        "q": (p_q, r_q, s_q, f_q, False),
        "k": (p_k, r_k, s_k, f_k, False),
        "v": (p_v, r_v, s_v, f_v, False),
    }
    gx = {name: [None] + many(1 if item[4] else nz) for name, item in grads.items()}
    gz = {name: [[None] + many(nz - 1) for _ in range(2 if item[4] else 1)] for name, item in grads.items()}

    def add_rows(rows, cols, body):
        step = min(rows, 16 if cols > 512 else 128)
        loop(rows // step, lambda i: body(tile(i, step)))

    def grad_send(name, k):
        p, r, s, _, ring_first = grads[name]
        if ring_first:
            send(p.at[lax.rem(x + k, 2), z_from(1)], s.at[k - 1, 0], z_next, gz[name][k - 1][1])
        else:
            send(p.at[1 - x, z_from(k)], r.at[k - 1], x_dev, gx[name][k])

    def grad_step(name, k):
        p, r, s, f, ring_first = grads[name]
        if ring_first:
            c, k = divmod(k, 10)
            xq = lax.rem(x + 1 + c, 2)
            recv(s.at[c, k - 2], gz[name][c][k - 1])
            last_own = k == nz and c == 1
            if last_own:
                recv(r.at[0], gx[name][1])

            def add_ring(rr):
                total = p[xq, z_from(k), rr, :].astype(F32) + s[c, k - 2, rr, :].astype(F32)
                if last_own:
                    f[rr, :] = (total + r[0, rr, :].astype(F32)).astype(f.dtype)
                else:
                    p[xq, z_from(k), rr, :] = total.astype(p.dtype)

            add_rows(*p.shape[2:], add_ring)
            if k < nz:
                send(p.at[xq, z_from(k)], s.at[c, k - 1], z_next, gz[name][c][k])
            elif c == 0:
                send(p.at[xq, z_from(k)], r.at[0], x_dev, gx[name][1])
            return
        zq = z_from(k)
        recv(r.at[k - 1], gx[name][k])
        if k > 1:
            recv(s.at[0, k - 2], gz[name][0][k - 1])

        def add(rr):
            total = p[x, zq, rr, :].astype(F32) + r[k - 1, rr, :].astype(F32)
            if k > 1:
                total = total + s[0, k - 2, rr, :].astype(F32)
            if k < nz:
                p[x, zq, rr, :] = total.astype(p.dtype)
            else:
                f[rr, :] = total.astype(f.dtype)

        add_rows(*p.shape[2:], add)
        if k < nz:
            send(p.at[x, zq], s.at[0, k - 1], z_next, gz[name][0][k])

    part_h = hidden // 2

    def place_of(name, yq):
        h = pl.ds(pl.multiple_of(yq * heads_w, heads_w), heads_w)
        u = pl.ds(pl.multiple_of(yq * hidden, hidden), hidden)
        if name in ("d0", "d1"):
            return o_d.at[pl.ds(pl.multiple_of(yq * hidden + (name == "d1") * part_h, part_h), part_h), :]
        if name == "o":
            return o_o.at[h, :]
        wide = {"g": o_g, "u": o_u}
        return wide[name].at[:, u] if name in wide else {"q": o_q, "k": o_k, "v": o_v}[name].at[:, h]

    out_idx = dict(zip(grads, many(len(grads))))
    last_local = []

    def grad_end(name):
        f = grads[name][3]
        last_local.append(local(f, place_of(name, y)))
        send(f, place_of(name, y), y_dev, out_idx[name])

    def grad_done(name):
        recv(place_of(name, 1 - y), out_idx[name])

    value = {}
    blocks = half_len // BLOCK
    pairs = heads_w // (2 * HEAD_DIM)
    out_c, gtok_c = many(2)
    ng_idx = many(len(plane))
    n_c, n_y = many(2)
    my_rows = tile(t, quarter)
    other_rows = tile(1 - t, quarter)
    row_sends = []

    def send_tok():
        send(tok.at[tile(t, quarter), :], xg.at[own_rows, :], y_dev, tok_y)

    def send_cot():
        send(cot.at[tile(t, quarter), :], cg.at[own_rows, :], y_dev, cot_y)

    def gather_gains():
        value["one"] = jnp.concatenate([gain_all[i, 0:1, :] for i in range(2 * nz)], axis=1)
        value["two"] = jnp.concatenate([gain_all[i, 1:2, :] for i in range(2 * nz)], axis=1)

    def norm_rows(start):
        gain_one = value["one"]

        def body(i):
            r = pl.ds(pl.multiple_of(start + i * 32, 32), 32)
            values = xg[r, :].astype(F32)
            inverse = lax.rsqrt(jnp.mean(values * values, axis=-1, keepdims=True) + EPSILON)
            h1[r, :] = (values * inverse * gain_one).astype(BF)

        loop(half_len // 32, body)

    def norm_own():
        tok_local.wait()
        norm_rows(y * half_len)

    def norm_far():
        recv(xg.at[far_other, :], tok_c)
        norm_rows((1 - y) * half_len)

    def segments():
        seg_local.wait()
        recv(seg_row.at[:, tile(1 - y, half_len)], seg_y)
        seg_col[...] = jnp.broadcast_to(seg_row[0:1, :], (128, 2 * half_len)).T

    def project():
        def body(i):
            r = tile(i, 512)
            rows = h1[r, :]
            query[r, :] = (dot_nn(rows, wqkv[:, 0:heads_w]).astype(BF).astype(F32) * SCALE).astype(BF)
            keys[r, :] = dot_nn(rows, wqkv[:, heads_w : 2 * heads_w]).astype(BF)
            vals[r, :] = dot_nn(rows, wqkv[:, 2 * heads_w : 3 * heads_w]).astype(BF)

        loop(xg.shape[0] // 512, body)
        keys_t[...] = keys[...].T
        vals_t[...] = vals[...].T

    def either(half, body):
        @pl.when(half == 0)
        def _():
            body(half_len)

        @pl.when(half == 1)
        def _():
            body(2 * half_len)

    def attend(half):
        def block(i):
            args = (pairs, query, keys, vals_t, bias, seg_col, seg_row, mixed, mixed_t, log_sum)
            either(half, lambda length: attend_block(half * blocks + i, length, *args))

        loop(blocks, block)

    def out_rows(r, dst):
        dst[...] = dot_nn(mixed[r, :], wo[...]).astype(BF)

    def first_residual():
        exchange("a", None, 5)
        gain_two = value["two"]

        def body(i):
            r = tile(i, 32)
            rr = pl.ds(pl.multiple_of(y * half_len + t * quarter + i * 32, 32), 32)
            values = xg[rr, :].astype(F32) + total_of("a", r)
            y1[r, :] = values
            inverse = lax.rsqrt(jnp.mean(values * values, axis=-1, keepdims=True) + EPSILON)
            h2[rr, :] = (values * inverse * gain_two).astype(BF)

        loop(quarter // 32, body)
        row_sends.extend(spread_rows(h2, h2_idx))

    def gate(start):
        r = pl.ds(start, quarter)
        rows = h2[r, :]

        def cols(j):
            c = tile(j, 256)
            g = dot_nn(rows, wg[:, c])
            u = dot_nn(rows, wu[:, c])
            sg = 1.0 / (1.0 + jnp.exp(-g))
            gs = g * sg
            act_u[r, c] = gs.astype(BF)
            act_g[r, c] = (u * sg * (1.0 + g * (1.0 - sg))).astype(BF)
            act_m[r, c] = (gs * u).astype(BF)

        loop(hidden // 256, cols)

    def grad_cols(left, start, right, p, index):
        c = tile(index, 2 * db)
        for i in range(p.shape[2] // 256):
            r = slice(start + i * 256, start + (i + 1) * 256)
            both = dot_tn(left[:, r], right[:, c]).astype(BF)
            rows = slice(i * 256, (i + 1) * 256)
            p[0, index, rows, :] = both[:, 0:db]
            p[1, index, rows, :] = both[:, db : 2 * db]

    def grad_rows(left, right, p, index):
        c = tile(index, 2 * db)
        both = dot_tn(left[:, c], right[...]).astype(BF)
        p[0, index] = both[0:db, :]
        p[1, index] = both[db : 2 * db, :]

    def grad_down(part_of, p):
        loop(nz, lambda i: grad_cols(act_m, part_of * part_h, cg, p, i))

    def some_blocks(name, left, right, ks):
        p = grads[name][0]
        loop(len(ks), lambda i: grad_rows(left, right, p, z_from(ks[0] + i)))
        for k in ks:
            grad_send(name, k)

    def qkv_blocks(ks):
        def body(i):
            index = z_from(ks[0] + i)
            both = dot_tn(h1[:, tile(index, 2 * db)], grad_qkv[...]).astype(BF)
            for j, p in enumerate((p_q, p_k, p_v)):
                c = slice(j * heads_w, (j + 1) * heads_w)
                p[0, index] = both[0:db, c]
                p[1, index] = both[db : 2 * db, c]

        loop(len(ks), body)

    def hidden_back(r, dst):
        rows = cg[r, :]

        def cols(j):
            c = tile(j, 256)
            dm = dot_nt(rows, wd[c, :])
            act_g[r, c] = (dm * act_g[r, c].astype(F32)).astype(BF)
            act_u[r, c] = (dm * act_u[r, c].astype(F32)).astype(BF)

        loop(hidden // 256, cols)

        def back(j):
            c = tile(j, 512)
            dst[:, c] = (dot_nt(act_g[r, :], wg[c, :]) + dot_nt(act_u[r, :], wu[c, :])).astype(BF)

        loop(width // 512, back)

    def second_residual():
        exchange("dh2", None, 5)
        gain_two = value["two"]

        def body(i, carry):
            r = tile(i, 32)
            rr = pl.ds(pl.multiple_of(y * half_len + t * quarter + i * 32, 32), 32)
            values = y1[r, :]
            inverse = lax.rsqrt(jnp.mean(values * values, axis=-1, keepdims=True) + EPSILON)
            normed = values * inverse
            grad = total_of("dh2", r)
            scaled = grad * gain_two
            mean = jnp.mean(scaled * normed, axis=-1, keepdims=True)
            full = cg[rr, :].astype(F32) + inverse * (scaled - normed * mean)
            final_rows[r, :] = full
            ab[rr, :] = full.astype(BF)
            return carry + jnp.sum(grad * normed, axis=0, keepdims=True)

        value["grad_two"] = lax.fori_loop(0, quarter // 32, body, jnp.zeros((1, width), F32))
        row_sends.extend(spread_rows(ab, ab_idx))

    def down_rows(r, dst):
        def cols(j):
            c = tile(j, 512)
            dst[:, c] = dot_nn(act_m[r, :], wd[:, c]).astype(BF)

        loop(width // 512, cols)

    def mixed_back(half):
        r = tile(half, half_len)
        grad_mixed[r, :] = dot_nt(ab[r, :], wo[...]).astype(BF)

    def clear_sums():
        grad_k[...] = jnp.zeros_like(grad_k)
        grad_v[...] = jnp.zeros_like(grad_v)

    def attend_back(half):
        def block(i):
            args = (
                pairs, query, keys, keys_t, vals, grad_mixed, bias, seg_col, seg_row, log_sum, grad_qkv, mixed_t, grad_k, grad_v,
            )
            either(half, lambda length: attend_back_block(half * blocks + i, length, *args))

        loop(blocks, block)

    def own_back():
        recv(ab.at[rows_of(y, 1 - t), :], ab_idx[0])
        clear_sums()
        mixed_back(y)

    def far_back():
        recv(ab.at[far_other, :], ab_idx[2])
        mixed_back(1 - y)

    def grad_out_all():
        loop(nz, lambda i: grad_cols(mixed, 0, ab, p_o, i))
        grad_send("o", 1)
        grad_send("o", 2)

    def sums_to_bf16():
        grad_qkv[:, heads_w : 2 * heads_w] = grad_k[...].astype(BF)
        grad_qkv[:, 2 * heads_w : 3 * heads_w] = grad_v[...].astype(BF)

    def hidden_one_back(r, dst):
        def cols(j):
            c = tile(j, 512)
            dst[:, c] = dot_nt(grad_qkv[r, :], wqkv[c, :]).astype(BF)

        loop(width // 512, cols)

    def finish_out():
        exchange("out", None, 5)

        def body(i):
            r = tile(i, 32)
            act_m[r, 0:width] = (y1[r, :] + total_of("out", r)).astype(BF)

        loop(quarter // 32, body)
        last_local.append(local(act_m.at[0:quarter, 0:width], out.at[my_rows, :]))
        send(act_m.at[0:quarter, 0:width], out.at[my_rows, :], c_dev, out_c)

    def finish_tokens():
        exchange("dh1", None, 5)
        drain(row_sends)
        gain_one = value["one"]

        def body(i, carry):
            r = tile(i, 32)
            rr = pl.ds(pl.multiple_of(y * half_len + t * quarter + i * 32, 32), 32)
            values = xg[rr, :].astype(F32)
            inverse = lax.rsqrt(jnp.mean(values * values, axis=-1, keepdims=True) + EPSILON)
            normed = values * inverse
            grad = total_of("dh1", r)
            scaled = grad * gain_one
            mean = jnp.mean(scaled * normed, axis=-1, keepdims=True)
            full = final_rows[r, :] + inverse * (scaled - normed * mean)
            h2[r, :] = full.astype(BF)
            return carry + jnp.sum(grad * normed, axis=0, keepdims=True)

        gain_one_grad = lax.fori_loop(0, quarter // 32, body, jnp.zeros((1, width), F32))
        for i in range(2 * nz):
            c = slice(i * db, (i + 1) * db)
            p_n[i % 2, i // 2] = jnp.concatenate(
                [gain_one_grad[:, c], value["grad_two"][:, c], jnp.zeros((6, db), F32)], axis=0
            )
        for i, (k, c) in enumerate(plane):
            send(p_n.at[lax.rem(x + c, 2), lax.rem(z + k, nz)], s_n.at[i], plane_dev(k, c), ng_idx[i])
        last_local.append(local(h2.at[0:quarter, :], g_tok.at[my_rows, :]))
        send(h2.at[0:quarter, :], g_tok.at[my_rows, :], c_dev, gtok_c)

    def gains_core():
        total = p_n[x, z]
        for i in range(len(plane)):
            recv(s_n.at[i], ng_idx[i])
            total = total + s_n[i]
        f_n[...] = total
        send(f_n, c_n, c_dev, n_c)

    def gains_y():
        recv(c_n, n_c)
        y_n[0] = f_n[...] + c_n[...]
        send(y_n.at[0], y_n.at[1], y_dev, n_y)

    def gains_end():
        recv(y_n.at[1], n_y)
        o_gain[...] = y_n[0] + y_n[1]

    def finish():
        for name in grads:
            grad_done(name)
        recv(out.at[other_rows, :], out_c)
        recv(g_tok.at[other_rows, :], gtok_c)
        for copy in last_local:
            copy.wait()
        drain(list(sent))

    two = (1, 2), (3, 4)
    tasks = [
        send_tok,
        send_cot,
        gather_gains,
        lambda: core_forward(xg, tok_y, tok_c),
        lambda: core_forward(cg, cot_y, cot_c),
        lambda: (cot_local.wait(), recv(cg.at[far_other, :], cot_c)),
        segments,
        norm_own,
        norm_far,
        project,
        lambda: attend(1 - y),
        lambda: attend(y),
        first_residual,
        lambda: row_sends.append(core_forward(h2, h2_idx[1], h2_idx[2])),
        lambda: gate(y * half_len + t * quarter),
        lambda: (recv(h2.at[rows_of(y, 1 - t), :], h2_idx[0]), gate(y * half_len + (1 - t) * quarter)),
        lambda: gate((1 - y) * half_len + t * quarter),
        lambda: (recv(h2.at[far_other, :], h2_idx[2]), gate((1 - y) * half_len + (1 - t) * quarter)),
        lambda: grad_down(0, p_d0),
        lambda: grad_down(1, p_d1),
        second_residual,
        lambda: row_sends.append(core_forward(ab, ab_idx[1], ab_idx[2])),
        own_back,
        far_back,
        lambda: attend_back(y),
        lambda: attend_back(1 - y),
        grad_out_all,
        sums_to_bf16,
        finish_out,
        finish_tokens,
        gains_core,
        gains_y,
        gains_end,
        finish,
    ]
    tasks += [functools.partial(some_blocks, "g", h2, act_g, ks) for ks in two]
    tasks += [functools.partial(some_blocks, "u", h2, act_u, ks) for ks in two]
    tasks += [functools.partial(qkv_blocks, ks) for ks in two]
    for name, compute in zip(kinds, (out_rows, down_rows, hidden_back, hidden_one_back)):
        tasks += [functools.partial(exchange, name, compute, i) for i in range(5)]
    for name in names:
        tasks += [functools.partial(start_z, name), functools.partial(start_x, name), functools.partial(arrived, name)]
        tasks += [functools.partial(relay, name, k) for k in range(1, nz)]
        if names[name][2]:
            tasks += [functools.partial(relay_other, name, k) for k in range(nz)]
    for name in grads:
        tasks.append(functools.partial(grad_end, name))
        if grads[name][4]:
            tasks += [functools.partial(grad_step, name, 10 * c + k) for c in (0, 1) for k in range(2, nz + 1)]
        else:
            tasks += [functools.partial(grad_step, name, k) for k in range(1, nz + 1)]
    for name in ("d0", "d1", "q", "k", "v"):
        tasks += [functools.partial(grad_send, name, k) for k in ((1, 2) if grads[name][4] else range(1, nz + 1))]
    assert sorted(ORDER) == list(range(len(tasks)))
    for index in ORDER:
        tasks[index]()


def fused(nz, tokens, segment_ids, w_query, w_key, w_value, w_out, w_gate, w_up, w_down, gain_attn, gain_ffn, cotangent):
    half_len, _, width = tokens.shape
    length = 2 * half_len
    quarter = half_len // 2
    heads_w = w_query.shape[1] // 2
    hidden = w_gate.shape[1] // 2
    db = w_query.shape[0]
    heads = heads_w // HEAD_DIM
    gains = jnp.stack([gain_attn, gain_ffn]).astype(F32)

    def vm(*shape, dtype=BF):
        return pltpu.VMEM(shape, dtype)

    shape_d, shape_g, shape_o, shape_q = (hidden // 2, db), (db, hidden), (heads_w, db), (db, heads_w)
    shapes = (shape_d, shape_d, shape_g, shape_g, shape_o, shape_q, shape_q, shape_q)
    ring_first = (True, False, False, False, True, False, False, False)
    scratch = [
        vm(length, width), vm(length, width), vm(1, length, dtype=I32), vm(2 * nz, 2, db, dtype=F32),
        vm(width, 3 * heads_w), vm(heads_w, width), vm(width, hidden), vm(width, hidden), vm(hidden, width),
        vm(length, width), vm(length, width), vm(length, width),
        vm(length, heads_w), vm(length, heads_w), vm(length, heads_w), vm(heads_w, length), vm(heads_w, length),
        vm(length, heads_w), vm(length, heads_w), vm(length, 3 * heads_w),
        vm(length, heads_w, dtype=F32), vm(length, heads_w, dtype=F32),
        vm(length, hidden), vm(length, hidden), vm(length, hidden),
        vm(quarter, width, dtype=F32), vm(length, BLOCK, dtype=F32), vm(heads_w, BLOCK, dtype=F32),
        vm(heads, 8, length, dtype=F32), vm(length, 128, dtype=I32),
        vm(4, quarter, width), vm(quarter, width), vm(4, 2, quarter, width), vm(4, quarter, width),
        vm(quarter, width, dtype=F32),
    ]
    scratch += [vm(2, nz, *shape) for shape in shapes]
    scratch += [vm(1 if first else nz, *shape) for shape, first in zip(shapes, ring_first)]
    scratch += [vm(2 if first else 1, nz - 1, *shape) for shape, first in zip(shapes, ring_first)]
    scratch += [vm(*shape) for shape in shapes]
    scratch += [
        vm(2, nz, 8, db, dtype=F32), vm(2 * nz - 1, 8, db, dtype=F32), vm(8, db, dtype=F32),
        vm(8, db, dtype=F32), vm(2, 8, db, dtype=F32),
    ]
    scratch += [pltpu.SemaphoreType.DMA((SEMS[0],)), pltpu.SemaphoreType.DMA((SEMS[1],)), pltpu.SemaphoreType.DMA((SEMS[2],))]
    anywhere = pl.BlockSpec(memory_space=pl.ANY)
    weights = (w_query, w_key, w_value, w_out, w_gate, w_up, w_down)
    results = pl.pallas_call(
        functools.partial(layer_kernel, nz),
        out_shape=[jax.ShapeDtypeStruct((half_len, width), BF)] * 2
        + [jax.ShapeDtypeStruct(item.shape, BF) for item in weights]
        + [jax.ShapeDtypeStruct((8, db), F32)],
        in_specs=[anywhere] * 11,
        out_specs=[anywhere] * 9 + [pl.BlockSpec(memory_space=pltpu.VMEM)],
        scratch_shapes=scratch,
        compiler_params=pltpu.CompilerParams(
            collective_id=0, has_side_effects=True, vmem_limit_bytes=VMEM_BYTES
        ),
        name="layer",
    )(tokens.reshape(half_len, width), cotangent.reshape(half_len, width), segment_ids, gains, *weights)
    bodies = results[:9]
    wide = [jax.ShapeDtypeStruct(item.shape, BF if i < 2 else F32) for i, item in enumerate(bodies)]

    def widen(*refs):
        srcs, rows, dsts, (one, two), held = refs[:9], refs[9], refs[10:19], refs[19:21], refs[21:30]
        finals, (load_sems, store_sems) = refs[30:37], refs[37:]
        order = [*range(6, 9), *range(2, 6), 0, 1]
        loads = {i: pltpu.make_async_copy(srcs[i], held[i], load_sems.at[i]) for i in order}
        for i in order:
            loads[i].start()
        one[...] = rows[0:1, :]
        two[...] = rows[1:2, :]
        stores = []
        for i in order:
            loads[i].wait()
            if i >= 2:
                finals[i - 2][...] = held[i][...].astype(F32)
            stores.append(pltpu.make_async_copy(finals[i - 2] if i >= 2 else held[i], dsts[i], store_sems.at[i]))
            stores[-1].start()
        for copy in stores:
            copy.wait()

    inside = pl.BlockSpec(memory_space=pltpu.VMEM)
    finals = pl.pallas_call(
        widen,
        out_shape=wide + [jax.ShapeDtypeStruct((1, db), F32)] * 2,
        in_specs=[anywhere] * 9 + [inside],
        out_specs=[anywhere] * 9 + [inside] * 2,
        scratch_shapes=[vm(*item.shape) for item in bodies]
        + [vm(*item.shape, dtype=F32) for item in wide[2:]]
        + [pltpu.SemaphoreType.DMA((9,)), pltpu.SemaphoreType.DMA((9,))],
        compiler_params=pltpu.CompilerParams(vmem_limit_bytes=VMEM_BYTES),
        name="widen",
    )(*results)
    shape = tokens.shape
    return (finals[0].reshape(shape), finals[1].reshape(shape), *finals[2:9], finals[9].reshape(db), finals[10].reshape(db))


def fits(mesh, tokens_shape):
    return mesh.shape["fsdp"] == 8 and mesh.shape["ctx"] == 2 and mesh.shape["tp"] == 2 and tokens_shape[1:] == (1, 1024)


def solution(mesh):
    def step(tokens, *rest):
        if fits(mesh, tokens.shape):
            return fused(mesh.shape["fsdp"] // 2, tokens, *rest)
        return local(tokens, *rest)

    return jax.shard_map(
        step,
        mesh=mesh,
        in_specs=(
            P("ctx", "fsdp", None),
            P("fsdp", "ctx"),
            P("fsdp", "tp"),
            P("fsdp", "tp"),
            P("fsdp", "tp"),
            P("tp", "fsdp"),
            P("fsdp", "tp"),
            P("fsdp", "tp"),
            P("tp", "fsdp"),
            P("fsdp"),
            P("fsdp"),
            P("ctx", "fsdp", None),
        ),
        out_specs=(
            P("ctx", "fsdp", None),
            P("ctx", "fsdp", None),
            P("fsdp", "tp"),
            P("fsdp", "tp"),
            P("fsdp", "tp"),
            P("tp", "fsdp"),
            P("fsdp", "tp"),
            P("fsdp", "tp"),
            P("tp", "fsdp"),
            P("fsdp"),
            P("fsdp"),
        ),
        check_vma=False,
    )
```

```python
import functools

import jax
import jax.numpy as jnp
from jax import lax
from jax.experimental import pallas as pl
from jax.experimental.pallas import tpu as pltpu
from jax.sharding import PartitionSpec as P

HEAD_DIM = 64


EPSILON = 1e-05
SCALE = 0.125
MASKED = -1e30


def normalize(values):
    inverse = lax.rsqrt(jnp.mean(values * values, axis=-1, keepdims=True) + EPSILON)
    return (values * inverse, inverse)


def norm_back(grad_normed, normed, inverse):
    return inverse * (grad_normed - normed * jnp.mean(grad_normed * normed, axis=-1, keepdims=True))


def inner_rows(left, right):
    return lax.dot_general(
        left, right, (((0,), (0,)), ((), ())), preferred_element_type=jnp.float32
    )


def times_transposed(left, weight):
    return lax.dot_general(
        left, weight, (((1,), (1,)), ((), ())), preferred_element_type=jnp.float32
    )


def head_sum(partial_sum):
    return lax.psum(partial_sum, "tp")


def split_heads(values, head_size):
    length, sequences, width = values.shape
    return jnp.moveaxis(values.reshape(length, sequences, width // head_size, head_size), 2, 0)


def join_heads(values):
    heads, length, sequences, head_size = values.shape
    return jnp.moveaxis(values, 0, 2).reshape(length, sequences, heads * head_size)


def make_mask(query_pos, query_seg, key_pos, key_seg):
    before = key_pos[None, None, :] <= query_pos[None, :, None]
    same = query_seg.T[:, :, None] == key_seg.T[:, None, :]
    return before & same


def key_head_grads(parts, use_mask):
    q_head, k_head, v_head, d_head, log_total, delta = parts
    scores = jnp.einsum("qsd,ksd->sqk", q_head, k_head, preferred_element_type=jnp.float32) * SCALE
    probs = jnp.exp(jnp.where(use_mask, scores, MASKED) - log_total)
    grad_probs = jnp.einsum("qsd,ksd->sqk", d_head, v_head, preferred_element_type=jnp.float32)
    grad_scores = (probs * (grad_probs - delta)).astype(jnp.bfloat16)
    grad_v = jnp.einsum(
        "sqk,qsd->ksd", probs.astype(jnp.bfloat16), d_head, preferred_element_type=jnp.float32
    )
    grad_k = (
        jnp.einsum("sqk,qsd->ksd", grad_scores, q_head, preferred_element_type=jnp.float32) * SCALE
    )
    return (grad_k, grad_v)


def local(
    tokens,
    segment_ids,
    w_query,
    w_key,
    w_value,
    w_out,
    w_gate,
    w_up,
    w_down,
    gain_attn,
    gain_ffn,
    cotangent,
):
    local_len, sequences, width = tokens.shape
    rows = local_len * sequences
    (
        full_query,
        full_key,
        full_value,
        full_out,
        full_gate,
        full_up,
        full_down,
        full_gain_one,
        full_gain_two,
    ) = (
        lax.all_gather(w_query, "fsdp", axis=0, tiled=True),
        lax.all_gather(w_key, "fsdp", axis=0, tiled=True),
        lax.all_gather(w_value, "fsdp", axis=0, tiled=True),
        lax.all_gather(w_out, "fsdp", axis=1, tiled=True),
        lax.all_gather(w_gate, "fsdp", axis=0, tiled=True),
        lax.all_gather(w_up, "fsdp", axis=0, tiled=True),
        lax.all_gather(w_down, "fsdp", axis=1, tiled=True),
        lax.all_gather(gain_attn, "fsdp", axis=0, tiled=True),
        lax.all_gather(gain_ffn, "fsdp", axis=0, tiled=True),
    )
    gain_one = full_gain_one.astype(jnp.float32)
    gain_two = full_gain_two.astype(jnp.float32)
    head_width = full_query.shape[1]
    flat = tokens.astype(jnp.float32).reshape(rows, width)
    normed_one, inverse_one = normalize(flat)
    hidden_one = (normed_one * gain_one).astype(jnp.bfloat16)
    query = (
        jnp.dot(hidden_one, full_query, preferred_element_type=jnp.float32)
        .astype(jnp.bfloat16)
        .reshape(local_len, sequences, head_width)
    )
    keys = (
        jnp.dot(hidden_one, full_key, preferred_element_type=jnp.float32)
        .astype(jnp.bfloat16)
        .reshape(local_len, sequences, head_width)
    )
    vals = (
        jnp.dot(hidden_one, full_value, preferred_element_type=jnp.float32)
        .astype(jnp.bfloat16)
        .reshape(local_len, sequences, head_width)
    )
    pair = jnp.concatenate([keys, vals], axis=-1)
    seg_local = segment_ids.T
    pair_all, seg_all = (
        lax.all_gather(pair, "ctx", axis=0, tiled=True),
        lax.all_gather(seg_local, "ctx", axis=0, tiled=True),
    )
    length = pair_all.shape[0]
    query_pos = lax.axis_index("ctx") * local_len + jnp.arange(local_len, dtype=jnp.int32)
    all_pos = jnp.arange(length, dtype=jnp.int32)
    mask = make_mask(query_pos, seg_local, all_pos, seg_all)
    q_heads = split_heads(query, HEAD_DIM)
    k_heads = split_heads(pair_all[..., :head_width], HEAD_DIM)
    v_heads = split_heads(pair_all[..., head_width:], HEAD_DIM)

    def attend(parts):
        q_head, k_head, v_head = parts
        scores = (
            jnp.einsum("qsd,ksd->sqk", q_head, k_head, preferred_element_type=jnp.float32) * SCALE
        )
        scores = jnp.where(mask, scores, MASKED)
        row_max = jnp.max(scores, axis=-1, keepdims=True)
        log_total = row_max + jnp.log(jnp.sum(jnp.exp(scores - row_max), axis=-1, keepdims=True))
        probs = jnp.exp(scores - log_total).astype(jnp.bfloat16)
        return (
            jnp.einsum("sqk,ksd->qsd", probs, v_head, preferred_element_type=jnp.float32),
            log_total,
        )

    attended, log_totals = lax.map(attend, (q_heads, k_heads, v_heads))
    mixed = join_heads(attended).astype(jnp.bfloat16).reshape(rows, head_width)
    resid = flat + head_sum(jnp.dot(mixed, full_out, preferred_element_type=jnp.float32))
    normed_two, inverse_two = normalize(resid)
    hidden_two = (normed_two * gain_two).astype(jnp.bfloat16)
    gate = jnp.dot(hidden_two, full_gate, preferred_element_type=jnp.float32)
    upward = jnp.dot(hidden_two, full_up, preferred_element_type=jnp.float32)
    sigmoid_gate = jax.nn.sigmoid(gate)
    swish_up = (gate * sigmoid_gate * upward).astype(jnp.bfloat16)
    result = resid + head_sum(jnp.dot(swish_up, full_down, preferred_element_type=jnp.float32))
    output = result.astype(jnp.bfloat16).reshape(local_len, sequences, width)
    (
        full_query,
        full_key,
        full_value,
        full_out,
        full_gate,
        full_up,
        full_down,
        full_gain_one,
        full_gain_two,
    ) = (
        lax.all_gather(w_query, "fsdp", axis=0, tiled=True),
        lax.all_gather(w_key, "fsdp", axis=0, tiled=True),
        lax.all_gather(w_value, "fsdp", axis=0, tiled=True),
        lax.all_gather(w_out, "fsdp", axis=1, tiled=True),
        lax.all_gather(w_gate, "fsdp", axis=0, tiled=True),
        lax.all_gather(w_up, "fsdp", axis=0, tiled=True),
        lax.all_gather(w_down, "fsdp", axis=1, tiled=True),
        lax.all_gather(gain_attn, "fsdp", axis=0, tiled=True),
        lax.all_gather(gain_ffn, "fsdp", axis=0, tiled=True),
    )
    gain_one = full_gain_one.astype(jnp.float32)
    gain_two = full_gain_two.astype(jnp.float32)
    grad_result = cotangent.astype(jnp.float32).reshape(rows, width)
    grad_low = grad_result.astype(jnp.bfloat16)
    grad_wdown = inner_rows(swish_up, grad_low)
    grad_swish = times_transposed(grad_low, full_down)
    grad_gate_act = (
        grad_swish * upward * sigmoid_gate * (1.0 + gate * (1.0 - sigmoid_gate))
    ).astype(jnp.bfloat16)
    grad_upward = (grad_swish * gate * sigmoid_gate).astype(jnp.bfloat16)
    grad_wgate = inner_rows(hidden_two, grad_gate_act)
    grad_wup = inner_rows(hidden_two, grad_upward)
    grad_hidden_two = head_sum(
        times_transposed(grad_gate_act, full_gate) + times_transposed(grad_upward, full_up)
    )
    grad_gain_two = jnp.sum(grad_hidden_two * normed_two, axis=0)
    grad_resid = grad_result + norm_back(grad_hidden_two * gain_two, normed_two, inverse_two)
    grad_branch = grad_resid.astype(jnp.bfloat16)
    grad_wout = inner_rows(mixed, grad_branch)
    grad_mixed = (
        times_transposed(grad_branch, full_out)
        .astype(jnp.bfloat16)
        .reshape(local_len, sequences, head_width)
    )
    d_heads = split_heads(grad_mixed, HEAD_DIM)

    def query_side(parts):
        q_head, k_head, v_head, d_head, log_total = parts
        scores = (
            jnp.einsum("qsd,ksd->sqk", q_head, k_head, preferred_element_type=jnp.float32) * SCALE
        )
        probs = jnp.exp(jnp.where(mask, scores, MASKED) - log_total)
        grad_probs = jnp.einsum("qsd,ksd->sqk", d_head, v_head, preferred_element_type=jnp.float32)
        delta = jnp.sum(probs * grad_probs, axis=-1, keepdims=True)
        grad_scores = (probs * (grad_probs - delta)).astype(jnp.bfloat16)
        return (
            jnp.einsum("sqk,ksd->qsd", grad_scores, k_head, preferred_element_type=jnp.float32)
            * SCALE,
            delta,
        )

    grad_q_heads, deltas = lax.map(query_side, (q_heads, k_heads, v_heads, d_heads, log_totals))
    grad_query = join_heads(grad_q_heads).astype(jnp.bfloat16).reshape(rows, head_width)
    piece_mask = make_mask(
        query_pos, seg_local, jnp.arange(local_len * lax.axis_size("ctx"), dtype=jnp.int32), seg_all
    )
    k_piece = split_heads(pair_all[..., :head_width], HEAD_DIM)
    v_piece = split_heads(pair_all[..., head_width:], HEAD_DIM)

    def per_head(parts):
        return key_head_grads(parts, piece_mask)

    grad_k_heads, grad_v_heads = lax.map(
        per_head, (q_heads, k_piece, v_piece, d_heads, log_totals, deltas)
    )
    grad_pair = lax.psum_scatter(
        jnp.concatenate([join_heads(grad_k_heads), join_heads(grad_v_heads)], axis=-1).astype(
            jnp.bfloat16
        ),
        "ctx",
        scatter_dimension=0,
        tiled=True,
    ).astype(jnp.float32)
    grad_keys = grad_pair[..., :head_width].astype(jnp.bfloat16).reshape(rows, head_width)
    grad_vals = grad_pair[..., head_width:].astype(jnp.bfloat16).reshape(rows, head_width)
    grad_wquery = inner_rows(hidden_one, grad_query)
    grad_wkey = inner_rows(hidden_one, grad_keys)
    grad_wvalue = inner_rows(hidden_one, grad_vals)
    grad_hidden_one = head_sum(
        times_transposed(grad_query, full_query)
        + times_transposed(grad_keys, full_key)
        + times_transposed(grad_vals, full_value)
    )
    grad_gain_one = jnp.sum(grad_hidden_one * normed_one, axis=0)
    grad_input = grad_resid + norm_back(grad_hidden_one * gain_one, normed_one, inverse_one)
    grad_input = grad_input.astype(jnp.bfloat16).reshape(local_len, sequences, width)
    shares = (
        lax.psum_scatter(
            grad_wquery.astype(jnp.bfloat16), "fsdp", scatter_dimension=0, tiled=True
        ).astype(jnp.float32),
        lax.psum_scatter(
            grad_wkey.astype(jnp.bfloat16), "fsdp", scatter_dimension=0, tiled=True
        ).astype(jnp.float32),
        lax.psum_scatter(
            grad_wvalue.astype(jnp.bfloat16), "fsdp", scatter_dimension=0, tiled=True
        ).astype(jnp.float32),
        lax.psum_scatter(
            grad_wout.astype(jnp.bfloat16), "fsdp", scatter_dimension=1, tiled=True
        ).astype(jnp.float32),
        lax.psum_scatter(
            grad_wgate.astype(jnp.bfloat16), "fsdp", scatter_dimension=0, tiled=True
        ).astype(jnp.float32),
        lax.psum_scatter(
            grad_wup.astype(jnp.bfloat16), "fsdp", scatter_dimension=0, tiled=True
        ).astype(jnp.float32),
        lax.psum_scatter(
            grad_wdown.astype(jnp.bfloat16), "fsdp", scatter_dimension=1, tiled=True
        ).astype(jnp.float32),
        lax.psum_scatter(
            grad_gain_one.astype(jnp.bfloat16), "fsdp", scatter_dimension=0, tiled=True
        ).astype(jnp.float32),
        lax.psum_scatter(
            grad_gain_two.astype(jnp.bfloat16), "fsdp", scatter_dimension=0, tiled=True
        ).astype(jnp.float32),
    )
    shares = (
        lax.psum(shares[0].astype(jnp.bfloat16), "ctx").astype(jnp.float32),
        lax.psum(shares[1].astype(jnp.bfloat16), "ctx").astype(jnp.float32),
        lax.psum(shares[2].astype(jnp.bfloat16), "ctx").astype(jnp.float32),
        lax.psum(shares[3].astype(jnp.bfloat16), "ctx").astype(jnp.float32),
        lax.psum(shares[4].astype(jnp.bfloat16), "ctx").astype(jnp.float32),
        lax.psum(shares[5].astype(jnp.bfloat16), "ctx").astype(jnp.float32),
        lax.psum(shares[6].astype(jnp.bfloat16), "ctx").astype(jnp.float32),
        lax.psum(shares[7].astype(jnp.bfloat16), "ctx").astype(jnp.float32),
        lax.psum(shares[8].astype(jnp.bfloat16), "ctx").astype(jnp.float32),
    )
    return (
        output,
        grad_input,
        shares[0],
        shares[1],
        shares[2],
        shares[3],
        shares[4],
        shares[5],
        shares[6],
        shares[7],
        shares[8],
    )


BF = jnp.bfloat16
F32 = jnp.float32
I32 = jnp.int32
MESH = pl.DeviceIdType.MESH
BLOCK = 256
VMEM_BYTES = 67043328
ORDER = (
    103, 96, 113, 78, 0, 84, 91, 90, 102, 79, 81, 99, 87, 93, 85, 108, 82, 100, 88, 94, 83, 6, 105, 97,
    112, 3, 89, 109, 80, 101, 2, 1, 95, 8, 125, 124, 7, 118, 119, 115, 143, 86, 106, 92, 98, 9, 110, 51,
    121, 127, 104, 50, 111, 107, 58, 116, 131, 59, 60, 122, 130, 52, 128, 136, 142, 53, 117, 148, 61, 133, 4, 62,
    123, 129, 10, 5, 139, 114, 149, 12, 120, 28, 29, 137, 134, 126, 37, 140, 36, 11, 145, 30, 38, 135, 144, 150,
    13, 31, 39, 141, 42, 40, 146, 14, 208, 151, 209, 132, 138, 34, 35, 147, 68, 175, 41, 69, 70, 153, 165, 43,
    32, 33, 176, 156, 71, 15, 166, 210, 72, 44, 177, 16, 157, 63, 64, 46, 211, 18, 45, 170, 167, 55, 47, 65,
    171, 66, 178, 180, 67, 160, 154, 174, 213, 17, 54, 168, 19, 56, 181, 57, 22, 21, 161, 212, 164, 73, 172, 20,
    74, 75, 182, 48, 218, 222, 223, 185, 214, 173, 162, 219, 49, 169, 76, 215, 186, 200, 155, 183, 179, 195, 77, 187,
    190, 23, 201, 196, 224, 163, 220, 216, 188, 225, 184, 204, 191, 159, 202, 158, 205, 152, 197, 221, 217, 192, 203, 199,
    206, 198, 194, 207, 24, 193, 189, 25, 26, 27,
)
SEMS = (48, 191, 26)


def dot_nn(left, right):
    return jnp.dot(left, right, preferred_element_type=F32)


def dot_nt(left, right):
    return lax.dot_general(left, right, (((1,), (1,)), ((), ())), preferred_element_type=F32)


def dot_tn(left, right):
    return lax.dot_general(left, right, (((0,), (0,)), ((), ())), preferred_element_type=F32)


def loop(count, body):
    def step(index, carry):
        body(index)
        return carry

    lax.fori_loop(0, count, step, 0)


def tile(index, size):
    return pl.ds(pl.multiple_of(index * size, size), size)


def only_half(values, half):
    lane = lax.broadcasted_iota(I32, values.shape, 1)
    keep = (lane < HEAD_DIM) if half == 0 else (lane >= HEAD_DIM)
    return jnp.where(keep, values, jnp.zeros_like(values))


def write_bias(bias, seg_col, seg_row, block, length):
    lanes = tile(block, BLOCK)
    keys = seg_col[0:length, :]
    key_pos = lax.broadcasted_iota(I32, (length, BLOCK), 0)
    query_pos = lax.broadcasted_iota(I32, (length, BLOCK), 1) + block * BLOCK
    same = jnp.concatenate([keys, keys], axis=1) == seg_row[0:1, lanes]
    bias[0:length, :] = jnp.where(same & (key_pos <= query_pos), 0.0, MASKED)


def attend_block(block, length, pairs, query, keys, vals_t, bias, seg_col, seg_row, mixed, mixed_t, log_sum):
    write_bias(bias, seg_col, seg_row, block, length)
    rows = tile(block, BLOCK)

    def pair(index):
        cols = tile(index, 2 * HEAD_DIM)
        two = query[rows, cols]
        for half in (0, 1):
            scores = dot_nt(keys[0:length, cols], only_half(two, half)) + bias[0:length, :]
            top = jnp.max(scores, axis=0, keepdims=True)
            expo = jnp.exp(scores - top)
            total = jnp.sum(expo, axis=0, keepdims=True)
            log_sum[2 * index + half, :, rows] = jnp.broadcast_to(top + jnp.log(total), (8, BLOCK))
            probs = (expo * (1.0 / total)).astype(BF)
            head = tile(2 * index + half, HEAD_DIM)
            mixed_t[head, :] = dot_nn(vals_t[head, 0:length], probs)

    loop(pairs, pair)
    mixed[rows, :] = mixed_t[...].T.astype(BF)


def attend_back_block(
    block, length, pairs, query, keys, keys_t, vals, grad_mixed, bias, seg_col, seg_row, log_sum, grad_qkv, grad_q_t, grad_k, grad_v
):
    write_bias(bias, seg_col, seg_row, block, length)
    rows = tile(block, BLOCK)

    def pair(index):
        cols = tile(index, 2 * HEAD_DIM)
        two = query[rows, cols]
        grad_two = grad_mixed[rows, cols]
        for half in (0, 1):
            one = only_half(two, half)
            grad_one = only_half(grad_two, half)
            scores = dot_nt(keys[0:length, cols], one) + bias[0:length, :]
            probs = jnp.exp(scores - log_sum[2 * index + half, 0:1, rows])
            grad_probs = dot_nt(vals[0:length, cols], grad_one)
            delta = jnp.sum(probs * grad_probs, axis=0, keepdims=True)
            grad_scores = (probs * (grad_probs - delta)).astype(BF)
            grad_v[0:length, cols] += dot_nn(probs.astype(BF), grad_one)
            grad_k[0:length, cols] += dot_nn(grad_scores, one)
            head = tile(2 * index + half, HEAD_DIM)
            grad_q_t[head, :] = dot_nn(keys_t[head, 0:length], grad_scores)

    loop(pairs, pair)
    grad_qkv[rows, 0 : grad_q_t.shape[0]] = (grad_q_t[...].T * SCALE).astype(BF)


def layer_kernel(
    nz,
    tok, cot, seg, gains, w_q, w_k, w_v, w_o, w_g, w_u, w_d,
    out, g_tok, o_q, o_k, o_v, o_o, o_g, o_u, o_d, o_gain,
    xg, cg, seg_row, gain_all, wqkv, wo, wg, wu, wd,
    h1, h2, ab, query, keys, vals, keys_t, vals_t, mixed, grad_mixed, grad_qkv, grad_k, grad_v,
    act_g, act_u, act_m, y1, bias, mixed_t, log_sum, seg_col,
    part, pair_sum, from_core, from_y, final_rows,
    p_d0, p_d1, p_g0, p_g1, p_u0, p_u1, p_o, p_q, p_k, p_v, r_d0, r_d1, r_g0, r_g1, r_u0, r_u1, r_o, r_q, r_k, r_v,
    s_d0, s_d1, s_g0, s_g1, s_u0, s_u1, s_o, s_q, s_k, s_v, f_d0, f_d1, f_g0, f_g1, f_u0, f_u1, f_o, f_q, f_k, f_v,
    p_n, r_n, s_n, f_n, c_n, y_n,
    send_sems, recv_sems, local_sems,
):
    fs = lax.axis_index("fsdp")
    y = lax.axis_index("ctx")
    t = lax.axis_index("tp")
    z = fs // 2
    x = lax.rem(fs, 2)
    width = xg.shape[1]
    half_len = xg.shape[0] // 2
    quarter = half_len // 2
    heads_w = query.shape[1]
    hidden = act_m.shape[1]
    db = width // (2 * nz)

    def dev(fq, yq, tq):
        return {"fsdp": fq, "ctx": yq, "tp": tq}

    x_dev = dev(2 * z + (1 - x), y, t)
    y_dev = dev(fs, 1 - y, t)
    c_dev = dev(fs, y, 1 - t)

    def z_from(k):
        return lax.rem(z + nz - k, nz)

    z_next = dev(2 * lax.rem(z + 1, nz) + x, y, t)

    barrier = pltpu.get_barrier_semaphore()
    z_prev = dev(2 * z_from(1) + x, y, t)
    for peer in (x_dev, y_dev, c_dev, z_next, z_prev):
        pl.semaphore_signal(barrier, inc=1, device_id=peer, device_id_type=MESH)
    pl.semaphore_wait(barrier, 5)

    count = {"send": 0, "recv": 0, "local": 0}
    sent = []

    def new(kind):
        count[kind] += 1
        return count[kind] - 1

    slots = [None] * SEMS[0]

    def send(src, dst, device, ridx):
        slot = new("send") % SEMS[0]
        if slots[slot] is not None:
            drain([copy for copy in sent if copy is slots[slot]])
        copy = pltpu.make_async_remote_copy(
            src, dst, send_sems.at[slot], recv_sems.at[ridx], device_id=device, device_id_type=MESH
        )
        slots[slot] = copy
        copy.start()
        sent.append(copy)
        return copy

    def recv(dst, ridx):
        pltpu.make_async_remote_copy(
            dst, dst, send_sems.at[0], recv_sems.at[ridx], device_id=y_dev, device_id_type=MESH
        ).wait_recv()

    def local(src, dst):
        copy = pltpu.make_async_copy(src, dst, local_sems.at[new("local")])
        copy.start()
        return copy

    def many(number):
        return [new("recv") for _ in range(number)]

    def drain(copies):
        left = [copy for copy in sent if any(copy is other for other in copies)]
        for copy in left:
            copy.wait_send()
        sent[:] = [copy for copy in sent if not any(copy is other for other in left)]

    hw = pl.ds(pl.multiple_of(y * heads_w, heads_w), heads_w)

    def rb(fq):
        return tile(fq, db)

    part_h = hidden // 2
    first, second = slice(0, part_h), slice(part_h, hidden)

    def half_of(half, yq):
        return pl.ds(pl.multiple_of(yq * hidden + half * part_h, part_h), part_h)

    names = {
        "n": (gains, lambda fq: gain_all.at[fq], False),
        "q": (w_q.at[:, hw], lambda fq: wqkv.at[rb(fq), 0:heads_w], False),
        "k": (w_k.at[:, hw], lambda fq: wqkv.at[rb(fq), heads_w : 2 * heads_w], False),
        "v": (w_v.at[:, hw], lambda fq: wqkv.at[rb(fq), 2 * heads_w : 3 * heads_w], False),
        "o": (w_o.at[hw, :], lambda fq: wo.at[:, rb(fq)], True),
    }
    for i, units in enumerate((first, second)):
        mine = half_of(i, y)
        names[f"g{i}"] = (w_g.at[:, mine], lambda fq, units=units: wg.at[rb(fq), units], False)
        names[f"u{i}"] = (w_u.at[:, mine], lambda fq, units=units: wu.at[rb(fq), units], False)
        names[f"d{i}"] = (w_d.at[mine, :], lambda fq, units=units: wd.at[units, rb(fq)], i == 1)
    ring_own = {name: [None] + many(nz - 1) for name in names}
    ring_other = {name: [None] + many(nz - 1) for name in names if names[name][2]}
    over_x = {name: many(1 if names[name][2] else nz) for name in names}
    own_copy = {}

    def start_z(name):
        src, place, _ = names[name]
        own_copy[name] = local(src, place(fs))
        send(src, place(fs), z_next, ring_own[name][1])

    def start_x(name):
        src, place, _ = names[name]
        send(src, place(fs), x_dev, over_x[name][0])

    def relay(name, k):
        place, pair_first = names[name][1:]
        block = place(2 * z_from(k) + x)
        recv(block, ring_own[name][k])
        if k < nz - 1:
            send(block, block, z_next, ring_own[name][k + 1])
        if not pair_first:
            send(block, block, x_dev, over_x[name][k])

    def relay_other(name, k):
        block = names[name][1](2 * z_from(k) + (1 - x))
        recv(block, over_x[name][0] if k == 0 else ring_other[name][k])
        if k < nz - 1:
            send(block, block, z_next, ring_other[name][k + 1])

    def arrived(name):
        place, pair_first = names[name][1:]
        own_copy[name].wait()
        if not pair_first:
            for k in range(nz):
                recv(place(2 * z_from(k) + (1 - x)), over_x[name][k])

    def rows_of(yq, tq):
        return pl.ds(pl.multiple_of(yq * half_len + tq * quarter, quarter), quarter)

    own_rows = rows_of(y, t)

    tok_y, tok_c, cot_y, cot_c, seg_y = many(5)
    seg_local = local(seg, seg_row.at[:, tile(y, half_len)])
    send(seg, seg_row.at[:, tile(y, half_len)], y_dev, seg_y)
    tok_local = local(tok, xg.at[tile(y, half_len), :])
    cot_local = local(cot, cg.at[tile(y, half_len), :])

    far = rows_of(1 - y, t)
    far_other = rows_of(1 - y, 1 - t)

    def core_forward(ref, y_idx, c_idx):
        recv(ref.at[far, :], y_idx)
        return send(ref.at[far, :], ref.at[far, :], c_dev, c_idx)

    kinds = {"a": 0, "out": 1, "dh2": 2, "dh1": 3}
    ex_recv = {name: many(3) for name in kinds}
    ex_sent = []

    def exchange(name, compute, stage):
        e = kinds[name]
        if stage == 0:
            drain(ex_sent)
            ex_sent.clear()
            compute(far_other, part.at[0])
            ex_sent.append(send(part.at[0], from_core.at[e, 0], c_dev, ex_recv[name][0]))
        elif stage == 1:
            compute(far, part.at[1])
        elif stage == 2:
            recv(from_core.at[e, 0], ex_recv[name][0])

            def add(i):
                r = tile(i, 32)
                pair_sum[r, :] = (part[1, r, :].astype(F32) + from_core[e, 0, r, :].astype(F32)).astype(BF)

            loop(quarter // 32, add)
            ex_sent.append(send(pair_sum, from_y.at[e], y_dev, ex_recv[name][2]))
        elif stage == 3:
            compute(rows_of(y, 1 - t), part.at[2])
            ex_sent.append(send(part.at[2], from_core.at[e, 1], c_dev, ex_recv[name][1]))
        elif stage == 4:
            compute(own_rows, part.at[3])
        else:
            recv(from_core.at[e, 1], ex_recv[name][1])
            recv(from_y.at[e], ex_recv[name][2])

    def total_of(name, r):
        e = kinds[name]
        return part[3, r, :].astype(F32) + from_core[e, 1, r, :].astype(F32) + from_y[e, r, :].astype(F32)

    def spread_rows(ref, idx):
        return [
            send(ref.at[own_rows, :], ref.at[own_rows, :], c_dev, idx[0]),
            send(ref.at[own_rows, :], ref.at[own_rows, :], y_dev, idx[1]),
        ]

    h2_idx = many(3)
    ab_idx = many(3)

    grads = {
        "d0": (p_d0, r_d0, s_d0, f_d0, True),
        "d1": (p_d1, r_d1, s_d1, f_d1, False),
        "g0": (p_g0, r_g0, s_g0, f_g0, False),
        "g1": (p_g1, r_g1, s_g1, f_g1, False),
        "u0": (p_u0, r_u0, s_u0, f_u0, False),
        "u1": (p_u1, r_u1, s_u1, f_u1, False),
        "o": (p_o, r_o, s_o, f_o, False),
        "q": (p_q, r_q, s_q, f_q, False),
        "k": (p_k, r_k, s_k, f_k, False),
        "v": (p_v, r_v, s_v, f_v, False),
        "n": (p_n, r_n, s_n, f_n, False),
    }
    gx = {name: [None] + many(1 if item[4] else nz) for name, item in grads.items()}
    gz = {name: [[None] + many(nz - 1) for _ in range(2 if item[4] else 1)] for name, item in grads.items()}

    def add_rows(rows, cols, body):
        step = min(rows, 16 if cols > 512 else 128)
        loop(rows // step, lambda i: body(tile(i, step)))

    def grad_send(name, k):
        p, r, s, _, ring_first = grads[name]
        if ring_first:
            send(p.at[lax.rem(x + k, 2), z_from(1)], s.at[k - 1, 0], z_next, gz[name][k - 1][1])
        else:
            send(p.at[1 - x, z_from(k)], r.at[k - 1], x_dev, gx[name][k])

    def grad_step(name, k):
        p, r, s, f, ring_first = grads[name]
        if ring_first:
            c, k = divmod(k, 10)
            xq = lax.rem(x + 1 + c, 2)
            recv(s.at[c, k - 2], gz[name][c][k - 1])
            last_own = k == nz and c == 1
            if last_own:
                recv(r.at[0], gx[name][1])

            def add_ring(rr):
                total = p[xq, z_from(k), rr, :].astype(F32) + s[c, k - 2, rr, :].astype(F32)
                if last_own:
                    f[rr, :] = (total + r[0, rr, :].astype(F32)).astype(f.dtype)
                else:
                    p[xq, z_from(k), rr, :] = total.astype(p.dtype)

            add_rows(*p.shape[2:], add_ring)
            if k < nz:
                send(p.at[xq, z_from(k)], s.at[c, k - 1], z_next, gz[name][c][k])
            elif c == 0:
                send(p.at[xq, z_from(k)], r.at[0], x_dev, gx[name][1])
            return
        zq = z_from(k)
        recv(r.at[k - 1], gx[name][k])
        if k > 1:
            recv(s.at[0, k - 2], gz[name][0][k - 1])

        def add(rr):
            total = p[x, zq, rr, :].astype(F32) + r[k - 1, rr, :].astype(F32)
            if k > 1:
                total = total + s[0, k - 2, rr, :].astype(F32)
            if k < nz:
                p[x, zq, rr, :] = total.astype(p.dtype)
            else:
                f[rr, :] = total.astype(f.dtype)

        add_rows(*p.shape[2:], add)
        if k < nz:
            send(p.at[x, zq], s.at[0, k - 1], z_next, gz[name][0][k])

    def place_of(name, yq):
        h = pl.ds(pl.multiple_of(yq * heads_w, heads_w), heads_w)
        if name[0] == "d":
            return o_d.at[half_of(int(name[1]), yq), :]
        if name == "o":
            return o_o.at[h, :]
        wide = {"g": o_g, "u": o_u}
        if name[0] in wide:
            return wide[name[0]].at[:, half_of(int(name[1]), yq)]
        return {"q": o_q, "k": o_k, "v": o_v}[name].at[:, h]

    out_idx = {name: many(1)[0] for name in grads if name != "n"}
    last_local = []

    def grad_end(name):
        f = grads[name][3]
        last_local.append(local(f, place_of(name, y)))
        send(f, place_of(name, y), y_dev, out_idx[name])

    def grad_done(name):
        recv(place_of(name, 1 - y), out_idx[name])

    value = {}
    blocks = half_len // BLOCK
    pairs = heads_w // (2 * HEAD_DIM)
    out_c, gtok_c = many(2)
    n_c, n_y = many(2)
    my_rows = tile(t, quarter)
    other_rows = tile(1 - t, quarter)
    row_sends = []

    def send_tok():
        send(tok.at[tile(t, quarter), :], xg.at[own_rows, :], y_dev, tok_y)

    def send_cot():
        send(cot.at[tile(t, quarter), :], cg.at[own_rows, :], y_dev, cot_y)

    def gather_gains():
        value["one"] = jnp.concatenate([gain_all[i, 0:1, :] for i in range(2 * nz)], axis=1)
        value["two"] = jnp.concatenate([gain_all[i, 1:2, :] for i in range(2 * nz)], axis=1)

    def norm_rows(start):
        gain_one = value["one"]

        def body(i):
            r = pl.ds(pl.multiple_of(start + i * 32, 32), 32)
            values = xg[r, :].astype(F32)
            inverse = lax.rsqrt(jnp.mean(values * values, axis=-1, keepdims=True) + EPSILON)
            h1[r, :] = (values * inverse * gain_one).astype(BF)

        loop(half_len // 32, body)

    def norm_own():
        tok_local.wait()
        norm_rows(y * half_len)

    def norm_far():
        recv(xg.at[far_other, :], tok_c)
        norm_rows((1 - y) * half_len)

    def segments():
        seg_local.wait()
        recv(seg_row.at[:, tile(1 - y, half_len)], seg_y)
        seg_col[...] = jnp.broadcast_to(seg_row[0:1, :], (128, 2 * half_len)).T

    def project():
        def body(i):
            r = tile(i, 512)
            rows = h1[r, :]
            query[r, :] = (dot_nn(rows, wqkv[:, 0:heads_w]).astype(BF).astype(F32) * SCALE).astype(BF)
            keys[r, :] = dot_nn(rows, wqkv[:, heads_w : 2 * heads_w]).astype(BF)
            vals[r, :] = dot_nn(rows, wqkv[:, 2 * heads_w : 3 * heads_w]).astype(BF)

        loop(xg.shape[0] // 512, body)
        keys_t[...] = keys[...].T
        vals_t[...] = vals[...].T

    def either(half, body):
        @pl.when(half == 0)
        def _():
            body(half_len)

        @pl.when(half == 1)
        def _():
            body(2 * half_len)

    def attend(half, i):
        args = (pairs, query, keys, vals_t, bias, seg_col, seg_row, mixed, mixed_t, log_sum)
        either(half, lambda length: attend_block(half * blocks + i, length, *args))

    def out_rows(r, dst):
        dst[...] = dot_nn(mixed[r, :], wo[...]).astype(BF)

    def first_residual():
        exchange("a", None, 5)
        gain_two = value["two"]

        def body(i):
            r = tile(i, 32)
            rr = pl.ds(pl.multiple_of(y * half_len + t * quarter + i * 32, 32), 32)
            values = xg[rr, :].astype(F32) + total_of("a", r)
            y1[r, :] = values
            inverse = lax.rsqrt(jnp.mean(values * values, axis=-1, keepdims=True) + EPSILON)
            h2[rr, :] = (values * inverse * gain_two).astype(BF)

        loop(quarter // 32, body)
        row_sends.extend(spread_rows(h2, h2_idx))

    def gate(half, r):
        rows = h2[r, :]

        def cols(j):
            c = pl.ds(pl.multiple_of(half * part_h + j * 256, 256), 256)
            g = dot_nn(rows, wg[:, c])
            u = dot_nn(rows, wu[:, c])
            sg = 1.0 / (1.0 + jnp.exp(-g))
            gs = g * sg
            act_u[r, c] = gs.astype(BF)
            act_g[r, c] = (u * sg * (1.0 + g * (1.0 - sg))).astype(BF)
            act_m[r, c] = (gs * u).astype(BF)

        loop(part_h // 256, cols)

    def grad_cols(left, start, right, p, index):
        c = tile(index, 2 * db)
        for i in range(p.shape[2] // 256):
            r = slice(start + i * 256, start + (i + 1) * 256)
            both = dot_tn(left[:, r], right[:, c]).astype(BF)
            rows = slice(i * 256, (i + 1) * 256)
            p[0, index, rows, :] = both[:, 0:db]
            p[1, index, rows, :] = both[:, db : 2 * db]

    def grad_rows(left, right, units, p, index):
        c = tile(index, 2 * db)
        both = dot_tn(left[:, c], right[:, units]).astype(BF)
        p[0, index] = both[0:db, :]
        p[1, index] = both[db : 2 * db, :]

    def grad_down(part_of, p):
        loop(nz, lambda i: grad_cols(act_m, part_of * part_h, cg, p, i))

    def some_blocks(name, left, right, units, ks):
        p = grads[name][0]
        loop(len(ks), lambda i: grad_rows(left, right, units, p, z_from(ks[0] + i)))
        for k in ks:
            grad_send(name, k)

    def qkv_blocks(ks):
        def body(i):
            index = z_from(ks[0] + i)
            both = dot_tn(h1[:, tile(index, 2 * db)], grad_qkv[...]).astype(BF)
            for j, p in enumerate((p_q, p_k, p_v)):
                c = slice(j * heads_w, (j + 1) * heads_w)
                p[0, index] = both[0:db, c]
                p[1, index] = both[db : 2 * db, c]

        loop(len(ks), body)

    def hidden_back(half, r, dst):
        rows = cg[r, :]
        units = (first, second)[half]

        def cols(j):
            c = pl.ds(pl.multiple_of(half * part_h + j * 256, 256), 256)
            dm = dot_nt(rows, wd[c, :])
            act_g[r, c] = (dm * act_g[r, c].astype(F32)).astype(BF)
            act_u[r, c] = (dm * act_u[r, c].astype(F32)).astype(BF)

        loop(part_h // 256, cols)

        def back(j):
            c = tile(j, 512)
            total = dot_nt(act_g[r, units], wg[c, units]) + dot_nt(act_u[r, units], wu[c, units])
            if half == 0:
                ab[r, c] = total.astype(BF)
            else:
                dst[:, c] = (total + ab[r, c].astype(F32)).astype(BF)

        loop(width // 512, back)

    def second_residual():
        exchange("dh2", None, 5)
        gain_two = value["two"]

        def body(i, carry):
            r = tile(i, 32)
            rr = pl.ds(pl.multiple_of(y * half_len + t * quarter + i * 32, 32), 32)
            values = y1[r, :]
            inverse = lax.rsqrt(jnp.mean(values * values, axis=-1, keepdims=True) + EPSILON)
            normed = values * inverse
            grad = total_of("dh2", r)
            scaled = grad * gain_two
            mean = jnp.mean(scaled * normed, axis=-1, keepdims=True)
            full = cg[rr, :].astype(F32) + inverse * (scaled - normed * mean)
            final_rows[r, :] = full
            ab[rr, :] = full.astype(BF)
            return carry + jnp.sum(grad * normed, axis=0, keepdims=True)

        value["grad_two"] = lax.fori_loop(0, quarter // 32, body, jnp.zeros((1, width), F32))
        row_sends.extend(spread_rows(ab, ab_idx))

    def down_rows(r, dst):
        def cols(j):
            c = tile(j, 512)
            dst[:, c] = dot_nn(act_m[r, :], wd[:, c]).astype(BF)

        loop(width // 512, cols)

    def mixed_back(half):
        r = tile(half, half_len)
        grad_mixed[r, :] = dot_nt(ab[r, :], wo[...]).astype(BF)

    def clear_sums():
        grad_k[...] = jnp.zeros_like(grad_k)
        grad_v[...] = jnp.zeros_like(grad_v)

    def attend_back(half, i):
        args = (
            pairs, query, keys, keys_t, vals, grad_mixed, bias, seg_col, seg_row, log_sum, grad_qkv, mixed_t, grad_k, grad_v,
        )
        either(half, lambda length: attend_back_block(half * blocks + i, length, *args))

    def own_back():
        recv(ab.at[rows_of(y, 1 - t), :], ab_idx[0])
        clear_sums()
        mixed_back(y)

    def far_back():
        recv(ab.at[far_other, :], ab_idx[2])
        mixed_back(1 - y)

    def grad_out_all():
        loop(nz, lambda i: grad_cols(mixed, 0, ab, p_o, i))
        for k in range(1, nz + 1):
            grad_send("o", k)

    def sums_to_bf16():
        grad_qkv[:, heads_w : 2 * heads_w] = grad_k[...].astype(BF)
        grad_qkv[:, 2 * heads_w : 3 * heads_w] = grad_v[...].astype(BF)

    def hidden_one_back(r, dst):
        def cols(j):
            c = tile(j, 512)
            dst[:, c] = dot_nt(grad_qkv[r, :], wqkv[c, :]).astype(BF)

        loop(width // 512, cols)

    def finish_out():
        exchange("out", None, 5)

        def body(i):
            r = tile(i, 32)
            act_m[r, 0:width] = (y1[r, :] + total_of("out", r)).astype(BF)

        loop(quarter // 32, body)
        last_local.append(local(act_m.at[0:quarter, 0:width], out.at[my_rows, :]))
        send(act_m.at[0:quarter, 0:width], out.at[my_rows, :], c_dev, out_c)

    def finish_tokens():
        exchange("dh1", None, 5)
        drain(row_sends)
        gain_one = value["one"]

        def body(i, carry):
            r = tile(i, 32)
            rr = pl.ds(pl.multiple_of(y * half_len + t * quarter + i * 32, 32), 32)
            values = xg[rr, :].astype(F32)
            inverse = lax.rsqrt(jnp.mean(values * values, axis=-1, keepdims=True) + EPSILON)
            normed = values * inverse
            grad = total_of("dh1", r)
            scaled = grad * gain_one
            mean = jnp.mean(scaled * normed, axis=-1, keepdims=True)
            full = final_rows[r, :] + inverse * (scaled - normed * mean)
            h2[r, :] = full.astype(BF)
            return carry + jnp.sum(grad * normed, axis=0, keepdims=True)

        gain_one_grad = lax.fori_loop(0, quarter // 32, body, jnp.zeros((1, width), F32))
        for i in range(2 * nz):
            c = slice(i * db, (i + 1) * db)
            p_n[i % 2, i // 2] = jnp.concatenate(
                [gain_one_grad[:, c], value["grad_two"][:, c], jnp.zeros((6, db), F32)], axis=0
            )
        for k in range(1, nz + 1):
            grad_send("n", k)
        last_local.append(local(h2.at[0:quarter, :], g_tok.at[my_rows, :]))
        send(h2.at[0:quarter, :], g_tok.at[my_rows, :], c_dev, gtok_c)

    def gains_core():
        send(f_n, c_n, c_dev, n_c)

    def gains_y():
        recv(c_n, n_c)
        y_n[0] = f_n[...] + c_n[...]
        send(y_n.at[0], y_n.at[1], y_dev, n_y)

    def gains_end():
        recv(y_n.at[1], n_y)
        o_gain[...] = y_n[0] + y_n[1]

    def finish():
        for name in out_idx:
            grad_done(name)
        recv(out.at[other_rows, :], out_c)
        recv(g_tok.at[other_rows, :], gtok_c)
        for copy in last_local:
            copy.wait()
        drain(list(sent))

    two = (1, 2), (3, 4)
    tasks = [
        send_tok,
        send_cot,
        gather_gains,
        lambda: core_forward(xg, tok_y, tok_c),
        lambda: core_forward(cg, cot_y, cot_c),
        lambda: (cot_local.wait(), recv(cg.at[far_other, :], cot_c)),
        segments,
        norm_own,
        norm_far,
        project,
        first_residual,
        lambda: row_sends.append(core_forward(h2, h2_idx[1], h2_idx[2])),
        lambda: recv(h2.at[rows_of(y, 1 - t), :], h2_idx[0]),
        lambda: recv(h2.at[far_other, :], h2_idx[2]),
        lambda: grad_down(0, p_d0),
        lambda: grad_down(1, p_d1),
        second_residual,
        lambda: row_sends.append(core_forward(ab, ab_idx[1], ab_idx[2])),
        own_back,
        far_back,
        grad_out_all,
        sums_to_bf16,
        finish_out,
        finish_tokens,
        gains_core,
        gains_y,
        gains_end,
        finish,
    ]
    all_rows = (own_rows, rows_of(y, 1 - t), far, far_other)
    tasks += [functools.partial(gate, half, r) for half in (0, 1) for r in all_rows]
    tasks += [functools.partial(hidden_back, 0, r, None) for r in all_rows]
    for i, units in enumerate((first, second)):
        tasks += [functools.partial(some_blocks, f"g{i}", h2, act_g, units, ks) for ks in two]
        tasks += [functools.partial(some_blocks, f"u{i}", h2, act_u, units, ks) for ks in two]
    tasks += [functools.partial(qkv_blocks, ks) for ks in two]
    tasks += [functools.partial(attend, half, i) for half in (1 - y, y) for i in range(blocks)]
    tasks += [functools.partial(attend_back, half, i) for half in (y, 1 - y) for i in range(blocks)]
    for name, compute in zip(kinds, (out_rows, down_rows, functools.partial(hidden_back, 1), hidden_one_back)):
        tasks += [functools.partial(exchange, name, compute, i) for i in range(5)]
    for name in names:
        tasks += [functools.partial(start_z, name), functools.partial(start_x, name), functools.partial(arrived, name)]
        tasks += [functools.partial(relay, name, k) for k in range(1, nz)]
        if names[name][2]:
            tasks += [functools.partial(relay_other, name, k) for k in range(nz)]
    for name in grads:
        if name in out_idx:
            tasks.append(functools.partial(grad_end, name))
        if grads[name][4]:
            tasks += [functools.partial(grad_step, name, 10 * c + k) for c in (0, 1) for k in range(2, nz + 1)]
        else:
            tasks += [functools.partial(grad_step, name, k) for k in range(1, nz + 1)]
    for name in ("d0", "d1", "q", "k", "v"):
        tasks += [functools.partial(grad_send, name, k) for k in ((1, 2) if grads[name][4] else range(1, nz + 1))]
    assert sorted(ORDER) == list(range(len(tasks)))
    for index in ORDER:
        tasks[index]()


def fused(nz, tokens, segment_ids, w_query, w_key, w_value, w_out, w_gate, w_up, w_down, gain_attn, gain_ffn, cotangent):
    half_len, _, width = tokens.shape
    length = 2 * half_len
    quarter = half_len // 2
    heads_w = w_query.shape[1] // 2
    hidden = w_gate.shape[1] // 2
    db = w_query.shape[0]
    heads = heads_w // HEAD_DIM
    gains = jnp.stack([gain_attn, gain_ffn]).astype(F32)

    def vm(*shape, dtype=BF):
        return pltpu.VMEM(shape, dtype)

    shape_d, shape_g, shape_o, shape_q = (hidden // 2, db), (db, hidden // 2), (heads_w, db), (db, heads_w)
    shapes = (shape_d, shape_d, *[shape_g] * 4, shape_o, shape_q, shape_q, shape_q)
    ring_first = (True, *[False] * 9)
    scratch = [
        vm(length, width), vm(length, width), vm(1, length, dtype=I32), vm(2 * nz, 2, db, dtype=F32),
        vm(width, 3 * heads_w), vm(heads_w, width), vm(width, hidden), vm(width, hidden), vm(hidden, width),
        vm(length, width), vm(length, width), vm(length, width),
        vm(length, heads_w), vm(length, heads_w), vm(length, heads_w), vm(heads_w, length), vm(heads_w, length),
        vm(length, heads_w), vm(length, heads_w), vm(length, 3 * heads_w),
        vm(length, heads_w, dtype=F32), vm(length, heads_w, dtype=F32),
        vm(length, hidden), vm(length, hidden), vm(length, hidden),
        vm(quarter, width, dtype=F32), vm(length, BLOCK, dtype=F32), vm(heads_w, BLOCK, dtype=F32),
        vm(heads, 8, length, dtype=F32), vm(length, 128, dtype=I32),
        vm(4, quarter, width), vm(quarter, width), vm(4, 2, quarter, width), vm(4, quarter, width),
        vm(quarter, width, dtype=F32),
    ]
    scratch += [vm(2, nz, *shape) for shape in shapes]
    scratch += [vm(1 if first else nz, *shape) for shape, first in zip(shapes, ring_first)]
    scratch += [vm(2 if first else 1, nz - 1, *shape) for shape, first in zip(shapes, ring_first)]
    scratch += [vm(*shape) for shape in shapes]
    scratch += [
        vm(2, nz, 8, db, dtype=F32), vm(nz, 8, db, dtype=F32), vm(1, nz - 1, 8, db, dtype=F32), vm(8, db, dtype=F32),
        vm(8, db, dtype=F32), vm(2, 8, db, dtype=F32),
    ]
    scratch += [pltpu.SemaphoreType.DMA((SEMS[0],)), pltpu.SemaphoreType.DMA((SEMS[1],)), pltpu.SemaphoreType.DMA((SEMS[2],))]
    anywhere = pl.BlockSpec(memory_space=pl.ANY)
    weights = (w_query, w_key, w_value, w_out, w_gate, w_up, w_down)
    results = pl.pallas_call(
        functools.partial(layer_kernel, nz),
        out_shape=[jax.ShapeDtypeStruct((half_len, width), BF)] * 2
        + [jax.ShapeDtypeStruct(item.shape, BF) for item in weights]
        + [jax.ShapeDtypeStruct((8, db), F32)],
        in_specs=[anywhere] * 11,
        out_specs=[anywhere] * 9 + [pl.BlockSpec(memory_space=pltpu.VMEM)],
        scratch_shapes=scratch,
        compiler_params=pltpu.CompilerParams(
            collective_id=0, has_side_effects=True, vmem_limit_bytes=VMEM_BYTES
        ),
        name="layer",
    )(tokens.reshape(half_len, width), cotangent.reshape(half_len, width), segment_ids, gains, *weights)
    bodies = results[:9]
    wide = [jax.ShapeDtypeStruct(item.shape, BF if i < 2 else F32) for i, item in enumerate(bodies)]

    def widen(*refs):
        srcs, rows, dsts, (one, two), held = refs[:9], refs[9], refs[10:19], refs[19:21], refs[21:30]
        finals, (load_sems, store_sems) = refs[30:37], refs[37:]
        order = [*range(6, 9), *range(2, 6), 0, 1]
        loads = {i: pltpu.make_async_copy(srcs[i], held[i], load_sems.at[i]) for i in order}
        for i in order:
            loads[i].start()
        one[...] = rows[0:1, :]
        two[...] = rows[1:2, :]
        stores = []
        for i in order:
            loads[i].wait()
            if i >= 2:
                finals[i - 2][...] = held[i][...].astype(F32)
            stores.append(pltpu.make_async_copy(finals[i - 2] if i >= 2 else held[i], dsts[i], store_sems.at[i]))
            stores[-1].start()
        for copy in stores:
            copy.wait()

    inside = pl.BlockSpec(memory_space=pltpu.VMEM)
    finals = pl.pallas_call(
        widen,
        out_shape=wide + [jax.ShapeDtypeStruct((1, db), F32)] * 2,
        in_specs=[anywhere] * 9 + [inside],
        out_specs=[anywhere] * 9 + [inside] * 2,
        scratch_shapes=[vm(*item.shape) for item in bodies]
        + [vm(*item.shape, dtype=F32) for item in wide[2:]]
        + [pltpu.SemaphoreType.DMA((9,)), pltpu.SemaphoreType.DMA((9,))],
        compiler_params=pltpu.CompilerParams(vmem_limit_bytes=VMEM_BYTES),
        name="widen",
    )(*results)
    shape = tokens.shape
    return (finals[0].reshape(shape), finals[1].reshape(shape), *finals[2:9], finals[9].reshape(db), finals[10].reshape(db))


def fits(mesh, tokens_shape):
    return mesh.shape["fsdp"] == 8 and mesh.shape["ctx"] == 2 and mesh.shape["tp"] == 2 and tokens_shape[1:] == (1, 1024)


def solution(mesh):
    def step(tokens, *rest):
        if fits(mesh, tokens.shape):
            return fused(mesh.shape["fsdp"] // 2, tokens, *rest)
        return local(tokens, *rest)

    return jax.shard_map(
        step,
        mesh=mesh,
        in_specs=(
            P("ctx", "fsdp", None),
            P("fsdp", "ctx"),
            P("fsdp", "tp"),
            P("fsdp", "tp"),
            P("fsdp", "tp"),
            P("tp", "fsdp"),
            P("fsdp", "tp"),
            P("fsdp", "tp"),
            P("tp", "fsdp"),
            P("fsdp"),
            P("fsdp"),
            P("ctx", "fsdp", None),
        ),
        out_specs=(
            P("ctx", "fsdp", None),
            P("ctx", "fsdp", None),
            P("fsdp", "tp"),
            P("fsdp", "tp"),
            P("fsdp", "tp"),
            P("tp", "fsdp"),
            P("fsdp", "tp"),
            P("fsdp", "tp"),
            P("tp", "fsdp"),
            P("fsdp"),
            P("fsdp"),
        ),
        check_vma=False,
    )
```

```python
import functools

import jax
import jax.numpy as jnp
from jax import lax
from jax.experimental import pallas as pl
from jax.experimental.pallas import tpu as pltpu
from jax.sharding import PartitionSpec as P

HEAD_DIM = 64


EPSILON = 1e-05
SCALE = 0.125
MASKED = -1e30


def normalize(values):
    inverse = lax.rsqrt(jnp.mean(values * values, axis=-1, keepdims=True) + EPSILON)
    return (values * inverse, inverse)


def norm_back(grad_normed, normed, inverse):
    return inverse * (grad_normed - normed * jnp.mean(grad_normed * normed, axis=-1, keepdims=True))


def inner_rows(left, right):
    return lax.dot_general(
        left, right, (((0,), (0,)), ((), ())), preferred_element_type=jnp.float32
    )


def times_transposed(left, weight):
    return lax.dot_general(
        left, weight, (((1,), (1,)), ((), ())), preferred_element_type=jnp.float32
    )


def head_sum(partial_sum):
    return lax.psum(partial_sum, "tp")


def split_heads(values, head_size):
    length, sequences, width = values.shape
    return jnp.moveaxis(values.reshape(length, sequences, width // head_size, head_size), 2, 0)


def join_heads(values):
    heads, length, sequences, head_size = values.shape
    return jnp.moveaxis(values, 0, 2).reshape(length, sequences, heads * head_size)


def make_mask(query_pos, query_seg, key_pos, key_seg):
    before = key_pos[None, None, :] <= query_pos[None, :, None]
    same = query_seg.T[:, :, None] == key_seg.T[:, None, :]
    return before & same


def key_head_grads(parts, use_mask):
    q_head, k_head, v_head, d_head, log_total, delta = parts
    scores = jnp.einsum("qsd,ksd->sqk", q_head, k_head, preferred_element_type=jnp.float32) * SCALE
    probs = jnp.exp(jnp.where(use_mask, scores, MASKED) - log_total)
    grad_probs = jnp.einsum("qsd,ksd->sqk", d_head, v_head, preferred_element_type=jnp.float32)
    grad_scores = (probs * (grad_probs - delta)).astype(jnp.bfloat16)
    grad_v = jnp.einsum(
        "sqk,qsd->ksd", probs.astype(jnp.bfloat16), d_head, preferred_element_type=jnp.float32
    )
    grad_k = (
        jnp.einsum("sqk,qsd->ksd", grad_scores, q_head, preferred_element_type=jnp.float32) * SCALE
    )
    return (grad_k, grad_v)


def local(
    tokens,
    segment_ids,
    w_query,
    w_key,
    w_value,
    w_out,
    w_gate,
    w_up,
    w_down,
    gain_attn,
    gain_ffn,
    cotangent,
):
    local_len, sequences, width = tokens.shape
    rows = local_len * sequences
    (
        full_query,
        full_key,
        full_value,
        full_out,
        full_gate,
        full_up,
        full_down,
        full_gain_one,
        full_gain_two,
    ) = (
        lax.all_gather(w_query, "fsdp", axis=0, tiled=True),
        lax.all_gather(w_key, "fsdp", axis=0, tiled=True),
        lax.all_gather(w_value, "fsdp", axis=0, tiled=True),
        lax.all_gather(w_out, "fsdp", axis=1, tiled=True),
        lax.all_gather(w_gate, "fsdp", axis=0, tiled=True),
        lax.all_gather(w_up, "fsdp", axis=0, tiled=True),
        lax.all_gather(w_down, "fsdp", axis=1, tiled=True),
        lax.all_gather(gain_attn, "fsdp", axis=0, tiled=True),
        lax.all_gather(gain_ffn, "fsdp", axis=0, tiled=True),
    )
    gain_one = full_gain_one.astype(jnp.float32)
    gain_two = full_gain_two.astype(jnp.float32)
    head_width = full_query.shape[1]
    flat = tokens.astype(jnp.float32).reshape(rows, width)
    normed_one, inverse_one = normalize(flat)
    hidden_one = (normed_one * gain_one).astype(jnp.bfloat16)
    query = (
        jnp.dot(hidden_one, full_query, preferred_element_type=jnp.float32)
        .astype(jnp.bfloat16)
        .reshape(local_len, sequences, head_width)
    )
    keys = (
        jnp.dot(hidden_one, full_key, preferred_element_type=jnp.float32)
        .astype(jnp.bfloat16)
        .reshape(local_len, sequences, head_width)
    )
    vals = (
        jnp.dot(hidden_one, full_value, preferred_element_type=jnp.float32)
        .astype(jnp.bfloat16)
        .reshape(local_len, sequences, head_width)
    )
    pair = jnp.concatenate([keys, vals], axis=-1)
    seg_local = segment_ids.T
    pair_all, seg_all = (
        lax.all_gather(pair, "ctx", axis=0, tiled=True),
        lax.all_gather(seg_local, "ctx", axis=0, tiled=True),
    )
    length = pair_all.shape[0]
    query_pos = lax.axis_index("ctx") * local_len + jnp.arange(local_len, dtype=jnp.int32)
    all_pos = jnp.arange(length, dtype=jnp.int32)
    mask = make_mask(query_pos, seg_local, all_pos, seg_all)
    q_heads = split_heads(query, HEAD_DIM)
    k_heads = split_heads(pair_all[..., :head_width], HEAD_DIM)
    v_heads = split_heads(pair_all[..., head_width:], HEAD_DIM)

    def attend(parts):
        q_head, k_head, v_head = parts
        scores = (
            jnp.einsum("qsd,ksd->sqk", q_head, k_head, preferred_element_type=jnp.float32) * SCALE
        )
        scores = jnp.where(mask, scores, MASKED)
        row_max = jnp.max(scores, axis=-1, keepdims=True)
        log_total = row_max + jnp.log(jnp.sum(jnp.exp(scores - row_max), axis=-1, keepdims=True))
        probs = jnp.exp(scores - log_total).astype(jnp.bfloat16)
        return (
            jnp.einsum("sqk,ksd->qsd", probs, v_head, preferred_element_type=jnp.float32),
            log_total,
        )

    attended, log_totals = lax.map(attend, (q_heads, k_heads, v_heads))
    mixed = join_heads(attended).astype(jnp.bfloat16).reshape(rows, head_width)
    resid = flat + head_sum(jnp.dot(mixed, full_out, preferred_element_type=jnp.float32))
    normed_two, inverse_two = normalize(resid)
    hidden_two = (normed_two * gain_two).astype(jnp.bfloat16)
    gate = jnp.dot(hidden_two, full_gate, preferred_element_type=jnp.float32)
    upward = jnp.dot(hidden_two, full_up, preferred_element_type=jnp.float32)
    sigmoid_gate = jax.nn.sigmoid(gate)
    swish_up = (gate * sigmoid_gate * upward).astype(jnp.bfloat16)
    result = resid + head_sum(jnp.dot(swish_up, full_down, preferred_element_type=jnp.float32))
    output = result.astype(jnp.bfloat16).reshape(local_len, sequences, width)
    (
        full_query,
        full_key,
        full_value,
        full_out,
        full_gate,
        full_up,
        full_down,
        full_gain_one,
        full_gain_two,
    ) = (
        lax.all_gather(w_query, "fsdp", axis=0, tiled=True),
        lax.all_gather(w_key, "fsdp", axis=0, tiled=True),
        lax.all_gather(w_value, "fsdp", axis=0, tiled=True),
        lax.all_gather(w_out, "fsdp", axis=1, tiled=True),
        lax.all_gather(w_gate, "fsdp", axis=0, tiled=True),
        lax.all_gather(w_up, "fsdp", axis=0, tiled=True),
        lax.all_gather(w_down, "fsdp", axis=1, tiled=True),
        lax.all_gather(gain_attn, "fsdp", axis=0, tiled=True),
        lax.all_gather(gain_ffn, "fsdp", axis=0, tiled=True),
    )
    gain_one = full_gain_one.astype(jnp.float32)
    gain_two = full_gain_two.astype(jnp.float32)
    grad_result = cotangent.astype(jnp.float32).reshape(rows, width)
    grad_low = grad_result.astype(jnp.bfloat16)
    grad_wdown = inner_rows(swish_up, grad_low)
    grad_swish = times_transposed(grad_low, full_down)
    grad_gate_act = (
        grad_swish * upward * sigmoid_gate * (1.0 + gate * (1.0 - sigmoid_gate))
    ).astype(jnp.bfloat16)
    grad_upward = (grad_swish * gate * sigmoid_gate).astype(jnp.bfloat16)
    grad_wgate = inner_rows(hidden_two, grad_gate_act)
    grad_wup = inner_rows(hidden_two, grad_upward)
    grad_hidden_two = head_sum(
        times_transposed(grad_gate_act, full_gate) + times_transposed(grad_upward, full_up)
    )
    grad_gain_two = jnp.sum(grad_hidden_two * normed_two, axis=0)
    grad_resid = grad_result + norm_back(grad_hidden_two * gain_two, normed_two, inverse_two)
    grad_branch = grad_resid.astype(jnp.bfloat16)
    grad_wout = inner_rows(mixed, grad_branch)
    grad_mixed = (
        times_transposed(grad_branch, full_out)
        .astype(jnp.bfloat16)
        .reshape(local_len, sequences, head_width)
    )
    d_heads = split_heads(grad_mixed, HEAD_DIM)

    def query_side(parts):
        q_head, k_head, v_head, d_head, log_total = parts
        scores = (
            jnp.einsum("qsd,ksd->sqk", q_head, k_head, preferred_element_type=jnp.float32) * SCALE
        )
        probs = jnp.exp(jnp.where(mask, scores, MASKED) - log_total)
        grad_probs = jnp.einsum("qsd,ksd->sqk", d_head, v_head, preferred_element_type=jnp.float32)
        delta = jnp.sum(probs * grad_probs, axis=-1, keepdims=True)
        grad_scores = (probs * (grad_probs - delta)).astype(jnp.bfloat16)
        return (
            jnp.einsum("sqk,ksd->qsd", grad_scores, k_head, preferred_element_type=jnp.float32)
            * SCALE,
            delta,
        )

    grad_q_heads, deltas = lax.map(query_side, (q_heads, k_heads, v_heads, d_heads, log_totals))
    grad_query = join_heads(grad_q_heads).astype(jnp.bfloat16).reshape(rows, head_width)
    piece_mask = make_mask(
        query_pos, seg_local, jnp.arange(local_len * lax.axis_size("ctx"), dtype=jnp.int32), seg_all
    )
    k_piece = split_heads(pair_all[..., :head_width], HEAD_DIM)
    v_piece = split_heads(pair_all[..., head_width:], HEAD_DIM)

    def per_head(parts):
        return key_head_grads(parts, piece_mask)

    grad_k_heads, grad_v_heads = lax.map(
        per_head, (q_heads, k_piece, v_piece, d_heads, log_totals, deltas)
    )
    grad_pair = lax.psum_scatter(
        jnp.concatenate([join_heads(grad_k_heads), join_heads(grad_v_heads)], axis=-1).astype(
            jnp.bfloat16
        ),
        "ctx",
        scatter_dimension=0,
        tiled=True,
    ).astype(jnp.float32)
    grad_keys = grad_pair[..., :head_width].astype(jnp.bfloat16).reshape(rows, head_width)
    grad_vals = grad_pair[..., head_width:].astype(jnp.bfloat16).reshape(rows, head_width)
    grad_wquery = inner_rows(hidden_one, grad_query)
    grad_wkey = inner_rows(hidden_one, grad_keys)
    grad_wvalue = inner_rows(hidden_one, grad_vals)
    grad_hidden_one = head_sum(
        times_transposed(grad_query, full_query)
        + times_transposed(grad_keys, full_key)
        + times_transposed(grad_vals, full_value)
    )
    grad_gain_one = jnp.sum(grad_hidden_one * normed_one, axis=0)
    grad_input = grad_resid + norm_back(grad_hidden_one * gain_one, normed_one, inverse_one)
    grad_input = grad_input.astype(jnp.bfloat16).reshape(local_len, sequences, width)
    shares = (
        lax.psum_scatter(
            grad_wquery.astype(jnp.bfloat16), "fsdp", scatter_dimension=0, tiled=True
        ).astype(jnp.float32),
        lax.psum_scatter(
            grad_wkey.astype(jnp.bfloat16), "fsdp", scatter_dimension=0, tiled=True
        ).astype(jnp.float32),
        lax.psum_scatter(
            grad_wvalue.astype(jnp.bfloat16), "fsdp", scatter_dimension=0, tiled=True
        ).astype(jnp.float32),
        lax.psum_scatter(
            grad_wout.astype(jnp.bfloat16), "fsdp", scatter_dimension=1, tiled=True
        ).astype(jnp.float32),
        lax.psum_scatter(
            grad_wgate.astype(jnp.bfloat16), "fsdp", scatter_dimension=0, tiled=True
        ).astype(jnp.float32),
        lax.psum_scatter(
            grad_wup.astype(jnp.bfloat16), "fsdp", scatter_dimension=0, tiled=True
        ).astype(jnp.float32),
        lax.psum_scatter(
            grad_wdown.astype(jnp.bfloat16), "fsdp", scatter_dimension=1, tiled=True
        ).astype(jnp.float32),
        lax.psum_scatter(
            grad_gain_one.astype(jnp.bfloat16), "fsdp", scatter_dimension=0, tiled=True
        ).astype(jnp.float32),
        lax.psum_scatter(
            grad_gain_two.astype(jnp.bfloat16), "fsdp", scatter_dimension=0, tiled=True
        ).astype(jnp.float32),
    )
    shares = (
        lax.psum(shares[0].astype(jnp.bfloat16), "ctx").astype(jnp.float32),
        lax.psum(shares[1].astype(jnp.bfloat16), "ctx").astype(jnp.float32),
        lax.psum(shares[2].astype(jnp.bfloat16), "ctx").astype(jnp.float32),
        lax.psum(shares[3].astype(jnp.bfloat16), "ctx").astype(jnp.float32),
        lax.psum(shares[4].astype(jnp.bfloat16), "ctx").astype(jnp.float32),
        lax.psum(shares[5].astype(jnp.bfloat16), "ctx").astype(jnp.float32),
        lax.psum(shares[6].astype(jnp.bfloat16), "ctx").astype(jnp.float32),
        lax.psum(shares[7].astype(jnp.bfloat16), "ctx").astype(jnp.float32),
        lax.psum(shares[8].astype(jnp.bfloat16), "ctx").astype(jnp.float32),
    )
    return (
        output,
        grad_input,
        shares[0],
        shares[1],
        shares[2],
        shares[3],
        shares[4],
        shares[5],
        shares[6],
        shares[7],
        shares[8],
    )


BF = jnp.bfloat16
F32 = jnp.float32
I32 = jnp.int32
MESH = pl.DeviceIdType.MESH
BLOCK = 256
VMEM_BYTES = 67043328
ORDER = (
    93, 92, 99, 74, 80, 121, 86, 98, 0, 95, 77, 75, 87, 83, 89, 96, 78, 104, 101, 81, 90, 79, 97, 84,
    3, 108, 6, 76, 114, 91, 85, 94, 2, 105, 127, 133, 7, 111, 8, 88, 102, 109, 82, 9, 139, 106, 120, 1,
    117, 132, 50, 123, 112, 107, 103, 115, 100, 54, 118, 144, 55, 56, 51, 113, 4, 124, 57, 126, 119, 58, 138, 110,
    10, 125, 135, 129, 136, 5, 116, 140, 12, 122, 29, 141, 28, 37, 130, 36, 137, 11, 30, 145, 38, 13, 142, 31,
    131, 39, 42, 134, 146, 14, 204, 128, 205, 40, 35, 143, 171, 147, 64, 34, 65, 66, 43, 33, 149, 161, 41, 67,
    32, 172, 15, 68, 162, 44, 46, 152, 16, 166, 59, 60, 173, 18, 206, 163, 45, 47, 61, 167, 153, 150, 52, 156,
    17, 207, 62, 208, 164, 160, 174, 63, 176, 170, 168, 19, 53, 22, 157, 21, 209, 177, 69, 48, 169, 214, 70, 218,
    210, 71, 20, 215, 158, 49, 72, 178, 211, 73, 181, 151, 159, 155, 191, 186, 182, 196, 179, 192, 165, 175, 219, 23,
    187, 212, 154, 183, 216, 200, 197, 148, 220, 213, 217, 188, 184, 201, 180, 193, 198, 221, 202, 189, 185, 194, 190, 203,
    24, 199, 195, 25, 26, 27,
)
SEMS = (48, 191, 26)


def dot_nn(left, right):
    return jnp.dot(left, right, preferred_element_type=F32)


def dot_nt(left, right):
    return lax.dot_general(left, right, (((1,), (1,)), ((), ())), preferred_element_type=F32)


def dot_tn(left, right):
    return lax.dot_general(left, right, (((0,), (0,)), ((), ())), preferred_element_type=F32)


def loop(count, body):
    def step(index, carry):
        body(index)
        return carry

    lax.fori_loop(0, count, step, 0)


def tile(index, size):
    return pl.ds(pl.multiple_of(index * size, size), size)


def only_half(values, half):
    lane = lax.broadcasted_iota(I32, values.shape, 1)
    keep = (lane < HEAD_DIM) if half == 0 else (lane >= HEAD_DIM)
    return jnp.where(keep, values, jnp.zeros_like(values))


def write_bias(bias, seg_col, seg_row, block, length):
    lanes = tile(block, BLOCK)
    keys = seg_col[0:length, :]
    key_pos = lax.broadcasted_iota(I32, (length, BLOCK), 0)
    query_pos = lax.broadcasted_iota(I32, (length, BLOCK), 1) + block * BLOCK
    same = jnp.concatenate([keys, keys], axis=1) == seg_row[0:1, lanes]
    bias[0:length, :] = jnp.where(same & (key_pos <= query_pos), 0.0, MASKED)


def attend_block(block, length, pairs, query, keys, vals_t, bias, seg_col, seg_row, mixed, mixed_t, log_sum):
    write_bias(bias, seg_col, seg_row, block, length)
    rows = tile(block, BLOCK)

    def pair(index):
        cols = tile(index, 2 * HEAD_DIM)
        two = query[rows, cols]
        for half in (0, 1):
            scores = dot_nt(keys[0:length, cols], only_half(two, half)) + bias[0:length, :]
            top = jnp.max(scores, axis=0, keepdims=True)
            expo = jnp.exp(scores - top)
            total = jnp.sum(expo, axis=0, keepdims=True)
            log_sum[2 * index + half, :, rows] = jnp.broadcast_to(top + jnp.log(total), (8, BLOCK))
            probs = (expo * (1.0 / total)).astype(BF)
            head = tile(2 * index + half, HEAD_DIM)
            mixed_t[head, :] = dot_nn(vals_t[head, 0:length], probs)

    loop(pairs, pair)
    mixed[rows, :] = mixed_t[...].T.astype(BF)


def attend_back_block(
    block, length, pairs, query, keys, keys_t, vals, grad_mixed, bias, seg_col, seg_row, log_sum, grad_qkv, grad_q_t, grad_k, grad_v
):
    write_bias(bias, seg_col, seg_row, block, length)
    rows = tile(block, BLOCK)

    def pair(index):
        cols = tile(index, 2 * HEAD_DIM)
        two = query[rows, cols]
        grad_two = grad_mixed[rows, cols]
        for half in (0, 1):
            one = only_half(two, half)
            grad_one = only_half(grad_two, half)
            scores = dot_nt(keys[0:length, cols], one) + bias[0:length, :]
            probs = jnp.exp(scores - log_sum[2 * index + half, 0:1, rows])
            grad_probs = dot_nt(vals[0:length, cols], grad_one)
            delta = jnp.sum(probs * grad_probs, axis=0, keepdims=True)
            grad_scores = (probs * (grad_probs - delta)).astype(BF)
            grad_v[0:length, cols] += dot_nn(probs.astype(BF), grad_one)
            grad_k[0:length, cols] += dot_nn(grad_scores, one)
            head = tile(2 * index + half, HEAD_DIM)
            grad_q_t[head, :] = dot_nn(keys_t[head, 0:length], grad_scores)

    loop(pairs, pair)
    grad_qkv[rows, 0 : grad_q_t.shape[0]] = (grad_q_t[...].T * SCALE).astype(BF)


def layer_kernel(
    nz,
    tok, cot, seg, gains, w_q, w_k, w_v, w_o, w_g, w_u, w_d,
    out, g_tok, o_q, o_k, o_v, o_o, o_g, o_u, o_d, o_gain,
    xg, cg, seg_row, gain_all, wqkv, wo, wg, wu, wd,
    h1, h2, ab, query, keys, vals, keys_t, vals_t, mixed, grad_mixed, grad_qkv, grad_k, grad_v,
    act_g, act_u, act_m, y1, bias, mixed_t, log_sum, seg_col,
    part, pair_sum, from_core, from_y, final_rows,
    p_d0, p_d1, p_g0, p_g1, p_u0, p_u1, p_o, p_q, p_k, p_v, r_d0, r_d1, r_g0, r_g1, r_u0, r_u1, r_o, r_q, r_k, r_v,
    s_d0, s_d1, s_g0, s_g1, s_u0, s_u1, s_o, s_q, s_k, s_v, f_d0, f_d1, f_g0, f_g1, f_u0, f_u1, f_o, f_q, f_k, f_v,
    p_n, r_n, s_n, f_n, c_n, y_n,
    send_sems, recv_sems, local_sems,
):
    fs = lax.axis_index("fsdp")
    y = lax.axis_index("ctx")
    t = lax.axis_index("tp")
    z = fs // 2
    x = lax.rem(fs, 2)
    width = xg.shape[1]
    half_len = xg.shape[0] // 2
    quarter = half_len // 2
    heads_w = query.shape[1]
    hidden = act_m.shape[1]
    db = width // (2 * nz)

    def dev(fq, yq, tq):
        return {"fsdp": fq, "ctx": yq, "tp": tq}

    x_dev = dev(2 * z + (1 - x), y, t)
    y_dev = dev(fs, 1 - y, t)
    c_dev = dev(fs, y, 1 - t)

    def z_from(k):
        return lax.rem(z + nz - k, nz)

    z_next = dev(2 * lax.rem(z + 1, nz) + x, y, t)

    barrier = pltpu.get_barrier_semaphore()
    z_prev = dev(2 * z_from(1) + x, y, t)
    for peer in (x_dev, y_dev, c_dev, z_next, z_prev):
        pl.semaphore_signal(barrier, inc=1, device_id=peer, device_id_type=MESH)
    pl.semaphore_wait(barrier, 5)

    count = {"send": 0, "recv": 0, "local": 0}
    sent = []

    def new(kind):
        count[kind] += 1
        return count[kind] - 1

    slots = [None] * SEMS[0]

    def send(src, dst, device, ridx):
        slot = new("send") % SEMS[0]
        if slots[slot] is not None:
            drain([copy for copy in sent if copy is slots[slot]])
        copy = pltpu.make_async_remote_copy(
            src, dst, send_sems.at[slot], recv_sems.at[ridx], device_id=device, device_id_type=MESH
        )
        slots[slot] = copy
        copy.start()
        sent.append(copy)
        return copy

    def recv(dst, ridx):
        pltpu.make_async_remote_copy(
            dst, dst, send_sems.at[0], recv_sems.at[ridx], device_id=y_dev, device_id_type=MESH
        ).wait_recv()

    def local(src, dst):
        copy = pltpu.make_async_copy(src, dst, local_sems.at[new("local")])
        copy.start()
        return copy

    def many(number):
        return [new("recv") for _ in range(number)]

    def drain(copies):
        left = [copy for copy in sent if any(copy is other for other in copies)]
        for copy in left:
            copy.wait_send()
        sent[:] = [copy for copy in sent if not any(copy is other for other in left)]

    hw = pl.ds(pl.multiple_of(y * heads_w, heads_w), heads_w)

    def rb(fq):
        return tile(fq, db)

    part_h = hidden // 2
    first, second = slice(0, part_h), slice(part_h, hidden)

    def half_of(half, yq):
        return pl.ds(pl.multiple_of(yq * hidden + half * part_h, part_h), part_h)

    names = {
        "n": (gains, lambda fq: gain_all.at[fq], False),
        "q": (w_q.at[:, hw], lambda fq: wqkv.at[rb(fq), 0:heads_w], False),
        "k": (w_k.at[:, hw], lambda fq: wqkv.at[rb(fq), heads_w : 2 * heads_w], False),
        "v": (w_v.at[:, hw], lambda fq: wqkv.at[rb(fq), 2 * heads_w : 3 * heads_w], False),
        "o": (w_o.at[hw, :], lambda fq: wo.at[:, rb(fq)], True),
    }
    for i, units in enumerate((first, second)):
        mine = half_of(i, y)
        names[f"g{i}"] = (w_g.at[:, mine], lambda fq, units=units: wg.at[rb(fq), units], False)
        names[f"u{i}"] = (w_u.at[:, mine], lambda fq, units=units: wu.at[rb(fq), units], False)
        names[f"d{i}"] = (w_d.at[mine, :], lambda fq, units=units: wd.at[units, rb(fq)], i == 1)
    ring_own = {name: [None] + many(nz - 1) for name in names}
    ring_other = {name: [None] + many(nz - 1) for name in names if names[name][2]}
    over_x = {name: many(1 if names[name][2] else nz) for name in names}
    own_copy = {}

    def start_z(name):
        src, place, _ = names[name]
        own_copy[name] = local(src, place(fs))
        send(src, place(fs), z_next, ring_own[name][1])

    def start_x(name):
        src, place, _ = names[name]
        send(src, place(fs), x_dev, over_x[name][0])

    def relay(name, k):
        place, pair_first = names[name][1:]
        block = place(2 * z_from(k) + x)
        recv(block, ring_own[name][k])
        if k < nz - 1:
            send(block, block, z_next, ring_own[name][k + 1])
        if not pair_first:
            send(block, block, x_dev, over_x[name][k])

    def relay_other(name, k):
        block = names[name][1](2 * z_from(k) + (1 - x))
        recv(block, over_x[name][0] if k == 0 else ring_other[name][k])
        if k < nz - 1:
            send(block, block, z_next, ring_other[name][k + 1])

    def arrived(name):
        place, pair_first = names[name][1:]
        own_copy[name].wait()
        if not pair_first:
            for k in range(nz):
                recv(place(2 * z_from(k) + (1 - x)), over_x[name][k])

    def rows_of(yq, tq):
        return pl.ds(pl.multiple_of(yq * half_len + tq * quarter, quarter), quarter)

    own_rows = rows_of(y, t)

    tok_y, tok_c, cot_y, cot_c, seg_y = many(5)
    seg_local = local(seg, seg_row.at[:, tile(y, half_len)])
    send(seg, seg_row.at[:, tile(y, half_len)], y_dev, seg_y)
    tok_local = local(tok, xg.at[tile(y, half_len), :])
    cot_local = local(cot, cg.at[tile(y, half_len), :])

    far = rows_of(1 - y, t)
    far_other = rows_of(1 - y, 1 - t)

    def core_forward(ref, y_idx, c_idx):
        recv(ref.at[far, :], y_idx)
        return send(ref.at[far, :], ref.at[far, :], c_dev, c_idx)

    kinds = {"a": 0, "out": 1, "dh2": 2, "dh1": 3}
    ex_recv = {name: many(3) for name in kinds}
    ex_sent = []

    def exchange(name, compute, stage):
        e = kinds[name]
        if stage == 0:
            drain(ex_sent)
            ex_sent.clear()
            compute(far_other, part.at[0])
            ex_sent.append(send(part.at[0], from_core.at[e, 0], c_dev, ex_recv[name][0]))
        elif stage == 1:
            compute(far, part.at[1])
        elif stage == 2:
            recv(from_core.at[e, 0], ex_recv[name][0])

            def add(i):
                r = tile(i, 32)
                pair_sum[r, :] = (part[1, r, :].astype(F32) + from_core[e, 0, r, :].astype(F32)).astype(BF)

            loop(quarter // 32, add)
            ex_sent.append(send(pair_sum, from_y.at[e], y_dev, ex_recv[name][2]))
        elif stage == 3:
            compute(rows_of(y, 1 - t), part.at[2])
            ex_sent.append(send(part.at[2], from_core.at[e, 1], c_dev, ex_recv[name][1]))
        elif stage == 4:
            compute(own_rows, part.at[3])
        else:
            recv(from_core.at[e, 1], ex_recv[name][1])
            recv(from_y.at[e], ex_recv[name][2])

    def total_of(name, r):
        e = kinds[name]
        return part[3, r, :].astype(F32) + from_core[e, 1, r, :].astype(F32) + from_y[e, r, :].astype(F32)

    def spread_rows(ref, idx):
        return [
            send(ref.at[own_rows, :], ref.at[own_rows, :], c_dev, idx[0]),
            send(ref.at[own_rows, :], ref.at[own_rows, :], y_dev, idx[1]),
        ]

    h2_idx = many(3)
    ab_idx = many(3)

    grads = {
        "d0": (p_d0, r_d0, s_d0, f_d0, True),
        "d1": (p_d1, r_d1, s_d1, f_d1, False),
        "g0": (p_g0, r_g0, s_g0, f_g0, False),
        "g1": (p_g1, r_g1, s_g1, f_g1, False),
        "u0": (p_u0, r_u0, s_u0, f_u0, False),
        "u1": (p_u1, r_u1, s_u1, f_u1, False),
        "o": (p_o, r_o, s_o, f_o, False),
        "q": (p_q, r_q, s_q, f_q, False),
        "k": (p_k, r_k, s_k, f_k, False),
        "v": (p_v, r_v, s_v, f_v, False),
        "n": (p_n, r_n, s_n, f_n, False),
    }
    gx = {name: [None] + many(1 if item[4] else nz) for name, item in grads.items()}
    gz = {name: [[None] + many(nz - 1) for _ in range(2 if item[4] else 1)] for name, item in grads.items()}

    def add_rows(rows, cols, body):
        step = min(rows, 16 if cols > 512 else 128)
        loop(rows // step, lambda i: body(tile(i, step)))

    def grad_send(name, k):
        p, r, s, _, ring_first = grads[name]
        if ring_first:
            send(p.at[lax.rem(x + k, 2), z_from(1)], s.at[k - 1, 0], z_next, gz[name][k - 1][1])
        else:
            send(p.at[1 - x, z_from(k)], r.at[k - 1], x_dev, gx[name][k])

    def grad_step(name, k):
        p, r, s, f, ring_first = grads[name]
        if ring_first:
            c, k = divmod(k, 10)
            xq = lax.rem(x + 1 + c, 2)
            recv(s.at[c, k - 2], gz[name][c][k - 1])
            last_own = k == nz and c == 1
            if last_own:
                recv(r.at[0], gx[name][1])

            def add_ring(rr):
                total = p[xq, z_from(k), rr, :].astype(F32) + s[c, k - 2, rr, :].astype(F32)
                if last_own:
                    f[rr, :] = (total + r[0, rr, :].astype(F32)).astype(f.dtype)
                else:
                    p[xq, z_from(k), rr, :] = total.astype(p.dtype)

            add_rows(*p.shape[2:], add_ring)
            if k < nz:
                send(p.at[xq, z_from(k)], s.at[c, k - 1], z_next, gz[name][c][k])
            elif c == 0:
                send(p.at[xq, z_from(k)], r.at[0], x_dev, gx[name][1])
            return
        zq = z_from(k)
        recv(r.at[k - 1], gx[name][k])
        if k > 1:
            recv(s.at[0, k - 2], gz[name][0][k - 1])

        def add(rr):
            total = p[x, zq, rr, :].astype(F32) + r[k - 1, rr, :].astype(F32)
            if k > 1:
                total = total + s[0, k - 2, rr, :].astype(F32)
            if k < nz:
                p[x, zq, rr, :] = total.astype(p.dtype)
            else:
                f[rr, :] = total.astype(f.dtype)

        add_rows(*p.shape[2:], add)
        if k < nz:
            send(p.at[x, zq], s.at[0, k - 1], z_next, gz[name][0][k])

    def place_of(name, yq):
        h = pl.ds(pl.multiple_of(yq * heads_w, heads_w), heads_w)
        if name[0] == "d":
            return o_d.at[half_of(int(name[1]), yq), :]
        if name == "o":
            return o_o.at[h, :]
        wide = {"g": o_g, "u": o_u}
        if name[0] in wide:
            return wide[name[0]].at[:, half_of(int(name[1]), yq)]
        return {"q": o_q, "k": o_k, "v": o_v}[name].at[:, h]

    out_idx = {name: many(1)[0] for name in grads if name != "n"}
    last_local = []

    def grad_end(name):
        f = grads[name][3]
        last_local.append(local(f, place_of(name, y)))
        send(f, place_of(name, y), y_dev, out_idx[name])

    def grad_done(name):
        recv(place_of(name, 1 - y), out_idx[name])

    value = {}
    blocks = half_len // BLOCK
    pairs = heads_w // (2 * HEAD_DIM)
    out_c, gtok_c = many(2)
    n_c, n_y = many(2)
    my_rows = tile(t, quarter)
    other_rows = tile(1 - t, quarter)
    row_sends = []

    def send_tok():
        send(tok.at[tile(t, quarter), :], xg.at[own_rows, :], y_dev, tok_y)

    def send_cot():
        send(cot.at[tile(t, quarter), :], cg.at[own_rows, :], y_dev, cot_y)

    def gather_gains():
        value["one"] = jnp.concatenate([gain_all[i, 0:1, :] for i in range(2 * nz)], axis=1)
        value["two"] = jnp.concatenate([gain_all[i, 1:2, :] for i in range(2 * nz)], axis=1)

    def norm_rows(start):
        gain_one = value["one"]

        def body(i):
            r = pl.ds(pl.multiple_of(start + i * 32, 32), 32)
            values = xg[r, :].astype(F32)
            inverse = lax.rsqrt(jnp.mean(values * values, axis=-1, keepdims=True) + EPSILON)
            h1[r, :] = (values * inverse * gain_one).astype(BF)

        loop(half_len // 32, body)

    def norm_own():
        tok_local.wait()
        norm_rows(y * half_len)

    def norm_far():
        recv(xg.at[far_other, :], tok_c)
        norm_rows((1 - y) * half_len)

    def segments():
        seg_local.wait()
        recv(seg_row.at[:, tile(1 - y, half_len)], seg_y)
        seg_col[...] = jnp.broadcast_to(seg_row[0:1, :], (128, 2 * half_len)).T

    def project():
        def body(i):
            r = tile(i, 512)
            rows = h1[r, :]
            query[r, :] = (dot_nn(rows, wqkv[:, 0:heads_w]).astype(BF).astype(F32) * SCALE).astype(BF)
            keys[r, :] = dot_nn(rows, wqkv[:, heads_w : 2 * heads_w]).astype(BF)
            vals[r, :] = dot_nn(rows, wqkv[:, 2 * heads_w : 3 * heads_w]).astype(BF)

        loop(xg.shape[0] // 512, body)
        keys_t[...] = keys[...].T
        vals_t[...] = vals[...].T

    def either(half, body):
        @pl.when(half == 0)
        def _():
            body(half_len)

        @pl.when(half == 1)
        def _():
            body(2 * half_len)

    def attend(half):
        def block(i):
            args = (pairs, query, keys, vals_t, bias, seg_col, seg_row, mixed, mixed_t, log_sum)
            either(half, lambda length: attend_block(half * blocks + i, length, *args))

        loop(blocks, block)

    def out_rows(r, dst):
        dst[...] = dot_nn(mixed[r, :], wo[...]).astype(BF)

    def first_residual():
        exchange("a", None, 5)
        gain_two = value["two"]

        def body(i):
            r = tile(i, 32)
            rr = pl.ds(pl.multiple_of(y * half_len + t * quarter + i * 32, 32), 32)
            values = xg[rr, :].astype(F32) + total_of("a", r)
            y1[r, :] = values
            inverse = lax.rsqrt(jnp.mean(values * values, axis=-1, keepdims=True) + EPSILON)
            h2[rr, :] = (values * inverse * gain_two).astype(BF)

        loop(quarter // 32, body)
        row_sends.extend(spread_rows(h2, h2_idx))

    def gate(half, r):
        rows = h2[r, :]

        def cols(j):
            c = pl.ds(pl.multiple_of(half * part_h + j * 256, 256), 256)
            g = dot_nn(rows, wg[:, c])
            u = dot_nn(rows, wu[:, c])
            sg = 1.0 / (1.0 + jnp.exp(-g))
            gs = g * sg
            act_u[r, c] = gs.astype(BF)
            act_g[r, c] = (u * sg * (1.0 + g * (1.0 - sg))).astype(BF)
            act_m[r, c] = (gs * u).astype(BF)

        loop(part_h // 256, cols)

    def grad_cols(left, start, right, p, index):
        c = tile(index, 2 * db)
        for i in range(p.shape[2] // 256):
            r = slice(start + i * 256, start + (i + 1) * 256)
            both = dot_tn(left[:, r], right[:, c]).astype(BF)
            rows = slice(i * 256, (i + 1) * 256)
            p[0, index, rows, :] = both[:, 0:db]
            p[1, index, rows, :] = both[:, db : 2 * db]

    def grad_rows(left, right, units, p, index):
        c = tile(index, 2 * db)
        both = dot_tn(left[:, c], right[:, units]).astype(BF)
        p[0, index] = both[0:db, :]
        p[1, index] = both[db : 2 * db, :]

    def grad_down(part_of, p):
        loop(nz, lambda i: grad_cols(act_m, part_of * part_h, cg, p, i))

    def some_blocks(name, left, right, units, ks):
        p = grads[name][0]
        loop(len(ks), lambda i: grad_rows(left, right, units, p, z_from(ks[0] + i)))
        for k in ks:
            grad_send(name, k)

    def qkv_blocks(ks):
        def body(i):
            index = z_from(ks[0] + i)
            both = dot_tn(h1[:, tile(index, 2 * db)], grad_qkv[...]).astype(BF)
            for j, p in enumerate((p_q, p_k, p_v)):
                c = slice(j * heads_w, (j + 1) * heads_w)
                p[0, index] = both[0:db, c]
                p[1, index] = both[db : 2 * db, c]

        loop(len(ks), body)

    def hidden_back(half, r, dst):
        rows = cg[r, :]
        units = (first, second)[half]

        def cols(j):
            c = pl.ds(pl.multiple_of(half * part_h + j * 256, 256), 256)
            dm = dot_nt(rows, wd[c, :])
            act_g[r, c] = (dm * act_g[r, c].astype(F32)).astype(BF)
            act_u[r, c] = (dm * act_u[r, c].astype(F32)).astype(BF)

        loop(part_h // 256, cols)

        def back(j):
            c = tile(j, 512)
            total = dot_nt(act_g[r, units], wg[c, units]) + dot_nt(act_u[r, units], wu[c, units])
            if half == 0:
                ab[r, c] = total.astype(BF)
            else:
                dst[:, c] = (total + ab[r, c].astype(F32)).astype(BF)

        loop(width // 512, back)

    def second_residual():
        exchange("dh2", None, 5)
        gain_two = value["two"]

        def body(i, carry):
            r = tile(i, 32)
            rr = pl.ds(pl.multiple_of(y * half_len + t * quarter + i * 32, 32), 32)
            values = y1[r, :]
            inverse = lax.rsqrt(jnp.mean(values * values, axis=-1, keepdims=True) + EPSILON)
            normed = values * inverse
            grad = total_of("dh2", r)
            scaled = grad * gain_two
            mean = jnp.mean(scaled * normed, axis=-1, keepdims=True)
            full = cg[rr, :].astype(F32) + inverse * (scaled - normed * mean)
            final_rows[r, :] = full
            ab[rr, :] = full.astype(BF)
            return carry + jnp.sum(grad * normed, axis=0, keepdims=True)

        value["grad_two"] = lax.fori_loop(0, quarter // 32, body, jnp.zeros((1, width), F32))
        row_sends.extend(spread_rows(ab, ab_idx))

    def down_rows(r, dst):
        def cols(j):
            c = tile(j, 512)
            dst[:, c] = dot_nn(act_m[r, :], wd[:, c]).astype(BF)

        loop(width // 512, cols)

    def mixed_back(half):
        r = tile(half, half_len)
        grad_mixed[r, :] = dot_nt(ab[r, :], wo[...]).astype(BF)

    def clear_sums():
        grad_k[...] = jnp.zeros_like(grad_k)
        grad_v[...] = jnp.zeros_like(grad_v)

    def attend_back(half):
        def block(i):
            args = (
                pairs, query, keys, keys_t, vals, grad_mixed, bias, seg_col, seg_row, log_sum, grad_qkv, mixed_t, grad_k, grad_v,
            )
            either(half, lambda length: attend_back_block(half * blocks + i, length, *args))

        loop(blocks, block)

    def own_back():
        recv(ab.at[rows_of(y, 1 - t), :], ab_idx[0])
        clear_sums()
        mixed_back(y)

    def far_back():
        recv(ab.at[far_other, :], ab_idx[2])
        mixed_back(1 - y)

    def grad_out_all():
        loop(nz, lambda i: grad_cols(mixed, 0, ab, p_o, i))
        for k in range(1, nz + 1):
            grad_send("o", k)

    def sums_to_bf16():
        grad_qkv[:, heads_w : 2 * heads_w] = grad_k[...].astype(BF)
        grad_qkv[:, 2 * heads_w : 3 * heads_w] = grad_v[...].astype(BF)

    def hidden_one_back(r, dst):
        def cols(j):
            c = tile(j, 512)
            dst[:, c] = dot_nt(grad_qkv[r, :], wqkv[c, :]).astype(BF)

        loop(width // 512, cols)

    def finish_out():
        exchange("out", None, 5)

        def body(i):
            r = tile(i, 32)
            act_m[r, 0:width] = (y1[r, :] + total_of("out", r)).astype(BF)

        loop(quarter // 32, body)
        last_local.append(local(act_m.at[0:quarter, 0:width], out.at[my_rows, :]))
        send(act_m.at[0:quarter, 0:width], out.at[my_rows, :], c_dev, out_c)

    def finish_tokens():
        exchange("dh1", None, 5)
        drain(row_sends)
        gain_one = value["one"]

        def body(i, carry):
            r = tile(i, 32)
            rr = pl.ds(pl.multiple_of(y * half_len + t * quarter + i * 32, 32), 32)
            values = xg[rr, :].astype(F32)
            inverse = lax.rsqrt(jnp.mean(values * values, axis=-1, keepdims=True) + EPSILON)
            normed = values * inverse
            grad = total_of("dh1", r)
            scaled = grad * gain_one
            mean = jnp.mean(scaled * normed, axis=-1, keepdims=True)
            full = final_rows[r, :] + inverse * (scaled - normed * mean)
            h2[r, :] = full.astype(BF)
            return carry + jnp.sum(grad * normed, axis=0, keepdims=True)

        gain_one_grad = lax.fori_loop(0, quarter // 32, body, jnp.zeros((1, width), F32))
        for i in range(2 * nz):
            c = slice(i * db, (i + 1) * db)
            p_n[i % 2, i // 2] = jnp.concatenate(
                [gain_one_grad[:, c], value["grad_two"][:, c], jnp.zeros((6, db), F32)], axis=0
            )
        for k in range(1, nz + 1):
            grad_send("n", k)
        last_local.append(local(h2.at[0:quarter, :], g_tok.at[my_rows, :]))
        send(h2.at[0:quarter, :], g_tok.at[my_rows, :], c_dev, gtok_c)

    def gains_core():
        send(f_n, c_n, c_dev, n_c)

    def gains_y():
        recv(c_n, n_c)
        y_n[0] = f_n[...] + c_n[...]
        send(y_n.at[0], y_n.at[1], y_dev, n_y)

    def gains_end():
        recv(y_n.at[1], n_y)
        o_gain[...] = y_n[0] + y_n[1]

    def finish():
        for name in out_idx:
            grad_done(name)
        recv(out.at[other_rows, :], out_c)
        recv(g_tok.at[other_rows, :], gtok_c)
        for copy in last_local:
            copy.wait()
        drain(list(sent))

    two = (1, 2), (3, 4)
    tasks = [
        send_tok,
        send_cot,
        gather_gains,
        lambda: core_forward(xg, tok_y, tok_c),
        lambda: core_forward(cg, cot_y, cot_c),
        lambda: (cot_local.wait(), recv(cg.at[far_other, :], cot_c)),
        segments,
        norm_own,
        norm_far,
        project,
        first_residual,
        lambda: row_sends.append(core_forward(h2, h2_idx[1], h2_idx[2])),
        lambda: recv(h2.at[rows_of(y, 1 - t), :], h2_idx[0]),
        lambda: recv(h2.at[far_other, :], h2_idx[2]),
        lambda: grad_down(0, p_d0),
        lambda: grad_down(1, p_d1),
        second_residual,
        lambda: row_sends.append(core_forward(ab, ab_idx[1], ab_idx[2])),
        own_back,
        far_back,
        grad_out_all,
        sums_to_bf16,
        finish_out,
        finish_tokens,
        gains_core,
        gains_y,
        gains_end,
        finish,
    ]
    all_rows = (own_rows, rows_of(y, 1 - t), far, far_other)
    tasks += [functools.partial(gate, half, r) for half in (0, 1) for r in all_rows]
    tasks += [functools.partial(hidden_back, 0, r, None) for r in all_rows]
    for i, units in enumerate((first, second)):
        tasks += [functools.partial(some_blocks, f"g{i}", h2, act_g, units, ks) for ks in two]
        tasks += [functools.partial(some_blocks, f"u{i}", h2, act_u, units, ks) for ks in two]
    tasks += [functools.partial(qkv_blocks, ks) for ks in two]
    tasks += [functools.partial(attend, half) for half in (1 - y, y)]
    tasks += [functools.partial(attend_back, half) for half in (y, 1 - y)]
    for name, compute in zip(kinds, (out_rows, down_rows, functools.partial(hidden_back, 1), hidden_one_back)):
        tasks += [functools.partial(exchange, name, compute, i) for i in range(5)]
    for name in names:
        tasks += [functools.partial(start_z, name), functools.partial(start_x, name), functools.partial(arrived, name)]
        tasks += [functools.partial(relay, name, k) for k in range(1, nz)]
        if names[name][2]:
            tasks += [functools.partial(relay_other, name, k) for k in range(nz)]
    for name in grads:
        if name in out_idx:
            tasks.append(functools.partial(grad_end, name))
        if grads[name][4]:
            tasks += [functools.partial(grad_step, name, 10 * c + k) for c in (0, 1) for k in range(2, nz + 1)]
        else:
            tasks += [functools.partial(grad_step, name, k) for k in range(1, nz + 1)]
    for name in ("d0", "d1", "q", "k", "v"):
        tasks += [functools.partial(grad_send, name, k) for k in ((1, 2) if grads[name][4] else range(1, nz + 1))]
    assert sorted(ORDER) == list(range(len(tasks)))
    for index in ORDER:
        tasks[index]()


def fused(nz, tokens, segment_ids, w_query, w_key, w_value, w_out, w_gate, w_up, w_down, gain_attn, gain_ffn, cotangent):
    half_len, _, width = tokens.shape
    length = 2 * half_len
    quarter = half_len // 2
    heads_w = w_query.shape[1] // 2
    hidden = w_gate.shape[1] // 2
    db = w_query.shape[0]
    heads = heads_w // HEAD_DIM
    gains = jnp.stack([gain_attn, gain_ffn]).astype(F32)

    def vm(*shape, dtype=BF):
        return pltpu.VMEM(shape, dtype)

    shape_d, shape_g, shape_o, shape_q = (hidden // 2, db), (db, hidden // 2), (heads_w, db), (db, heads_w)
    shapes = (shape_d, shape_d, *[shape_g] * 4, shape_o, shape_q, shape_q, shape_q)
    ring_first = (True, *[False] * 9)
    scratch = [
        vm(length, width), vm(length, width), vm(1, length, dtype=I32), vm(2 * nz, 2, db, dtype=F32),
        vm(width, 3 * heads_w), vm(heads_w, width), vm(width, hidden), vm(width, hidden), vm(hidden, width),
        vm(length, width), vm(length, width), vm(length, width),
        vm(length, heads_w), vm(length, heads_w), vm(length, heads_w), vm(heads_w, length), vm(heads_w, length),
        vm(length, heads_w), vm(length, heads_w), vm(length, 3 * heads_w),
        vm(length, heads_w, dtype=F32), vm(length, heads_w, dtype=F32),
        vm(length, hidden), vm(length, hidden), vm(length, hidden),
        vm(quarter, width, dtype=F32), vm(length, BLOCK, dtype=F32), vm(heads_w, BLOCK, dtype=F32),
        vm(heads, 8, length, dtype=F32), vm(length, 128, dtype=I32),
        vm(4, quarter, width), vm(quarter, width), vm(4, 2, quarter, width), vm(4, quarter, width),
        vm(quarter, width, dtype=F32),
    ]
    scratch += [vm(2, nz, *shape) for shape in shapes]
    scratch += [vm(1 if first else nz, *shape) for shape, first in zip(shapes, ring_first)]
    scratch += [vm(2 if first else 1, nz - 1, *shape) for shape, first in zip(shapes, ring_first)]
    scratch += [vm(*shape) for shape in shapes]
    scratch += [
        vm(2, nz, 8, db, dtype=F32), vm(nz, 8, db, dtype=F32), vm(1, nz - 1, 8, db, dtype=F32), vm(8, db, dtype=F32),
        vm(8, db, dtype=F32), vm(2, 8, db, dtype=F32),
    ]
    scratch += [pltpu.SemaphoreType.DMA((SEMS[0],)), pltpu.SemaphoreType.DMA((SEMS[1],)), pltpu.SemaphoreType.DMA((SEMS[2],))]
    anywhere = pl.BlockSpec(memory_space=pl.ANY)
    weights = (w_query, w_key, w_value, w_out, w_gate, w_up, w_down)
    results = pl.pallas_call(
        functools.partial(layer_kernel, nz),
        out_shape=[jax.ShapeDtypeStruct((half_len, width), BF)] * 2
        + [jax.ShapeDtypeStruct(item.shape, BF) for item in weights]
        + [jax.ShapeDtypeStruct((8, db), F32)],
        in_specs=[anywhere] * 11,
        out_specs=[anywhere] * 9 + [pl.BlockSpec(memory_space=pltpu.VMEM)],
        scratch_shapes=scratch,
        compiler_params=pltpu.CompilerParams(
            collective_id=0, has_side_effects=True, vmem_limit_bytes=VMEM_BYTES
        ),
        name="layer",
    )(tokens.reshape(half_len, width), cotangent.reshape(half_len, width), segment_ids, gains, *weights)
    bodies = results[:9]
    wide = [jax.ShapeDtypeStruct(item.shape, BF if i < 2 else F32) for i, item in enumerate(bodies)]

    def widen(*refs):
        srcs, rows, dsts, (one, two), held = refs[:9], refs[9], refs[10:19], refs[19:21], refs[21:30]
        finals, (load_sems, store_sems) = refs[30:37], refs[37:]
        order = [*range(6, 9), *range(2, 6), 0, 1]
        loads = {i: pltpu.make_async_copy(srcs[i], held[i], load_sems.at[i]) for i in order}
        for i in order:
            loads[i].start()
        one[...] = rows[0:1, :]
        two[...] = rows[1:2, :]
        stores = []
        for i in order:
            loads[i].wait()
            if i >= 2:
                finals[i - 2][...] = held[i][...].astype(F32)
            stores.append(pltpu.make_async_copy(finals[i - 2] if i >= 2 else held[i], dsts[i], store_sems.at[i]))
            stores[-1].start()
        for copy in stores:
            copy.wait()

    inside = pl.BlockSpec(memory_space=pltpu.VMEM)
    finals = pl.pallas_call(
        widen,
        out_shape=wide + [jax.ShapeDtypeStruct((1, db), F32)] * 2,
        in_specs=[anywhere] * 9 + [inside],
        out_specs=[anywhere] * 9 + [inside] * 2,
        scratch_shapes=[vm(*item.shape) for item in bodies]
        + [vm(*item.shape, dtype=F32) for item in wide[2:]]
        + [pltpu.SemaphoreType.DMA((9,)), pltpu.SemaphoreType.DMA((9,))],
        compiler_params=pltpu.CompilerParams(vmem_limit_bytes=VMEM_BYTES),
        name="widen",
    )(*results)
    shape = tokens.shape
    return (finals[0].reshape(shape), finals[1].reshape(shape), *finals[2:9], finals[9].reshape(db), finals[10].reshape(db))


def fits(mesh, tokens_shape):
    return mesh.shape["fsdp"] == 8 and mesh.shape["ctx"] == 2 and mesh.shape["tp"] == 2 and tokens_shape[1:] == (1, 1024)


def solution(mesh):
    def step(tokens, *rest):
        if fits(mesh, tokens.shape):
            return fused(mesh.shape["fsdp"] // 2, tokens, *rest)
        return local(tokens, *rest)

    return jax.shard_map(
        step,
        mesh=mesh,
        in_specs=(
            P("ctx", "fsdp", None),
            P("fsdp", "ctx"),
            P("fsdp", "tp"),
            P("fsdp", "tp"),
            P("fsdp", "tp"),
            P("tp", "fsdp"),
            P("fsdp", "tp"),
            P("fsdp", "tp"),
            P("tp", "fsdp"),
            P("fsdp"),
            P("fsdp"),
            P("ctx", "fsdp", None),
        ),
        out_specs=(
            P("ctx", "fsdp", None),
            P("ctx", "fsdp", None),
            P("fsdp", "tp"),
            P("fsdp", "tp"),
            P("fsdp", "tp"),
            P("tp", "fsdp"),
            P("fsdp", "tp"),
            P("fsdp", "tp"),
            P("tp", "fsdp"),
            P("fsdp"),
            P("fsdp"),
        ),
        check_vma=False,
    )
```

```python
import functools

import jax
import jax.numpy as jnp
from jax import lax
from jax.experimental import pallas as pl
from jax.experimental.pallas import tpu as pltpu
from jax.sharding import PartitionSpec as P

HEAD_DIM = 64


EPSILON = 1e-05
SCALE = 0.125
MASKED = -1e30


def normalize(values):
    inverse = lax.rsqrt(jnp.mean(values * values, axis=-1, keepdims=True) + EPSILON)
    return (values * inverse, inverse)


def norm_back(grad_normed, normed, inverse):
    return inverse * (grad_normed - normed * jnp.mean(grad_normed * normed, axis=-1, keepdims=True))


def inner_rows(left, right):
    return lax.dot_general(
        left, right, (((0,), (0,)), ((), ())), preferred_element_type=jnp.float32
    )


def times_transposed(left, weight):
    return lax.dot_general(
        left, weight, (((1,), (1,)), ((), ())), preferred_element_type=jnp.float32
    )


def head_sum(partial_sum):
    return lax.psum(partial_sum, "tp")


def split_heads(values, head_size):
    length, sequences, width = values.shape
    return jnp.moveaxis(values.reshape(length, sequences, width // head_size, head_size), 2, 0)


def join_heads(values):
    heads, length, sequences, head_size = values.shape
    return jnp.moveaxis(values, 0, 2).reshape(length, sequences, heads * head_size)


def make_mask(query_pos, query_seg, key_pos, key_seg):
    before = key_pos[None, None, :] <= query_pos[None, :, None]
    same = query_seg.T[:, :, None] == key_seg.T[:, None, :]
    return before & same


def key_head_grads(parts, use_mask):
    q_head, k_head, v_head, d_head, log_total, delta = parts
    scores = jnp.einsum("qsd,ksd->sqk", q_head, k_head, preferred_element_type=jnp.float32) * SCALE
    probs = jnp.exp(jnp.where(use_mask, scores, MASKED) - log_total)
    grad_probs = jnp.einsum("qsd,ksd->sqk", d_head, v_head, preferred_element_type=jnp.float32)
    grad_scores = (probs * (grad_probs - delta)).astype(jnp.bfloat16)
    grad_v = jnp.einsum(
        "sqk,qsd->ksd", probs.astype(jnp.bfloat16), d_head, preferred_element_type=jnp.float32
    )
    grad_k = (
        jnp.einsum("sqk,qsd->ksd", grad_scores, q_head, preferred_element_type=jnp.float32) * SCALE
    )
    return (grad_k, grad_v)


def local(
    tokens,
    segment_ids,
    w_query,
    w_key,
    w_value,
    w_out,
    w_gate,
    w_up,
    w_down,
    gain_attn,
    gain_ffn,
    cotangent,
):
    local_len, sequences, width = tokens.shape
    rows = local_len * sequences
    (
        full_query,
        full_key,
        full_value,
        full_out,
        full_gate,
        full_up,
        full_down,
        full_gain_one,
        full_gain_two,
    ) = (
        lax.all_gather(w_query, "fsdp", axis=0, tiled=True),
        lax.all_gather(w_key, "fsdp", axis=0, tiled=True),
        lax.all_gather(w_value, "fsdp", axis=0, tiled=True),
        lax.all_gather(w_out, "fsdp", axis=1, tiled=True),
        lax.all_gather(w_gate, "fsdp", axis=0, tiled=True),
        lax.all_gather(w_up, "fsdp", axis=0, tiled=True),
        lax.all_gather(w_down, "fsdp", axis=1, tiled=True),
        lax.all_gather(gain_attn, "fsdp", axis=0, tiled=True),
        lax.all_gather(gain_ffn, "fsdp", axis=0, tiled=True),
    )
    gain_one = full_gain_one.astype(jnp.float32)
    gain_two = full_gain_two.astype(jnp.float32)
    head_width = full_query.shape[1]
    flat = tokens.astype(jnp.float32).reshape(rows, width)
    normed_one, inverse_one = normalize(flat)
    hidden_one = (normed_one * gain_one).astype(jnp.bfloat16)
    query = (
        jnp.dot(hidden_one, full_query, preferred_element_type=jnp.float32)
        .astype(jnp.bfloat16)
        .reshape(local_len, sequences, head_width)
    )
    keys = (
        jnp.dot(hidden_one, full_key, preferred_element_type=jnp.float32)
        .astype(jnp.bfloat16)
        .reshape(local_len, sequences, head_width)
    )
    vals = (
        jnp.dot(hidden_one, full_value, preferred_element_type=jnp.float32)
        .astype(jnp.bfloat16)
        .reshape(local_len, sequences, head_width)
    )
    pair = jnp.concatenate([keys, vals], axis=-1)
    seg_local = segment_ids.T
    pair_all, seg_all = (
        lax.all_gather(pair, "ctx", axis=0, tiled=True),
        lax.all_gather(seg_local, "ctx", axis=0, tiled=True),
    )
    length = pair_all.shape[0]
    query_pos = lax.axis_index("ctx") * local_len + jnp.arange(local_len, dtype=jnp.int32)
    all_pos = jnp.arange(length, dtype=jnp.int32)
    mask = make_mask(query_pos, seg_local, all_pos, seg_all)
    q_heads = split_heads(query, HEAD_DIM)
    k_heads = split_heads(pair_all[..., :head_width], HEAD_DIM)
    v_heads = split_heads(pair_all[..., head_width:], HEAD_DIM)

    def attend(parts):
        q_head, k_head, v_head = parts
        scores = (
            jnp.einsum("qsd,ksd->sqk", q_head, k_head, preferred_element_type=jnp.float32) * SCALE
        )
        scores = jnp.where(mask, scores, MASKED)
        row_max = jnp.max(scores, axis=-1, keepdims=True)
        log_total = row_max + jnp.log(jnp.sum(jnp.exp(scores - row_max), axis=-1, keepdims=True))
        probs = jnp.exp(scores - log_total).astype(jnp.bfloat16)
        return (
            jnp.einsum("sqk,ksd->qsd", probs, v_head, preferred_element_type=jnp.float32),
            log_total,
        )

    attended, log_totals = lax.map(attend, (q_heads, k_heads, v_heads))
    mixed = join_heads(attended).astype(jnp.bfloat16).reshape(rows, head_width)
    resid = flat + head_sum(jnp.dot(mixed, full_out, preferred_element_type=jnp.float32))
    normed_two, inverse_two = normalize(resid)
    hidden_two = (normed_two * gain_two).astype(jnp.bfloat16)
    gate = jnp.dot(hidden_two, full_gate, preferred_element_type=jnp.float32)
    upward = jnp.dot(hidden_two, full_up, preferred_element_type=jnp.float32)
    sigmoid_gate = jax.nn.sigmoid(gate)
    swish_up = (gate * sigmoid_gate * upward).astype(jnp.bfloat16)
    result = resid + head_sum(jnp.dot(swish_up, full_down, preferred_element_type=jnp.float32))
    output = result.astype(jnp.bfloat16).reshape(local_len, sequences, width)
    (
        full_query,
        full_key,
        full_value,
        full_out,
        full_gate,
        full_up,
        full_down,
        full_gain_one,
        full_gain_two,
    ) = (
        lax.all_gather(w_query, "fsdp", axis=0, tiled=True),
        lax.all_gather(w_key, "fsdp", axis=0, tiled=True),
        lax.all_gather(w_value, "fsdp", axis=0, tiled=True),
        lax.all_gather(w_out, "fsdp", axis=1, tiled=True),
        lax.all_gather(w_gate, "fsdp", axis=0, tiled=True),
        lax.all_gather(w_up, "fsdp", axis=0, tiled=True),
        lax.all_gather(w_down, "fsdp", axis=1, tiled=True),
        lax.all_gather(gain_attn, "fsdp", axis=0, tiled=True),
        lax.all_gather(gain_ffn, "fsdp", axis=0, tiled=True),
    )
    gain_one = full_gain_one.astype(jnp.float32)
    gain_two = full_gain_two.astype(jnp.float32)
    grad_result = cotangent.astype(jnp.float32).reshape(rows, width)
    grad_low = grad_result.astype(jnp.bfloat16)
    grad_wdown = inner_rows(swish_up, grad_low)
    grad_swish = times_transposed(grad_low, full_down)
    grad_gate_act = (
        grad_swish * upward * sigmoid_gate * (1.0 + gate * (1.0 - sigmoid_gate))
    ).astype(jnp.bfloat16)
    grad_upward = (grad_swish * gate * sigmoid_gate).astype(jnp.bfloat16)
    grad_wgate = inner_rows(hidden_two, grad_gate_act)
    grad_wup = inner_rows(hidden_two, grad_upward)
    grad_hidden_two = head_sum(
        times_transposed(grad_gate_act, full_gate) + times_transposed(grad_upward, full_up)
    )
    grad_gain_two = jnp.sum(grad_hidden_two * normed_two, axis=0)
    grad_resid = grad_result + norm_back(grad_hidden_two * gain_two, normed_two, inverse_two)
    grad_branch = grad_resid.astype(jnp.bfloat16)
    grad_wout = inner_rows(mixed, grad_branch)
    grad_mixed = (
        times_transposed(grad_branch, full_out)
        .astype(jnp.bfloat16)
        .reshape(local_len, sequences, head_width)
    )
    d_heads = split_heads(grad_mixed, HEAD_DIM)

    def query_side(parts):
        q_head, k_head, v_head, d_head, log_total = parts
        scores = (
            jnp.einsum("qsd,ksd->sqk", q_head, k_head, preferred_element_type=jnp.float32) * SCALE
        )
        probs = jnp.exp(jnp.where(mask, scores, MASKED) - log_total)
        grad_probs = jnp.einsum("qsd,ksd->sqk", d_head, v_head, preferred_element_type=jnp.float32)
        delta = jnp.sum(probs * grad_probs, axis=-1, keepdims=True)
        grad_scores = (probs * (grad_probs - delta)).astype(jnp.bfloat16)
        return (
            jnp.einsum("sqk,ksd->qsd", grad_scores, k_head, preferred_element_type=jnp.float32)
            * SCALE,
            delta,
        )

    grad_q_heads, deltas = lax.map(query_side, (q_heads, k_heads, v_heads, d_heads, log_totals))
    grad_query = join_heads(grad_q_heads).astype(jnp.bfloat16).reshape(rows, head_width)
    piece_mask = make_mask(
        query_pos, seg_local, jnp.arange(local_len * lax.axis_size("ctx"), dtype=jnp.int32), seg_all
    )
    k_piece = split_heads(pair_all[..., :head_width], HEAD_DIM)
    v_piece = split_heads(pair_all[..., head_width:], HEAD_DIM)

    def per_head(parts):
        return key_head_grads(parts, piece_mask)

    grad_k_heads, grad_v_heads = lax.map(
        per_head, (q_heads, k_piece, v_piece, d_heads, log_totals, deltas)
    )
    grad_pair = lax.psum_scatter(
        jnp.concatenate([join_heads(grad_k_heads), join_heads(grad_v_heads)], axis=-1).astype(
            jnp.bfloat16
        ),
        "ctx",
        scatter_dimension=0,
        tiled=True,
    ).astype(jnp.float32)
    grad_keys = grad_pair[..., :head_width].astype(jnp.bfloat16).reshape(rows, head_width)
    grad_vals = grad_pair[..., head_width:].astype(jnp.bfloat16).reshape(rows, head_width)
    grad_wquery = inner_rows(hidden_one, grad_query)
    grad_wkey = inner_rows(hidden_one, grad_keys)
    grad_wvalue = inner_rows(hidden_one, grad_vals)
    grad_hidden_one = head_sum(
        times_transposed(grad_query, full_query)
        + times_transposed(grad_keys, full_key)
        + times_transposed(grad_vals, full_value)
    )
    grad_gain_one = jnp.sum(grad_hidden_one * normed_one, axis=0)
    grad_input = grad_resid + norm_back(grad_hidden_one * gain_one, normed_one, inverse_one)
    grad_input = grad_input.astype(jnp.bfloat16).reshape(local_len, sequences, width)
    shares = (
        lax.psum_scatter(
            grad_wquery.astype(jnp.bfloat16), "fsdp", scatter_dimension=0, tiled=True
        ).astype(jnp.float32),
        lax.psum_scatter(
            grad_wkey.astype(jnp.bfloat16), "fsdp", scatter_dimension=0, tiled=True
        ).astype(jnp.float32),
        lax.psum_scatter(
            grad_wvalue.astype(jnp.bfloat16), "fsdp", scatter_dimension=0, tiled=True
        ).astype(jnp.float32),
        lax.psum_scatter(
            grad_wout.astype(jnp.bfloat16), "fsdp", scatter_dimension=1, tiled=True
        ).astype(jnp.float32),
        lax.psum_scatter(
            grad_wgate.astype(jnp.bfloat16), "fsdp", scatter_dimension=0, tiled=True
        ).astype(jnp.float32),
        lax.psum_scatter(
            grad_wup.astype(jnp.bfloat16), "fsdp", scatter_dimension=0, tiled=True
        ).astype(jnp.float32),
        lax.psum_scatter(
            grad_wdown.astype(jnp.bfloat16), "fsdp", scatter_dimension=1, tiled=True
        ).astype(jnp.float32),
        lax.psum_scatter(
            grad_gain_one.astype(jnp.bfloat16), "fsdp", scatter_dimension=0, tiled=True
        ).astype(jnp.float32),
        lax.psum_scatter(
            grad_gain_two.astype(jnp.bfloat16), "fsdp", scatter_dimension=0, tiled=True
        ).astype(jnp.float32),
    )
    shares = (
        lax.psum(shares[0].astype(jnp.bfloat16), "ctx").astype(jnp.float32),
        lax.psum(shares[1].astype(jnp.bfloat16), "ctx").astype(jnp.float32),
        lax.psum(shares[2].astype(jnp.bfloat16), "ctx").astype(jnp.float32),
        lax.psum(shares[3].astype(jnp.bfloat16), "ctx").astype(jnp.float32),
        lax.psum(shares[4].astype(jnp.bfloat16), "ctx").astype(jnp.float32),
        lax.psum(shares[5].astype(jnp.bfloat16), "ctx").astype(jnp.float32),
        lax.psum(shares[6].astype(jnp.bfloat16), "ctx").astype(jnp.float32),
        lax.psum(shares[7].astype(jnp.bfloat16), "ctx").astype(jnp.float32),
        lax.psum(shares[8].astype(jnp.bfloat16), "ctx").astype(jnp.float32),
    )
    return (
        output,
        grad_input,
        shares[0],
        shares[1],
        shares[2],
        shares[3],
        shares[4],
        shares[5],
        shares[6],
        shares[7],
        shares[8],
    )


BF = jnp.bfloat16
F32 = jnp.float32
I32 = jnp.int32
MESH = pl.DeviceIdType.MESH
BLOCK = 256
VMEM_BYTES = 67043328
ORDER = (
    93, 92, 99, 74, 80, 121, 86, 98, 0, 95, 77, 75, 87, 83, 89, 96, 78, 104, 101, 81, 90, 79, 97, 84,
    3, 108, 6, 76, 114, 91, 85, 94, 2, 105, 127, 133, 7, 111, 8, 88, 102, 109, 82, 9, 139, 106, 120, 1,
    117, 132, 50, 123, 112, 107, 103, 115, 100, 54, 118, 144, 55, 56, 51, 113, 4, 124, 57, 126, 119, 58, 138, 110,
    10, 125, 135, 129, 136, 5, 116, 140, 12, 122, 29, 141, 28, 37, 130, 36, 137, 11, 30, 145, 38, 13, 142, 31,
    131, 39, 42, 134, 146, 14, 204, 128, 205, 40, 35, 143, 171, 147, 64, 34, 65, 66, 43, 33, 149, 161, 41, 67,
    32, 172, 15, 68, 162, 44, 46, 152, 16, 166, 59, 60, 173, 18, 206, 163, 45, 47, 61, 167, 153, 150, 52, 156,
    17, 207, 62, 208, 164, 160, 174, 63, 176, 170, 168, 19, 53, 22, 157, 21, 209, 177, 69, 48, 169, 214, 70, 218,
    210, 71, 20, 215, 158, 49, 72, 178, 211, 73, 181, 151, 159, 155, 191, 186, 182, 196, 179, 192, 165, 175, 219, 23,
    187, 212, 154, 183, 216, 200, 197, 148, 220, 213, 217, 188, 184, 201, 180, 193, 198, 221, 202, 189, 185, 194, 190, 203,
    24, 199, 195, 25, 26, 27,
)
SEMS = (48, 191, 28)


def dot_nn(left, right):
    return jnp.dot(left, right, preferred_element_type=F32)


def dot_nt(left, right):
    return lax.dot_general(left, right, (((1,), (1,)), ((), ())), preferred_element_type=F32)


def dot_tn(left, right):
    return lax.dot_general(left, right, (((0,), (0,)), ((), ())), preferred_element_type=F32)


def loop(count, body):
    def step(index, carry):
        body(index)
        return carry

    lax.fori_loop(0, count, step, 0)


def tile(index, size):
    return pl.ds(pl.multiple_of(index * size, size), size)


def only_half(values, half):
    lane = lax.broadcasted_iota(I32, values.shape, 1)
    keep = (lane < HEAD_DIM) if half == 0 else (lane >= HEAD_DIM)
    return jnp.where(keep, values, jnp.zeros_like(values))


def write_bias(bias, seg_col, seg_row, block, length):
    lanes = tile(block, BLOCK)
    keys = seg_col[0:length, :]
    key_pos = lax.broadcasted_iota(I32, (length, BLOCK), 0)
    query_pos = lax.broadcasted_iota(I32, (length, BLOCK), 1) + block * BLOCK
    same = jnp.concatenate([keys, keys], axis=1) == seg_row[0:1, lanes]
    bias[0:length, :] = jnp.where(same & (key_pos <= query_pos), 0.0, MASKED)


def attend_block(block, length, pairs, query, keys, vals_t, bias, seg_col, seg_row, mixed, mixed_t, log_sum):
    write_bias(bias, seg_col, seg_row, block, length)
    rows = tile(block, BLOCK)

    def pair(index):
        cols = tile(index, 2 * HEAD_DIM)
        two = query[rows, cols]
        for half in (0, 1):
            scores = dot_nt(keys[0:length, cols], only_half(two, half)) + bias[0:length, :]
            top = jnp.max(scores, axis=0, keepdims=True)
            expo = jnp.exp(scores - top)
            total = jnp.sum(expo, axis=0, keepdims=True)
            log_sum[2 * index + half, :, rows] = jnp.broadcast_to(top + jnp.log(total), (8, BLOCK))
            probs = (expo * (1.0 / total)).astype(BF)
            head = tile(2 * index + half, HEAD_DIM)
            mixed_t[head, :] = dot_nn(vals_t[head, 0:length], probs)

    loop(pairs, pair)
    mixed[rows, :] = mixed_t[...].T.astype(BF)


def attend_back_block(
    block, length, pairs, query, keys, keys_t, vals, grad_mixed, bias, seg_col, seg_row, log_sum, grad_qkv, grad_q_t, grad_k, grad_v
):
    write_bias(bias, seg_col, seg_row, block, length)
    rows = tile(block, BLOCK)

    def pair(index):
        cols = tile(index, 2 * HEAD_DIM)
        two = query[rows, cols]
        grad_two = grad_mixed[rows, cols]
        for half in (0, 1):
            one = only_half(two, half)
            grad_one = only_half(grad_two, half)
            scores = dot_nt(keys[0:length, cols], one) + bias[0:length, :]
            probs = jnp.exp(scores - log_sum[2 * index + half, 0:1, rows])
            grad_probs = dot_nt(vals[0:length, cols], grad_one)
            delta = jnp.sum(probs * grad_probs, axis=0, keepdims=True)
            grad_scores = (probs * (grad_probs - delta)).astype(BF)
            grad_v[0:length, cols] += dot_nn(probs.astype(BF), grad_one)
            grad_k[0:length, cols] += dot_nn(grad_scores, one)
            head = tile(2 * index + half, HEAD_DIM)
            grad_q_t[head, :] = dot_nn(keys_t[head, 0:length], grad_scores)

    loop(pairs, pair)
    grad_qkv[rows, 0 : grad_q_t.shape[0]] = (grad_q_t[...].T * SCALE).astype(BF)


def layer_kernel(
    nz,
    tok, cot, seg, gain_a, gain_f, w_q, w_k, w_v, w_o, w_g, w_u, w_d,
    out, g_tok, o_q, o_k, o_v, o_o, o_g, o_u, o_d, o_gain,
    xg, cg, seg_row, own_gains, gain_all, wqkv, wo, wg, wu, wd,
    h1, h2, ab, query, keys, vals, keys_t, vals_t, mixed, grad_mixed, grad_qkv, grad_k, grad_v,
    act_g, act_u, act_m, y1, bias, mixed_t, log_sum, seg_col,
    part, pair_sum, from_core, from_y, final_rows,
    p_d0, p_d1, p_g0, p_g1, p_u0, p_u1, p_o, p_q, p_k, p_v, r_d0, r_d1, r_g0, r_g1, r_u0, r_u1, r_o, r_q, r_k, r_v,
    s_d0, s_d1, s_g0, s_g1, s_u0, s_u1, s_o, s_q, s_k, s_v, f_d0, f_d1, f_g0, f_g1, f_u0, f_u1, f_o, f_q, f_k, f_v,
    p_n, r_n, s_n, f_n, c_n, y_n,
    send_sems, recv_sems, local_sems,
):
    fs = lax.axis_index("fsdp")
    y = lax.axis_index("ctx")
    t = lax.axis_index("tp")
    z = fs // 2
    x = lax.rem(fs, 2)
    width = xg.shape[1]
    half_len = xg.shape[0] // 2
    quarter = half_len // 2
    heads_w = query.shape[1]
    hidden = act_m.shape[1]
    db = width // (2 * nz)

    def dev(fq, yq, tq):
        return {"fsdp": fq, "ctx": yq, "tp": tq}

    x_dev = dev(2 * z + (1 - x), y, t)
    y_dev = dev(fs, 1 - y, t)
    c_dev = dev(fs, y, 1 - t)

    def z_from(k):
        return lax.rem(z + nz - k, nz)

    z_next = dev(2 * lax.rem(z + 1, nz) + x, y, t)

    barrier = pltpu.get_barrier_semaphore()
    z_prev = dev(2 * z_from(1) + x, y, t)
    for peer in (x_dev, y_dev, c_dev, z_next, z_prev):
        pl.semaphore_signal(barrier, inc=1, device_id=peer, device_id_type=MESH)
    own_gain_copies = [
        pltpu.make_async_copy(src, own_gains.at[i], local_sems.at[SEMS[2] - 1 - i]) for i, src in enumerate((gain_a, gain_f))
    ]
    for copy in own_gain_copies:
        copy.start()
    for i, copy in enumerate(own_gain_copies):
        copy.wait()
        gain_all[fs, i : i + 1, :] = own_gains[i].astype(F32)
    pl.semaphore_wait(barrier, 5)

    count = {"send": 0, "recv": 0, "local": 0}
    sent = []

    def new(kind):
        count[kind] += 1
        return count[kind] - 1

    slots = [None] * SEMS[0]

    def send(src, dst, device, ridx):
        slot = new("send") % SEMS[0]
        if slots[slot] is not None:
            drain([copy for copy in sent if copy is slots[slot]])
        copy = pltpu.make_async_remote_copy(
            src, dst, send_sems.at[slot], recv_sems.at[ridx], device_id=device, device_id_type=MESH
        )
        slots[slot] = copy
        copy.start()
        sent.append(copy)
        return copy

    def recv(dst, ridx):
        pltpu.make_async_remote_copy(
            dst, dst, send_sems.at[0], recv_sems.at[ridx], device_id=y_dev, device_id_type=MESH
        ).wait_recv()

    def local(src, dst):
        copy = pltpu.make_async_copy(src, dst, local_sems.at[new("local")])
        copy.start()
        return copy

    def many(number):
        return [new("recv") for _ in range(number)]

    def drain(copies):
        left = [copy for copy in sent if any(copy is other for other in copies)]
        for copy in left:
            copy.wait_send()
        sent[:] = [copy for copy in sent if not any(copy is other for other in left)]

    hw = pl.ds(pl.multiple_of(y * heads_w, heads_w), heads_w)

    def rb(fq):
        return tile(fq, db)

    part_h = hidden // 2
    first, second = slice(0, part_h), slice(part_h, hidden)

    def half_of(half, yq):
        return pl.ds(pl.multiple_of(yq * hidden + half * part_h, part_h), part_h)

    names = {
        "n": (gain_all.at[fs], lambda fq: gain_all.at[fq], False),
        "q": (w_q.at[:, hw], lambda fq: wqkv.at[rb(fq), 0:heads_w], False),
        "k": (w_k.at[:, hw], lambda fq: wqkv.at[rb(fq), heads_w : 2 * heads_w], False),
        "v": (w_v.at[:, hw], lambda fq: wqkv.at[rb(fq), 2 * heads_w : 3 * heads_w], False),
        "o": (w_o.at[hw, :], lambda fq: wo.at[:, rb(fq)], True),
    }
    for i, units in enumerate((first, second)):
        mine = half_of(i, y)
        names[f"g{i}"] = (w_g.at[:, mine], lambda fq, units=units: wg.at[rb(fq), units], False)
        names[f"u{i}"] = (w_u.at[:, mine], lambda fq, units=units: wu.at[rb(fq), units], False)
        names[f"d{i}"] = (w_d.at[mine, :], lambda fq, units=units: wd.at[units, rb(fq)], i == 1)
    ring_own = {name: [None] + many(nz - 1) for name in names}
    ring_other = {name: [None] + many(nz - 1) for name in names if names[name][2]}
    over_x = {name: many(1 if names[name][2] else nz) for name in names}
    own_copy = {}

    def start_z(name):
        src, place, _ = names[name]
        if name != "n":
            own_copy[name] = local(src, place(fs))
        send(src, place(fs), z_next, ring_own[name][1])

    def start_x(name):
        src, place, _ = names[name]
        send(src, place(fs), x_dev, over_x[name][0])

    def relay(name, k):
        place, pair_first = names[name][1:]
        block = place(2 * z_from(k) + x)
        recv(block, ring_own[name][k])
        if k < nz - 1:
            send(block, block, z_next, ring_own[name][k + 1])
        if not pair_first:
            send(block, block, x_dev, over_x[name][k])

    def relay_other(name, k):
        block = names[name][1](2 * z_from(k) + (1 - x))
        recv(block, over_x[name][0] if k == 0 else ring_other[name][k])
        if k < nz - 1:
            send(block, block, z_next, ring_other[name][k + 1])

    def arrived(name):
        place, pair_first = names[name][1:]
        if name != "n":
            own_copy[name].wait()
        if not pair_first:
            for k in range(nz):
                recv(place(2 * z_from(k) + (1 - x)), over_x[name][k])

    def rows_of(yq, tq):
        return pl.ds(pl.multiple_of(yq * half_len + tq * quarter, quarter), quarter)

    own_rows = rows_of(y, t)

    tok_y, tok_c, cot_y, cot_c, seg_y = many(5)
    seg_local = local(seg, seg_row.at[:, tile(y, half_len)])
    send(seg, seg_row.at[:, tile(y, half_len)], y_dev, seg_y)
    tok_local = local(tok, xg.at[tile(y, half_len), :])
    cot_local = local(cot, cg.at[tile(y, half_len), :])

    far = rows_of(1 - y, t)
    far_other = rows_of(1 - y, 1 - t)

    def core_forward(ref, y_idx, c_idx):
        recv(ref.at[far, :], y_idx)
        return send(ref.at[far, :], ref.at[far, :], c_dev, c_idx)

    kinds = {"a": 0, "out": 0, "dh2": 1, "dh1": 1}
    ex_recv = {name: many(3) for name in kinds}
    ex_sent = []

    def exchange(name, compute, stage):
        e = kinds[name]
        if stage == 0:
            drain(ex_sent)
            ex_sent.clear()
            compute(far_other, part.at[0])
            ex_sent.append(send(part.at[0], from_core.at[e, 0], c_dev, ex_recv[name][0]))
        elif stage == 1:
            compute(far, part.at[1])
        elif stage == 2:
            recv(from_core.at[e, 0], ex_recv[name][0])

            def add(i):
                r = tile(i, 32)
                pair_sum[r, :] = (part[1, r, :].astype(F32) + from_core[e, 0, r, :].astype(F32)).astype(BF)

            loop(quarter // 32, add)
            ex_sent.append(send(pair_sum, from_y.at[e], y_dev, ex_recv[name][2]))
        elif stage == 3:
            compute(rows_of(y, 1 - t), part.at[2])
            ex_sent.append(send(part.at[2], from_core.at[e, 1], c_dev, ex_recv[name][1]))
        elif stage == 4:
            compute(own_rows, part.at[3])
        else:
            recv(from_core.at[e, 1], ex_recv[name][1])
            recv(from_y.at[e], ex_recv[name][2])

    def total_of(name, r):
        e = kinds[name]
        return part[3, r, :].astype(F32) + from_core[e, 1, r, :].astype(F32) + from_y[e, r, :].astype(F32)

    def spread_rows(ref, idx):
        return [
            send(ref.at[own_rows, :], ref.at[own_rows, :], c_dev, idx[0]),
            send(ref.at[own_rows, :], ref.at[own_rows, :], y_dev, idx[1]),
        ]

    h2_idx = many(3)
    ab_idx = many(3)

    grads = {
        "d0": (p_d0, r_d0, s_d0, f_d0, True),
        "d1": (p_d1, r_d1, s_d1, f_d1, False),
        "g0": (p_g0, r_g0, s_g0, f_g0, False),
        "g1": (p_g1, r_g1, s_g1, f_g1, False),
        "u0": (p_u0, r_u0, s_u0, f_u0, False),
        "u1": (p_u1, r_u1, s_u1, f_u1, False),
        "o": (p_o, r_o, s_o, f_o, False),
        "q": (p_q, r_q, s_q, f_q, False),
        "k": (p_k, r_k, s_k, f_k, False),
        "v": (p_v, r_v, s_v, f_v, False),
        "n": (p_n, r_n, s_n, f_n, False),
    }
    gx = {name: [None] + many(1 if item[4] else nz) for name, item in grads.items()}
    gz = {name: [[None] + many(nz - 1) for _ in range(2 if item[4] else 1)] for name, item in grads.items()}

    def add_rows(rows, cols, body):
        step = min(rows, 16 if cols > 512 else 128)
        loop(rows // step, lambda i: body(tile(i, step)))

    def grad_send(name, k):
        p, r, s, _, ring_first = grads[name]
        if ring_first:
            send(p.at[lax.rem(x + k, 2), z_from(1)], s.at[k - 1, 0], z_next, gz[name][k - 1][1])
        else:
            send(p.at[1 - x, z_from(k)], r.at[k - 1], x_dev, gx[name][k])

    def grad_step(name, k):
        p, r, s, f, ring_first = grads[name]
        if ring_first:
            c, k = divmod(k, 10)
            xq = lax.rem(x + 1 + c, 2)
            recv(s.at[c, k - 2], gz[name][c][k - 1])
            last_own = k == nz and c == 1
            if last_own:
                recv(r.at[0], gx[name][1])

            def add_ring(rr):
                total = p[xq, z_from(k), rr, :].astype(F32) + s[c, k - 2, rr, :].astype(F32)
                if last_own:
                    f[rr, :] = (total + r[0, rr, :].astype(F32)).astype(f.dtype)
                else:
                    p[xq, z_from(k), rr, :] = total.astype(p.dtype)

            add_rows(*p.shape[2:], add_ring)
            if k < nz:
                send(p.at[xq, z_from(k)], s.at[c, k - 1], z_next, gz[name][c][k])
            elif c == 0:
                send(p.at[xq, z_from(k)], r.at[0], x_dev, gx[name][1])
            return
        zq = z_from(k)
        recv(r.at[k - 1], gx[name][k])
        if k > 1:
            recv(s.at[0, k - 2], gz[name][0][k - 1])

        def add(rr):
            total = p[x, zq, rr, :].astype(F32) + r[k - 1, rr, :].astype(F32)
            if k > 1:
                total = total + s[0, k - 2, rr, :].astype(F32)
            if k < nz:
                p[x, zq, rr, :] = total.astype(p.dtype)
            else:
                f[rr, :] = total.astype(f.dtype)

        add_rows(*p.shape[2:], add)
        if k < nz:
            send(p.at[x, zq], s.at[0, k - 1], z_next, gz[name][0][k])

    def place_of(name, yq):
        h = pl.ds(pl.multiple_of(yq * heads_w, heads_w), heads_w)
        if name[0] == "d":
            return o_d.at[half_of(int(name[1]), yq), :]
        if name == "o":
            return o_o.at[h, :]
        wide = {"g": o_g, "u": o_u}
        if name[0] in wide:
            return wide[name[0]].at[:, half_of(int(name[1]), yq)]
        return {"q": o_q, "k": o_k, "v": o_v}[name].at[:, h]

    out_idx = {name: many(1)[0] for name in grads if name != "n"}
    last_local = []

    def grad_end(name):
        f = grads[name][3]
        last_local.append(local(f, place_of(name, y)))
        send(f, place_of(name, y), y_dev, out_idx[name])

    def grad_done(name):
        recv(place_of(name, 1 - y), out_idx[name])

    value = {}
    blocks = half_len // BLOCK
    pairs = heads_w // (2 * HEAD_DIM)
    out_c, gtok_c = many(2)
    n_c, n_y = many(2)
    my_rows = tile(t, quarter)
    other_rows = tile(1 - t, quarter)
    row_sends = []

    def send_tok():
        send(tok.at[tile(t, quarter), :], xg.at[own_rows, :], y_dev, tok_y)

    def send_cot():
        send(cot.at[tile(t, quarter), :], cg.at[own_rows, :], y_dev, cot_y)

    def gather_gains():
        value["one"] = jnp.concatenate([gain_all[i, 0:1, :] for i in range(2 * nz)], axis=1)
        value["two"] = jnp.concatenate([gain_all[i, 1:2, :] for i in range(2 * nz)], axis=1)

    def norm_rows(start):
        gain_one = value["one"]

        def body(i):
            r = pl.ds(pl.multiple_of(start + i * 32, 32), 32)
            values = xg[r, :].astype(F32)
            inverse = lax.rsqrt(jnp.mean(values * values, axis=-1, keepdims=True) + EPSILON)
            h1[r, :] = (values * inverse * gain_one).astype(BF)

        loop(half_len // 32, body)

    def norm_own():
        tok_local.wait()
        norm_rows(y * half_len)

    def norm_far():
        recv(xg.at[far_other, :], tok_c)
        norm_rows((1 - y) * half_len)

    def segments():
        seg_local.wait()
        recv(seg_row.at[:, tile(1 - y, half_len)], seg_y)
        seg_col[...] = jnp.broadcast_to(seg_row[0:1, :], (128, 2 * half_len)).T

    def project():
        def body(i):
            r = tile(i, 512)
            rows = h1[r, :]
            query[r, :] = (dot_nn(rows, wqkv[:, 0:heads_w]).astype(BF).astype(F32) * SCALE).astype(BF)
            keys[r, :] = dot_nn(rows, wqkv[:, heads_w : 2 * heads_w]).astype(BF)
            vals[r, :] = dot_nn(rows, wqkv[:, 2 * heads_w : 3 * heads_w]).astype(BF)

        loop(xg.shape[0] // 512, body)
        keys_t[...] = keys[...].T
        vals_t[...] = vals[...].T

    def either(half, body):
        @pl.when(half == 0)
        def _():
            body(half_len)

        @pl.when(half == 1)
        def _():
            body(2 * half_len)

    def attend(half):
        def block(i):
            args = (pairs, query, keys, vals_t, bias, seg_col, seg_row, mixed, mixed_t, log_sum)
            either(half, lambda length: attend_block(half * blocks + i, length, *args))

        loop(blocks, block)

    def out_rows(r, dst):
        dst[...] = dot_nn(mixed[r, :], wo[...]).astype(BF)

    def first_residual():
        exchange("a", None, 5)
        gain_two = value["two"]

        def body(i):
            r = tile(i, 32)
            rr = pl.ds(pl.multiple_of(y * half_len + t * quarter + i * 32, 32), 32)
            values = xg[rr, :].astype(F32) + total_of("a", r)
            y1[r, :] = values
            inverse = lax.rsqrt(jnp.mean(values * values, axis=-1, keepdims=True) + EPSILON)
            h2[rr, :] = (values * inverse * gain_two).astype(BF)

        loop(quarter // 32, body)
        row_sends.extend(spread_rows(h2, h2_idx))

    def gate(half, r):
        rows = h2[r, :]

        def cols(j):
            c = pl.ds(pl.multiple_of(half * part_h + j * 256, 256), 256)
            g = dot_nn(rows, wg[:, c])
            u = dot_nn(rows, wu[:, c])
            sg = 1.0 / (1.0 + jnp.exp(-g))
            gs = g * sg
            act_u[r, c] = gs.astype(BF)
            act_g[r, c] = (u * sg * (1.0 + g * (1.0 - sg))).astype(BF)
            act_m[r, c] = (gs * u).astype(BF)

        loop(part_h // 256, cols)

    def grad_cols(left, start, right, p, index):
        c = tile(index, 2 * db)
        for i in range(p.shape[2] // 256):
            r = slice(start + i * 256, start + (i + 1) * 256)
            both = dot_tn(left[:, r], right[:, c]).astype(BF)
            rows = slice(i * 256, (i + 1) * 256)
            p[0, index, rows, :] = both[:, 0:db]
            p[1, index, rows, :] = both[:, db : 2 * db]

    def grad_rows(left, right, units, p, index):
        c = tile(index, 2 * db)
        both = dot_tn(left[:, c], right[:, units]).astype(BF)
        p[0, index] = both[0:db, :]
        p[1, index] = both[db : 2 * db, :]

    def grad_down(part_of, p):
        loop(nz, lambda i: grad_cols(act_m, part_of * part_h, cg, p, i))

    def some_blocks(name, left, right, units, ks):
        p = grads[name][0]
        loop(len(ks), lambda i: grad_rows(left, right, units, p, z_from(ks[0] + i)))
        for k in ks:
            grad_send(name, k)

    def qkv_blocks(ks):
        def body(i):
            index = z_from(ks[0] + i)
            both = dot_tn(h1[:, tile(index, 2 * db)], grad_qkv[...]).astype(BF)
            for j, p in enumerate((p_q, p_k, p_v)):
                c = slice(j * heads_w, (j + 1) * heads_w)
                p[0, index] = both[0:db, c]
                p[1, index] = both[db : 2 * db, c]

        loop(len(ks), body)

    def hidden_back(half, r, dst):
        rows = cg[r, :]
        units = (first, second)[half]

        def cols(j):
            c = pl.ds(pl.multiple_of(half * part_h + j * 256, 256), 256)
            dm = dot_nt(rows, wd[c, :])
            act_g[r, c] = (dm * act_g[r, c].astype(F32)).astype(BF)
            act_u[r, c] = (dm * act_u[r, c].astype(F32)).astype(BF)

        loop(part_h // 256, cols)

        def back(j):
            c = tile(j, 512)
            total = dot_nt(act_g[r, units], wg[c, units]) + dot_nt(act_u[r, units], wu[c, units])
            if half == 0:
                ab[r, c] = total.astype(BF)
            else:
                dst[:, c] = (total + ab[r, c].astype(F32)).astype(BF)

        loop(width // 512, back)

    def second_residual():
        exchange("dh2", None, 5)
        gain_two = value["two"]

        def body(i, carry):
            r = tile(i, 32)
            rr = pl.ds(pl.multiple_of(y * half_len + t * quarter + i * 32, 32), 32)
            values = y1[r, :]
            inverse = lax.rsqrt(jnp.mean(values * values, axis=-1, keepdims=True) + EPSILON)
            normed = values * inverse
            grad = total_of("dh2", r)
            scaled = grad * gain_two
            mean = jnp.mean(scaled * normed, axis=-1, keepdims=True)
            full = cg[rr, :].astype(F32) + inverse * (scaled - normed * mean)
            final_rows[r, :] = full
            ab[rr, :] = full.astype(BF)
            return carry + jnp.sum(grad * normed, axis=0, keepdims=True)

        value["grad_two"] = lax.fori_loop(0, quarter // 32, body, jnp.zeros((1, width), F32))
        row_sends.extend(spread_rows(ab, ab_idx))

    def down_rows(r, dst):
        def cols(j):
            c = tile(j, 512)
            dst[:, c] = dot_nn(act_m[r, :], wd[:, c]).astype(BF)

        loop(width // 512, cols)

    def mixed_back(half):
        r = tile(half, half_len)
        grad_mixed[r, :] = dot_nt(ab[r, :], wo[...]).astype(BF)

    def clear_sums():
        grad_k[...] = jnp.zeros_like(grad_k)
        grad_v[...] = jnp.zeros_like(grad_v)

    def attend_back(half):
        def block(i):
            args = (
                pairs, query, keys, keys_t, vals, grad_mixed, bias, seg_col, seg_row, log_sum, grad_qkv, mixed_t, grad_k, grad_v,
            )
            either(half, lambda length: attend_back_block(half * blocks + i, length, *args))

        loop(blocks, block)

    def own_back():
        recv(ab.at[rows_of(y, 1 - t), :], ab_idx[0])
        clear_sums()
        mixed_back(y)

    def far_back():
        recv(ab.at[far_other, :], ab_idx[2])
        mixed_back(1 - y)

    def grad_out_all():
        loop(nz, lambda i: grad_cols(mixed, 0, ab, p_o, i))
        for k in range(1, nz + 1):
            grad_send("o", k)

    def sums_to_bf16():
        grad_qkv[:, heads_w : 2 * heads_w] = grad_k[...].astype(BF)
        grad_qkv[:, 2 * heads_w : 3 * heads_w] = grad_v[...].astype(BF)

    def hidden_one_back(r, dst):
        def cols(j):
            c = tile(j, 512)
            dst[:, c] = dot_nt(grad_qkv[r, :], wqkv[c, :]).astype(BF)

        loop(width // 512, cols)

    def finish_out():
        exchange("out", None, 5)

        def body(i):
            r = tile(i, 32)
            act_m[r, 0:width] = (y1[r, :] + total_of("out", r)).astype(BF)

        loop(quarter // 32, body)
        last_local.append(local(act_m.at[0:quarter, 0:width], out.at[my_rows, :]))
        send(act_m.at[0:quarter, 0:width], out.at[my_rows, :], c_dev, out_c)

    def finish_tokens():
        exchange("dh1", None, 5)
        drain(row_sends)
        gain_one = value["one"]

        def body(i, carry):
            r = tile(i, 32)
            rr = pl.ds(pl.multiple_of(y * half_len + t * quarter + i * 32, 32), 32)
            values = xg[rr, :].astype(F32)
            inverse = lax.rsqrt(jnp.mean(values * values, axis=-1, keepdims=True) + EPSILON)
            normed = values * inverse
            grad = total_of("dh1", r)
            scaled = grad * gain_one
            mean = jnp.mean(scaled * normed, axis=-1, keepdims=True)
            full = final_rows[r, :] + inverse * (scaled - normed * mean)
            h2[r, :] = full.astype(BF)
            return carry + jnp.sum(grad * normed, axis=0, keepdims=True)

        gain_one_grad = lax.fori_loop(0, quarter // 32, body, jnp.zeros((1, width), F32))
        for i in range(2 * nz):
            c = slice(i * db, (i + 1) * db)
            p_n[i % 2, i // 2] = jnp.concatenate(
                [gain_one_grad[:, c], value["grad_two"][:, c], jnp.zeros((6, db), F32)], axis=0
            )
        for k in range(1, nz + 1):
            grad_send("n", k)
        last_local.append(local(h2.at[0:quarter, :], g_tok.at[my_rows, :]))
        send(h2.at[0:quarter, :], g_tok.at[my_rows, :], c_dev, gtok_c)

    def gains_core():
        send(f_n, c_n, c_dev, n_c)

    def gains_y():
        recv(c_n, n_c)
        y_n[0] = f_n[...] + c_n[...]
        send(y_n.at[0], y_n.at[1], y_dev, n_y)

    def gains_end():
        recv(y_n.at[1], n_y)
        c_n[...] = y_n[0] + y_n[1]
        last_local.append(local(c_n, o_gain))

    def finish():
        for name in out_idx:
            grad_done(name)
        recv(out.at[other_rows, :], out_c)
        recv(g_tok.at[other_rows, :], gtok_c)
        for copy in last_local:
            copy.wait()
        drain(list(sent))

    two = (1, 2), (3, 4)
    tasks = [
        send_tok,
        send_cot,
        gather_gains,
        lambda: core_forward(xg, tok_y, tok_c),
        lambda: core_forward(cg, cot_y, cot_c),
        lambda: (cot_local.wait(), recv(cg.at[far_other, :], cot_c)),
        segments,
        norm_own,
        norm_far,
        project,
        first_residual,
        lambda: row_sends.append(core_forward(h2, h2_idx[1], h2_idx[2])),
        lambda: recv(h2.at[rows_of(y, 1 - t), :], h2_idx[0]),
        lambda: recv(h2.at[far_other, :], h2_idx[2]),
        lambda: grad_down(0, p_d0),
        lambda: grad_down(1, p_d1),
        second_residual,
        lambda: row_sends.append(core_forward(ab, ab_idx[1], ab_idx[2])),
        own_back,
        far_back,
        grad_out_all,
        sums_to_bf16,
        finish_out,
        finish_tokens,
        gains_core,
        gains_y,
        gains_end,
        finish,
    ]
    all_rows = (own_rows, rows_of(y, 1 - t), far, far_other)
    tasks += [functools.partial(gate, half, r) for half in (0, 1) for r in all_rows]
    tasks += [functools.partial(hidden_back, 0, r, None) for r in all_rows]
    for i, units in enumerate((first, second)):
        tasks += [functools.partial(some_blocks, f"g{i}", h2, act_g, units, ks) for ks in two]
        tasks += [functools.partial(some_blocks, f"u{i}", h2, act_u, units, ks) for ks in two]
    tasks += [functools.partial(qkv_blocks, ks) for ks in two]
    tasks += [functools.partial(attend, half) for half in (1 - y, y)]
    tasks += [functools.partial(attend_back, half) for half in (y, 1 - y)]
    for name, compute in zip(kinds, (out_rows, down_rows, functools.partial(hidden_back, 1), hidden_one_back)):
        tasks += [functools.partial(exchange, name, compute, i) for i in range(5)]
    for name in names:
        tasks += [functools.partial(start_z, name), functools.partial(start_x, name), functools.partial(arrived, name)]
        tasks += [functools.partial(relay, name, k) for k in range(1, nz)]
        if names[name][2]:
            tasks += [functools.partial(relay_other, name, k) for k in range(nz)]
    for name in grads:
        if name in out_idx:
            tasks.append(functools.partial(grad_end, name))
        if grads[name][4]:
            tasks += [functools.partial(grad_step, name, 10 * c + k) for c in (0, 1) for k in range(2, nz + 1)]
        else:
            tasks += [functools.partial(grad_step, name, k) for k in range(1, nz + 1)]
    for name in ("d0", "d1", "q", "k", "v"):
        tasks += [functools.partial(grad_send, name, k) for k in ((1, 2) if grads[name][4] else range(1, nz + 1))]
    assert sorted(ORDER) == list(range(len(tasks)))
    for index in ORDER:
        tasks[index]()


def fused(nz, tokens, segment_ids, w_query, w_key, w_value, w_out, w_gate, w_up, w_down, gain_attn, gain_ffn, cotangent):
    half_len, _, width = tokens.shape
    length = 2 * half_len
    quarter = half_len // 2
    heads_w = w_query.shape[1] // 2
    hidden = w_gate.shape[1] // 2
    db = w_query.shape[0]
    heads = heads_w // HEAD_DIM
    gains = (gain_attn.reshape(1, db), gain_ffn.reshape(1, db))

    def vm(*shape, dtype=BF):
        return pltpu.VMEM(shape, dtype)

    shape_d, shape_g, shape_o, shape_q = (hidden // 2, db), (db, hidden // 2), (heads_w, db), (db, heads_w)
    shapes = (shape_d, shape_d, *[shape_g] * 4, shape_o, shape_q, shape_q, shape_q)
    ring_first = (True, *[False] * 9)
    scratch = [
        vm(length, width), vm(length, width), vm(1, length, dtype=I32), vm(2, 1, db), vm(2 * nz, 2, db, dtype=F32),
        vm(width, 3 * heads_w), vm(heads_w, width), vm(width, hidden), vm(width, hidden), vm(hidden, width),
        vm(length, width), vm(length, width), vm(length, width),
        vm(length, heads_w), vm(length, heads_w), vm(length, heads_w), vm(heads_w, length), vm(heads_w, length),
        vm(length, heads_w), vm(length, heads_w), vm(length, 3 * heads_w),
        vm(length, heads_w, dtype=F32), vm(length, heads_w, dtype=F32),
        vm(length, hidden), vm(length, hidden), vm(length, hidden),
        vm(quarter, width, dtype=F32), vm(length, BLOCK, dtype=F32), vm(heads_w, BLOCK, dtype=F32),
        vm(heads, 8, length, dtype=F32), vm(length, 128, dtype=I32),
        vm(4, quarter, width), vm(quarter, width), vm(2, 2, quarter, width), vm(2, quarter, width),
        vm(quarter, width, dtype=F32),
    ]
    scratch += [vm(2, nz, *shape) for shape in shapes]
    scratch += [vm(1 if first else nz, *shape) for shape, first in zip(shapes, ring_first)]
    scratch += [vm(2 if first else 1, nz - 1, *shape) for shape, first in zip(shapes, ring_first)]
    scratch += [vm(*shape) for shape in shapes]
    scratch += [
        vm(2, nz, 8, db, dtype=F32), vm(nz, 8, db, dtype=F32), vm(1, nz - 1, 8, db, dtype=F32), vm(8, db, dtype=F32),
        vm(8, db, dtype=F32), vm(2, 8, db, dtype=F32),
    ]
    scratch += [pltpu.SemaphoreType.DMA((SEMS[0],)), pltpu.SemaphoreType.DMA((SEMS[1],)), pltpu.SemaphoreType.DMA((SEMS[2],))]
    anywhere = pl.BlockSpec(memory_space=pl.ANY)
    weights = (w_query, w_key, w_value, w_out, w_gate, w_up, w_down)
    results_bytes = (9 << 19) - (1 << 16)
    results = pl.pallas_call(
        functools.partial(layer_kernel, nz),
        out_shape=[pltpu.VMEM((half_len, width), BF)] * 2
        + [pltpu.VMEM(item.shape, BF) for item in weights]
        + [pltpu.VMEM((8, db), F32)],
        in_specs=[anywhere] * 12,
        out_specs=[anywhere] * 10,
        scratch_shapes=scratch,
        compiler_params=pltpu.CompilerParams(
            collective_id=0, has_side_effects=True, vmem_limit_bytes=VMEM_BYTES - results_bytes
        ),
        name="layer",
    )(tokens.reshape(half_len, width), cotangent.reshape(half_len, width), segment_ids, *gains, *weights)
    bodies = results[:9]
    wide = [jax.ShapeDtypeStruct(item.shape, BF if i < 2 else F32) for i, item in enumerate(bodies)]

    def widen(*refs):
        srcs, rows, dsts = refs[:9], refs[9], refs[10:21]
        finals, store_sems = refs[21:28], refs[28]
        stores = []

        def put(src, dst):
            stores.append(pltpu.make_async_copy(src, dst, store_sems.at[len(stores)]))
            stores[-1].start()

        for i in (0, 1):
            put(srcs[i], dsts[i])
            put(rows.at[i : i + 1, :], dsts[9 + i])
        for i in (*range(6, 9), *range(2, 6)):
            finals[i - 2][...] = srcs[i][...].astype(F32)
            put(finals[i - 2], dsts[i])
        for copy in stores:
            copy.wait()

    finals = pl.pallas_call(
        widen,
        out_shape=wide + [jax.ShapeDtypeStruct((1, db), F32)] * 2,
        in_specs=[pl.BlockSpec(memory_space=pltpu.VMEM)] * 10,
        out_specs=[anywhere] * 11,
        scratch_shapes=[vm(*item.shape, dtype=F32) for item in wide[2:]]
        + [pltpu.SemaphoreType.DMA((11,))],
        compiler_params=pltpu.CompilerParams(vmem_limit_bytes=16 << 20),
        name="widen",
    )(*results)
    shape = tokens.shape
    return (finals[0].reshape(shape), finals[1].reshape(shape), *finals[2:9], finals[9].reshape(db), finals[10].reshape(db))


def fits(mesh, tokens_shape):
    return mesh.shape["fsdp"] == 8 and mesh.shape["ctx"] == 2 and mesh.shape["tp"] == 2 and tokens_shape[1:] == (1, 1024)


def solution(mesh):
    def step(tokens, *rest):
        if fits(mesh, tokens.shape):
            return fused(mesh.shape["fsdp"] // 2, tokens, *rest)
        return local(tokens, *rest)

    return jax.shard_map(
        step,
        mesh=mesh,
        in_specs=(
            P("ctx", "fsdp", None),
            P("fsdp", "ctx"),
            P("fsdp", "tp"),
            P("fsdp", "tp"),
            P("fsdp", "tp"),
            P("tp", "fsdp"),
            P("fsdp", "tp"),
            P("fsdp", "tp"),
            P("tp", "fsdp"),
            P("fsdp"),
            P("fsdp"),
            P("ctx", "fsdp", None),
        ),
        out_specs=(
            P("ctx", "fsdp", None),
            P("ctx", "fsdp", None),
            P("fsdp", "tp"),
            P("fsdp", "tp"),
            P("fsdp", "tp"),
            P("tp", "fsdp"),
            P("fsdp", "tp"),
            P("fsdp", "tp"),
            P("tp", "fsdp"),
            P("fsdp"),
            P("fsdp"),
        ),
        check_vma=False,
    )
```

```python
import functools

import jax
import jax.numpy as jnp
from jax import lax
from jax.experimental import pallas as pl
from jax.experimental.pallas import tpu as pltpu
from jax.sharding import PartitionSpec as P

HEAD_DIM = 64


EPSILON = 1e-05
SCALE = 0.125
MASKED = -1e30


def normalize(values):
    inverse = lax.rsqrt(jnp.mean(values * values, axis=-1, keepdims=True) + EPSILON)
    return (values * inverse, inverse)


def norm_back(grad_normed, normed, inverse):
    return inverse * (grad_normed - normed * jnp.mean(grad_normed * normed, axis=-1, keepdims=True))


def inner_rows(left, right):
    return lax.dot_general(
        left, right, (((0,), (0,)), ((), ())), preferred_element_type=jnp.float32
    )


def times_transposed(left, weight):
    return lax.dot_general(
        left, weight, (((1,), (1,)), ((), ())), preferred_element_type=jnp.float32
    )


def head_sum(partial_sum):
    return lax.psum(partial_sum, "tp")


def split_heads(values, head_size):
    length, sequences, width = values.shape
    return jnp.moveaxis(values.reshape(length, sequences, width // head_size, head_size), 2, 0)


def join_heads(values):
    heads, length, sequences, head_size = values.shape
    return jnp.moveaxis(values, 0, 2).reshape(length, sequences, heads * head_size)


def make_mask(query_pos, query_seg, key_pos, key_seg):
    before = key_pos[None, None, :] <= query_pos[None, :, None]
    same = query_seg.T[:, :, None] == key_seg.T[:, None, :]
    return before & same


def key_head_grads(parts, use_mask):
    q_head, k_head, v_head, d_head, log_total, delta = parts
    scores = jnp.einsum("qsd,ksd->sqk", q_head, k_head, preferred_element_type=jnp.float32) * SCALE
    probs = jnp.exp(jnp.where(use_mask, scores, MASKED) - log_total)
    grad_probs = jnp.einsum("qsd,ksd->sqk", d_head, v_head, preferred_element_type=jnp.float32)
    grad_scores = (probs * (grad_probs - delta)).astype(jnp.bfloat16)
    grad_v = jnp.einsum(
        "sqk,qsd->ksd", probs.astype(jnp.bfloat16), d_head, preferred_element_type=jnp.float32
    )
    grad_k = (
        jnp.einsum("sqk,qsd->ksd", grad_scores, q_head, preferred_element_type=jnp.float32) * SCALE
    )
    return (grad_k, grad_v)


def local(
    tokens,
    segment_ids,
    w_query,
    w_key,
    w_value,
    w_out,
    w_gate,
    w_up,
    w_down,
    gain_attn,
    gain_ffn,
    cotangent,
):
    local_len, sequences, width = tokens.shape
    rows = local_len * sequences
    (
        full_query,
        full_key,
        full_value,
        full_out,
        full_gate,
        full_up,
        full_down,
        full_gain_one,
        full_gain_two,
    ) = (
        lax.all_gather(w_query, "fsdp", axis=0, tiled=True),
        lax.all_gather(w_key, "fsdp", axis=0, tiled=True),
        lax.all_gather(w_value, "fsdp", axis=0, tiled=True),
        lax.all_gather(w_out, "fsdp", axis=1, tiled=True),
        lax.all_gather(w_gate, "fsdp", axis=0, tiled=True),
        lax.all_gather(w_up, "fsdp", axis=0, tiled=True),
        lax.all_gather(w_down, "fsdp", axis=1, tiled=True),
        lax.all_gather(gain_attn, "fsdp", axis=0, tiled=True),
        lax.all_gather(gain_ffn, "fsdp", axis=0, tiled=True),
    )
    gain_one = full_gain_one.astype(jnp.float32)
    gain_two = full_gain_two.astype(jnp.float32)
    head_width = full_query.shape[1]
    flat = tokens.astype(jnp.float32).reshape(rows, width)
    normed_one, inverse_one = normalize(flat)
    hidden_one = (normed_one * gain_one).astype(jnp.bfloat16)
    query = (
        jnp.dot(hidden_one, full_query, preferred_element_type=jnp.float32)
        .astype(jnp.bfloat16)
        .reshape(local_len, sequences, head_width)
    )
    keys = (
        jnp.dot(hidden_one, full_key, preferred_element_type=jnp.float32)
        .astype(jnp.bfloat16)
        .reshape(local_len, sequences, head_width)
    )
    vals = (
        jnp.dot(hidden_one, full_value, preferred_element_type=jnp.float32)
        .astype(jnp.bfloat16)
        .reshape(local_len, sequences, head_width)
    )
    pair = jnp.concatenate([keys, vals], axis=-1)
    seg_local = segment_ids.T
    pair_all, seg_all = (
        lax.all_gather(pair, "ctx", axis=0, tiled=True),
        lax.all_gather(seg_local, "ctx", axis=0, tiled=True),
    )
    length = pair_all.shape[0]
    query_pos = lax.axis_index("ctx") * local_len + jnp.arange(local_len, dtype=jnp.int32)
    all_pos = jnp.arange(length, dtype=jnp.int32)
    mask = make_mask(query_pos, seg_local, all_pos, seg_all)
    q_heads = split_heads(query, HEAD_DIM)
    k_heads = split_heads(pair_all[..., :head_width], HEAD_DIM)
    v_heads = split_heads(pair_all[..., head_width:], HEAD_DIM)

    def attend(parts):
        q_head, k_head, v_head = parts
        scores = (
            jnp.einsum("qsd,ksd->sqk", q_head, k_head, preferred_element_type=jnp.float32) * SCALE
        )
        scores = jnp.where(mask, scores, MASKED)
        row_max = jnp.max(scores, axis=-1, keepdims=True)
        log_total = row_max + jnp.log(jnp.sum(jnp.exp(scores - row_max), axis=-1, keepdims=True))
        probs = jnp.exp(scores - log_total).astype(jnp.bfloat16)
        return (
            jnp.einsum("sqk,ksd->qsd", probs, v_head, preferred_element_type=jnp.float32),
            log_total,
        )

    attended, log_totals = lax.map(attend, (q_heads, k_heads, v_heads))
    mixed = join_heads(attended).astype(jnp.bfloat16).reshape(rows, head_width)
    resid = flat + head_sum(jnp.dot(mixed, full_out, preferred_element_type=jnp.float32))
    normed_two, inverse_two = normalize(resid)
    hidden_two = (normed_two * gain_two).astype(jnp.bfloat16)
    gate = jnp.dot(hidden_two, full_gate, preferred_element_type=jnp.float32)
    upward = jnp.dot(hidden_two, full_up, preferred_element_type=jnp.float32)
    sigmoid_gate = jax.nn.sigmoid(gate)
    swish_up = (gate * sigmoid_gate * upward).astype(jnp.bfloat16)
    result = resid + head_sum(jnp.dot(swish_up, full_down, preferred_element_type=jnp.float32))
    output = result.astype(jnp.bfloat16).reshape(local_len, sequences, width)
    (
        full_query,
        full_key,
        full_value,
        full_out,
        full_gate,
        full_up,
        full_down,
        full_gain_one,
        full_gain_two,
    ) = (
        lax.all_gather(w_query, "fsdp", axis=0, tiled=True),
        lax.all_gather(w_key, "fsdp", axis=0, tiled=True),
        lax.all_gather(w_value, "fsdp", axis=0, tiled=True),
        lax.all_gather(w_out, "fsdp", axis=1, tiled=True),
        lax.all_gather(w_gate, "fsdp", axis=0, tiled=True),
        lax.all_gather(w_up, "fsdp", axis=0, tiled=True),
        lax.all_gather(w_down, "fsdp", axis=1, tiled=True),
        lax.all_gather(gain_attn, "fsdp", axis=0, tiled=True),
        lax.all_gather(gain_ffn, "fsdp", axis=0, tiled=True),
    )
    gain_one = full_gain_one.astype(jnp.float32)
    gain_two = full_gain_two.astype(jnp.float32)
    grad_result = cotangent.astype(jnp.float32).reshape(rows, width)
    grad_low = grad_result.astype(jnp.bfloat16)
    grad_wdown = inner_rows(swish_up, grad_low)
    grad_swish = times_transposed(grad_low, full_down)
    grad_gate_act = (
        grad_swish * upward * sigmoid_gate * (1.0 + gate * (1.0 - sigmoid_gate))
    ).astype(jnp.bfloat16)
    grad_upward = (grad_swish * gate * sigmoid_gate).astype(jnp.bfloat16)
    grad_wgate = inner_rows(hidden_two, grad_gate_act)
    grad_wup = inner_rows(hidden_two, grad_upward)
    grad_hidden_two = head_sum(
        times_transposed(grad_gate_act, full_gate) + times_transposed(grad_upward, full_up)
    )
    grad_gain_two = jnp.sum(grad_hidden_two * normed_two, axis=0)
    grad_resid = grad_result + norm_back(grad_hidden_two * gain_two, normed_two, inverse_two)
    grad_branch = grad_resid.astype(jnp.bfloat16)
    grad_wout = inner_rows(mixed, grad_branch)
    grad_mixed = (
        times_transposed(grad_branch, full_out)
        .astype(jnp.bfloat16)
        .reshape(local_len, sequences, head_width)
    )
    d_heads = split_heads(grad_mixed, HEAD_DIM)

    def query_side(parts):
        q_head, k_head, v_head, d_head, log_total = parts
        scores = (
            jnp.einsum("qsd,ksd->sqk", q_head, k_head, preferred_element_type=jnp.float32) * SCALE
        )
        probs = jnp.exp(jnp.where(mask, scores, MASKED) - log_total)
        grad_probs = jnp.einsum("qsd,ksd->sqk", d_head, v_head, preferred_element_type=jnp.float32)
        delta = jnp.sum(probs * grad_probs, axis=-1, keepdims=True)
        grad_scores = (probs * (grad_probs - delta)).astype(jnp.bfloat16)
        return (
            jnp.einsum("sqk,ksd->qsd", grad_scores, k_head, preferred_element_type=jnp.float32)
            * SCALE,
            delta,
        )

    grad_q_heads, deltas = lax.map(query_side, (q_heads, k_heads, v_heads, d_heads, log_totals))
    grad_query = join_heads(grad_q_heads).astype(jnp.bfloat16).reshape(rows, head_width)
    piece_mask = make_mask(
        query_pos, seg_local, jnp.arange(local_len * lax.axis_size("ctx"), dtype=jnp.int32), seg_all
    )
    k_piece = split_heads(pair_all[..., :head_width], HEAD_DIM)
    v_piece = split_heads(pair_all[..., head_width:], HEAD_DIM)

    def per_head(parts):
        return key_head_grads(parts, piece_mask)

    grad_k_heads, grad_v_heads = lax.map(
        per_head, (q_heads, k_piece, v_piece, d_heads, log_totals, deltas)
    )
    grad_pair = lax.psum_scatter(
        jnp.concatenate([join_heads(grad_k_heads), join_heads(grad_v_heads)], axis=-1).astype(
            jnp.bfloat16
        ),
        "ctx",
        scatter_dimension=0,
        tiled=True,
    ).astype(jnp.float32)
    grad_keys = grad_pair[..., :head_width].astype(jnp.bfloat16).reshape(rows, head_width)
    grad_vals = grad_pair[..., head_width:].astype(jnp.bfloat16).reshape(rows, head_width)
    grad_wquery = inner_rows(hidden_one, grad_query)
    grad_wkey = inner_rows(hidden_one, grad_keys)
    grad_wvalue = inner_rows(hidden_one, grad_vals)
    grad_hidden_one = head_sum(
        times_transposed(grad_query, full_query)
        + times_transposed(grad_keys, full_key)
        + times_transposed(grad_vals, full_value)
    )
    grad_gain_one = jnp.sum(grad_hidden_one * normed_one, axis=0)
    grad_input = grad_resid + norm_back(grad_hidden_one * gain_one, normed_one, inverse_one)
    grad_input = grad_input.astype(jnp.bfloat16).reshape(local_len, sequences, width)
    shares = (
        lax.psum_scatter(
            grad_wquery.astype(jnp.bfloat16), "fsdp", scatter_dimension=0, tiled=True
        ).astype(jnp.float32),
        lax.psum_scatter(
            grad_wkey.astype(jnp.bfloat16), "fsdp", scatter_dimension=0, tiled=True
        ).astype(jnp.float32),
        lax.psum_scatter(
            grad_wvalue.astype(jnp.bfloat16), "fsdp", scatter_dimension=0, tiled=True
        ).astype(jnp.float32),
        lax.psum_scatter(
            grad_wout.astype(jnp.bfloat16), "fsdp", scatter_dimension=1, tiled=True
        ).astype(jnp.float32),
        lax.psum_scatter(
            grad_wgate.astype(jnp.bfloat16), "fsdp", scatter_dimension=0, tiled=True
        ).astype(jnp.float32),
        lax.psum_scatter(
            grad_wup.astype(jnp.bfloat16), "fsdp", scatter_dimension=0, tiled=True
        ).astype(jnp.float32),
        lax.psum_scatter(
            grad_wdown.astype(jnp.bfloat16), "fsdp", scatter_dimension=1, tiled=True
        ).astype(jnp.float32),
        lax.psum_scatter(
            grad_gain_one.astype(jnp.bfloat16), "fsdp", scatter_dimension=0, tiled=True
        ).astype(jnp.float32),
        lax.psum_scatter(
            grad_gain_two.astype(jnp.bfloat16), "fsdp", scatter_dimension=0, tiled=True
        ).astype(jnp.float32),
    )
    shares = (
        lax.psum(shares[0].astype(jnp.bfloat16), "ctx").astype(jnp.float32),
        lax.psum(shares[1].astype(jnp.bfloat16), "ctx").astype(jnp.float32),
        lax.psum(shares[2].astype(jnp.bfloat16), "ctx").astype(jnp.float32),
        lax.psum(shares[3].astype(jnp.bfloat16), "ctx").astype(jnp.float32),
        lax.psum(shares[4].astype(jnp.bfloat16), "ctx").astype(jnp.float32),
        lax.psum(shares[5].astype(jnp.bfloat16), "ctx").astype(jnp.float32),
        lax.psum(shares[6].astype(jnp.bfloat16), "ctx").astype(jnp.float32),
        lax.psum(shares[7].astype(jnp.bfloat16), "ctx").astype(jnp.float32),
        lax.psum(shares[8].astype(jnp.bfloat16), "ctx").astype(jnp.float32),
    )
    return (
        output,
        grad_input,
        shares[0],
        shares[1],
        shares[2],
        shares[3],
        shares[4],
        shares[5],
        shares[6],
        shares[7],
        shares[8],
    )


BF = jnp.bfloat16
F32 = jnp.float32
I32 = jnp.int32
MESH = pl.DeviceIdType.MESH
BLOCK = 256
VMEM_BYTES = 67043328
ORDER = (
    93, 92, 99, 74, 80, 121, 86, 98, 0, 95, 77, 75, 87, 83, 89, 96, 78, 104, 101, 81, 90, 79, 97, 84,
    3, 108, 6, 76, 114, 91, 85, 94, 2, 105, 127, 133, 7, 111, 8, 88, 102, 109, 82, 9, 139, 106, 120, 1,
    117, 132, 50, 123, 112, 107, 103, 115, 100, 54, 118, 144, 55, 56, 51, 113, 4, 124, 57, 126, 119, 58, 138, 110,
    10, 125, 135, 129, 136, 5, 116, 140, 12, 122, 29, 141, 28, 37, 130, 36, 137, 11, 30, 145, 38, 13, 142, 31,
    131, 39, 42, 134, 146, 14, 204, 128, 205, 40, 35, 143, 171, 147, 64, 34, 65, 66, 43, 33, 149, 161, 41, 67,
    32, 172, 15, 68, 162, 44, 46, 152, 16, 166, 59, 60, 173, 18, 206, 163, 45, 47, 61, 167, 153, 150, 52, 156,
    17, 207, 62, 208, 164, 160, 174, 63, 176, 170, 168, 19, 53, 22, 157, 21, 209, 177, 69, 48, 169, 214, 70, 218,
    210, 71, 20, 215, 158, 49, 72, 178, 211, 73, 181, 151, 159, 155, 191, 186, 182, 196, 179, 192, 165, 175, 219, 23,
    187, 212, 154, 183, 216, 200, 197, 148, 220, 213, 217, 188, 184, 201, 180, 193, 198, 221, 202, 189, 185, 194, 190, 203,
    24, 199, 195, 25, 26, 27,
)
SEMS = (32, 164, 15)


def dot_nn(left, right):
    return jnp.dot(left, right, preferred_element_type=F32)


def dot_nt(left, right):
    return lax.dot_general(left, right, (((1,), (1,)), ((), ())), preferred_element_type=F32)


def dot_tn(left, right):
    return lax.dot_general(left, right, (((0,), (0,)), ((), ())), preferred_element_type=F32)


def loop(count, body):
    def step(index, carry):
        body(index)
        return carry

    lax.fori_loop(0, count, step, 0)


def tile(index, size):
    return pl.ds(pl.multiple_of(index * size, size), size)


def only_half(values, half):
    lane = lax.broadcasted_iota(I32, values.shape, 1)
    keep = (lane < HEAD_DIM) if half == 0 else (lane >= HEAD_DIM)
    return jnp.where(keep, values, jnp.zeros_like(values))


def write_bias(bias, seg_col, seg_row, block, length):
    lanes = tile(block, BLOCK)
    keys = seg_col[0:length, :]
    key_pos = lax.broadcasted_iota(I32, (length, BLOCK), 0)
    query_pos = lax.broadcasted_iota(I32, (length, BLOCK), 1) + block * BLOCK
    same = jnp.concatenate([keys, keys], axis=1) == seg_row[0:1, lanes]
    bias[0:length, :] = jnp.where(same & (key_pos <= query_pos), 0.0, MASKED)


def attend_block(block, length, pairs, query, keys, vals_t, bias, seg_col, seg_row, mixed, mixed_t, log_sum):
    write_bias(bias, seg_col, seg_row, block, length)
    rows = tile(block, BLOCK)

    def pair(index):
        cols = tile(index, 2 * HEAD_DIM)
        two = query[rows, cols]
        for half in (0, 1):
            scores = dot_nt(keys[0:length, cols], only_half(two, half)) + bias[0:length, :]
            top = jnp.max(scores, axis=0, keepdims=True)
            expo = jnp.exp(scores - top)
            total = jnp.sum(expo, axis=0, keepdims=True)
            log_sum[2 * index + half, :, rows] = jnp.broadcast_to(top + jnp.log(total), (8, BLOCK))
            probs = (expo * (1.0 / total)).astype(BF)
            head = tile(2 * index + half, HEAD_DIM)
            mixed_t[head, :] = dot_nn(vals_t[head, 0:length], probs)

    loop(pairs, pair)
    mixed[rows, :] = mixed_t[...].T.astype(BF)


def attend_back_block(
    block, length, pairs, query, keys, keys_t, vals, grad_mixed, bias, seg_col, seg_row, log_sum, grad_qkv, grad_q_t, grad_k, grad_v
):
    write_bias(bias, seg_col, seg_row, block, length)
    rows = tile(block, BLOCK)

    def pair(index):
        cols = tile(index, 2 * HEAD_DIM)
        two = query[rows, cols]
        grad_two = grad_mixed[rows, cols]
        for half in (0, 1):
            one = only_half(two, half)
            grad_one = only_half(grad_two, half)
            scores = dot_nt(keys[0:length, cols], one) + bias[0:length, :]
            probs = jnp.exp(scores - log_sum[2 * index + half, 0:1, rows])
            grad_probs = dot_nt(vals[0:length, cols], grad_one)
            delta = jnp.sum(probs * grad_probs, axis=0, keepdims=True)
            grad_scores = (probs * (grad_probs - delta)).astype(BF)
            grad_v[0:length, cols] += dot_nn(probs.astype(BF), grad_one)
            grad_k[0:length, cols] += dot_nn(grad_scores, one)
            head = tile(2 * index + half, HEAD_DIM)
            grad_q_t[head, :] = dot_nn(keys_t[head, 0:length], grad_scores)

    loop(pairs, pair)
    grad_qkv[rows, 0 : grad_q_t.shape[0]] = (grad_q_t[...].T * SCALE).astype(BF)


def layer_kernel(
    nz,
    tok, cot, seg, gain_a, gain_f, w_q, w_k, w_v, w_o, w_g, w_u, w_d,
    out, g_tok, o_q, o_k, o_v, o_o, o_g, o_u, o_d, o_gain,
    xg, cg, seg_row, own_gains, gain_all, wqkv, wo, wg, wu, wd,
    h1, h2, ab, query, keys, vals, keys_t, vals_t, mixed, grad_mixed, grad_qkv, grad_k, grad_v,
    act_g, act_u, act_m, y1, bias, mixed_t, log_sum, seg_col,
    part, pair_sum, from_core, from_y, final_rows,
    p_d0, p_d1, p_g0, p_g1, p_u0, p_u1, p_o, p_q, p_k, p_v, r_d0, r_d1, r_g0, r_g1, r_u0, r_u1, r_o, r_q, r_k, r_v,
    s_d0, s_d1, s_g0, s_g1, s_u0, s_u1, s_o, s_q, s_k, s_v,
    p_n, r_n, s_n, f_n, c_n, y_n,
    send_sems, recv_sems, local_sems,
):
    fs = lax.axis_index("fsdp")
    y = lax.axis_index("ctx")
    t = lax.axis_index("tp")
    z = fs // 2
    x = lax.rem(fs, 2)
    width = xg.shape[1]
    half_len = xg.shape[0] // 2
    quarter = half_len // 2
    heads_w = query.shape[1]
    hidden = act_m.shape[1]
    db = width // (2 * nz)

    def dev(fq, yq, tq):
        return {"fsdp": fq, "ctx": yq, "tp": tq}

    x_dev = dev(2 * z + (1 - x), y, t)
    y_dev = dev(fs, 1 - y, t)
    c_dev = dev(fs, y, 1 - t)

    def z_from(k):
        return lax.rem(z + nz - k, nz)

    z_next = dev(2 * lax.rem(z + 1, nz) + x, y, t)

    barrier = pltpu.get_barrier_semaphore()
    z_prev = dev(2 * z_from(1) + x, y, t)
    for peer in (x_dev, y_dev, c_dev, z_next, z_prev):
        pl.semaphore_signal(barrier, inc=1, device_id=peer, device_id_type=MESH)
    own_gain_copies = [
        pltpu.make_async_copy(src, own_gains.at[i], local_sems.at[SEMS[2] - 1 - i]) for i, src in enumerate((gain_a, gain_f))
    ]
    for copy in own_gain_copies:
        copy.start()
    pl.semaphore_wait(barrier, 5)

    count = {"send": 0, "recv": 0, "local": 0}
    sent = []

    def new(kind):
        count[kind] += 1
        return count[kind] - 1

    slots = [None] * SEMS[0]

    def send(src, dst, device, ridx):
        slot = new("send") % SEMS[0]
        if slots[slot] is not None:
            drain([copy for copy in sent if copy is slots[slot]])
        copy = pltpu.make_async_remote_copy(
            src, dst, send_sems.at[slot], recv_sems.at[ridx], device_id=device, device_id_type=MESH
        )
        slots[slot] = copy
        copy.start()
        sent.append(copy)
        return copy

    def recv(dst, ridx):
        pltpu.make_async_remote_copy(
            dst, dst, send_sems.at[0], recv_sems.at[ridx], device_id=y_dev, device_id_type=MESH
        ).wait_recv()

    def local(src, dst):
        copy = pltpu.make_async_copy(src, dst, local_sems.at[new("local")])
        copy.start()
        return copy

    def many(number):
        return [new("recv") for _ in range(number)]

    def drain(copies):
        left = [copy for copy in sent if any(copy is other for other in copies)]
        for copy in left:
            copy.wait_send()
        sent[:] = [copy for copy in sent if not any(copy is other for other in left)]

    hw = pl.ds(pl.multiple_of(y * heads_w, heads_w), heads_w)

    def rb(fq):
        return tile(fq, db)

    part_h = hidden // 2
    first, second = slice(0, part_h), slice(part_h, hidden)

    def half_of(half, yq):
        return pl.ds(pl.multiple_of(yq * hidden + half * part_h, part_h), part_h)

    names = {
        "n": (gain_all.at[fs], lambda fq: gain_all.at[fq], False),
        "q": (w_q.at[:, hw], lambda fq: wqkv.at[rb(fq), 0:heads_w], False),
        "k": (w_k.at[:, hw], lambda fq: wqkv.at[rb(fq), heads_w : 2 * heads_w], False),
        "v": (w_v.at[:, hw], lambda fq: wqkv.at[rb(fq), 2 * heads_w : 3 * heads_w], False),
        "o": (w_o.at[hw, :], lambda fq: wo.at[:, rb(fq)], True),
    }
    for i, units in enumerate((first, second)):
        mine = half_of(i, y)
        names[f"g{i}"] = (w_g.at[:, mine], lambda fq, units=units: wg.at[rb(fq), units], False)
        names[f"u{i}"] = (w_u.at[:, mine], lambda fq, units=units: wu.at[rb(fq), units], False)
        names[f"d{i}"] = (w_d.at[mine, :], lambda fq, units=units: wd.at[units, rb(fq)], i == 1)
    together = {"n": gain_all.at[0:nz]}
    for i, name in enumerate(("q", "k", "v")):
        together[name] = wqkv.at[0 : nz * db, i * heads_w : (i + 1) * heads_w]
    for i, units in enumerate((first, second)):
        together[f"g{i}"] = wg.at[0 : nz * db, units]
        together[f"u{i}"] = wu.at[0 : nz * db, units]
        together[f"d{i}"] = wd.at[units, 0 : nz * db]
    ring_own = {name: [None] + many(nz - 1) for name in names}
    ring_other = {name: [None] + many(nz - 1) for name in names if names[name][2]}
    over_x = {name: many(1) * nz for name in names}
    own_copy = {}

    def start_z(name):
        src, place, _ = names[name]
        if name != "n":
            own_copy[name] = local(src, place(fs))
        else:
            for i, copy in enumerate(own_gain_copies):
                copy.wait()
                gain_all[fs, i : i + 1, :] = own_gains[i].astype(F32)
        send(src, place(fs), z_next, ring_own[name][1])

    def start_x(name):
        src, place, _ = names[name]
        send(src, place(fs), x_dev, over_x[name][0])

    def relay(name, k):
        place, pair_first = names[name][1:]
        block = place(2 * z_from(k) + x)
        recv(block, ring_own[name][k])
        if k < nz - 1:
            send(block, block, z_next, ring_own[name][k + 1])
        if not pair_first:
            send(block, block, x_dev, over_x[name][k])

    def relay_other(name, k):
        block = names[name][1](2 * z_from(k) + (1 - x))
        recv(block, over_x[name][0] if k == 0 else ring_other[name][k])
        if k < nz - 1:
            send(block, block, z_next, ring_other[name][k + 1])

    def arrived(name):
        place, pair_first = names[name][1:]
        if name != "n":
            own_copy[name].wait()
        if not pair_first:
            recv(together[name], over_x[name][0])

    def rows_of(yq, tq):
        return pl.ds(pl.multiple_of(yq * half_len + tq * quarter, quarter), quarter)

    own_rows = rows_of(y, t)

    tok_y, tok_c, cot_y, cot_c, seg_y = many(5)
    seg_local = local(seg, seg_row.at[:, tile(y, half_len)])
    send(seg, seg_row.at[:, tile(y, half_len)], y_dev, seg_y)
    tok_local = local(tok, xg.at[tile(y, half_len), :])
    cot_local = local(cot, cg.at[tile(y, half_len), :])

    far = rows_of(1 - y, t)
    far_other = rows_of(1 - y, 1 - t)

    def core_forward(ref, y_idx, c_idx):
        recv(ref.at[far, :], y_idx)
        return send(ref.at[far, :], ref.at[far, :], c_dev, c_idx)

    kinds = {"a": 0, "out": 0, "dh2": 1, "dh1": 1}
    ex_recv = {name: many(3) for name in kinds}
    ex_sent = []

    def exchange(name, compute, stage):
        e = kinds[name]
        if stage == 0:
            drain(ex_sent)
            ex_sent.clear()
            compute(far_other, part.at[0])
            ex_sent.append(send(part.at[0], from_core.at[e, 0], c_dev, ex_recv[name][0]))
        elif stage == 1:
            compute(far, part.at[1])
        elif stage == 2:
            recv(from_core.at[e, 0], ex_recv[name][0])

            def add(i):
                r = tile(i, 32)
                pair_sum[r, :] = (part[1, r, :].astype(F32) + from_core[e, 0, r, :].astype(F32)).astype(BF)

            loop(quarter // 32, add)
            ex_sent.append(send(pair_sum, from_y.at[e], y_dev, ex_recv[name][2]))
        elif stage == 3:
            compute(rows_of(y, 1 - t), part.at[2])
            ex_sent.append(send(part.at[2], from_core.at[e, 1], c_dev, ex_recv[name][1]))
        elif stage == 4:
            compute(own_rows, part.at[3])
        else:
            recv(from_core.at[e, 1], ex_recv[name][1])
            recv(from_y.at[e], ex_recv[name][2])

    def total_of(name, r):
        e = kinds[name]
        return part[3, r, :].astype(F32) + from_core[e, 1, r, :].astype(F32) + from_y[e, r, :].astype(F32)

    def spread_rows(ref, idx):
        return [
            send(ref.at[own_rows, :], ref.at[own_rows, :], c_dev, idx[0]),
            send(ref.at[own_rows, :], ref.at[own_rows, :], y_dev, idx[1]),
        ]

    h2_idx = many(3)
    ab_idx = many(3)

    grads = {
        "d0": (p_d0, r_d0, s_d0, None, True),
        "d1": (p_d1, r_d1, s_d1, None, False),
        "g0": (p_g0, r_g0, s_g0, None, False),
        "g1": (p_g1, r_g1, s_g1, None, False),
        "u0": (p_u0, r_u0, s_u0, None, False),
        "u1": (p_u1, r_u1, s_u1, None, False),
        "o": (p_o, r_o, s_o, None, False),
        "q": (p_q, r_q, s_q, None, False),
        "k": (p_k, r_k, s_k, None, False),
        "v": (p_v, r_v, s_v, None, False),
        "n": (p_n, r_n, s_n, f_n, False),
    }
    gx = {name: [None] + many(1 if item[4] else nz) for name, item in grads.items()}
    gz = {name: [[None] + many(nz - 1) for _ in range(2 if item[4] else 1)] for name, item in grads.items()}

    def add_rows(rows, cols, body):
        step = min(rows, 16 if cols > 512 else 128)
        loop(rows // step, lambda i: body(tile(i, step)))

    def grad_send(name, k):
        p, r, s, _, ring_first = grads[name]
        if ring_first:
            send(p.at[lax.rem(x + k, 2), z_from(1)], s.at[k - 1, 0], z_next, gz[name][k - 1][1])
        else:
            send(p.at[1 - x, z_from(k)], r.at[k - 1], x_dev, gx[name][k])

    def grad_step(name, k):
        p, r, s, f, ring_first = grads[name]
        f = place_of(name, y) if f is None else f
        if ring_first:
            c, k = divmod(k, 10)
            xq = lax.rem(x + 1 + c, 2)
            recv(s.at[c, k - 2], gz[name][c][k - 1])
            last_own = k == nz and c == 1
            if last_own:
                recv(r.at[0], gx[name][1])

            def add_ring(rr):
                total = p[xq, z_from(k), rr, :].astype(F32) + s[c, k - 2, rr, :].astype(F32)
                if last_own:
                    f[rr, :] = (total + r[0, rr, :].astype(F32)).astype(p.dtype)
                else:
                    p[xq, z_from(k), rr, :] = total.astype(p.dtype)

            add_rows(*p.shape[2:], add_ring)
            if k < nz:
                send(p.at[xq, z_from(k)], s.at[c, k - 1], z_next, gz[name][c][k])
            elif c == 0:
                send(p.at[xq, z_from(k)], r.at[0], x_dev, gx[name][1])
            return
        zq = z_from(k)
        recv(r.at[k - 1], gx[name][k])
        if k > 1:
            recv(s.at[0, k - 2], gz[name][0][k - 1])

        def add(rr):
            total = p[x, zq, rr, :].astype(F32) + r[k - 1, rr, :].astype(F32)
            if k > 1:
                total = total + s[0, k - 2, rr, :].astype(F32)
            if k < nz:
                p[x, zq, rr, :] = total.astype(p.dtype)
            else:
                f[rr, :] = total.astype(p.dtype)

        add_rows(*p.shape[2:], add)
        if k < nz:
            send(p.at[x, zq], s.at[0, k - 1], z_next, gz[name][0][k])

    def place_of(name, yq):
        h = pl.ds(pl.multiple_of(yq * heads_w, heads_w), heads_w)
        if name[0] == "d":
            return o_d.at[half_of(int(name[1]), yq), :]
        if name == "o":
            return o_o.at[h, :]
        wide = {"g": o_g, "u": o_u}
        if name[0] in wide:
            return wide[name[0]].at[:, half_of(int(name[1]), yq)]
        return {"q": o_q, "k": o_k, "v": o_v}[name].at[:, h]

    out_idx = {name: many(1)[0] for name in grads if name != "n"}

    def grad_end(name):
        send(place_of(name, y), place_of(name, y), y_dev, out_idx[name])

    def grad_done(name):
        recv(place_of(name, 1 - y), out_idx[name])

    value = {}
    blocks = half_len // BLOCK
    pairs = heads_w // (2 * HEAD_DIM)
    out_c, gtok_c = many(2)
    n_c, n_y = many(2)
    my_rows = tile(t, quarter)
    other_rows = tile(1 - t, quarter)
    row_sends = []

    def send_tok():
        send(tok.at[tile(t, quarter), :], xg.at[own_rows, :], y_dev, tok_y)

    def send_cot():
        send(cot.at[tile(t, quarter), :], cg.at[own_rows, :], y_dev, cot_y)

    def gather_gains():
        value["one"] = jnp.concatenate([gain_all[i, 0:1, :] for i in range(2 * nz)], axis=1)
        value["two"] = jnp.concatenate([gain_all[i, 1:2, :] for i in range(2 * nz)], axis=1)

    def norm_rows(start):
        gain_one = value["one"]

        def body(i):
            r = pl.ds(pl.multiple_of(start + i * 32, 32), 32)
            values = xg[r, :].astype(F32)
            inverse = lax.rsqrt(jnp.mean(values * values, axis=-1, keepdims=True) + EPSILON)
            h1[r, :] = (values * inverse * gain_one).astype(BF)

        loop(half_len // 32, body)

    def norm_own():
        tok_local.wait()
        norm_rows(y * half_len)

    def norm_far():
        recv(xg.at[far_other, :], tok_c)
        norm_rows((1 - y) * half_len)

    def segments():
        seg_local.wait()
        recv(seg_row.at[:, tile(1 - y, half_len)], seg_y)
        seg_col[...] = jnp.broadcast_to(seg_row[0:1, :], (128, 2 * half_len)).T

    def project():
        def body(i):
            r = tile(i, 512)
            rows = h1[r, :]
            query[r, :] = (dot_nn(rows, wqkv[:, 0:heads_w]).astype(BF).astype(F32) * SCALE).astype(BF)
            keys[r, :] = dot_nn(rows, wqkv[:, heads_w : 2 * heads_w]).astype(BF)
            vals[r, :] = dot_nn(rows, wqkv[:, 2 * heads_w : 3 * heads_w]).astype(BF)

        loop(xg.shape[0] // 512, body)
        keys_t[...] = keys[...].T
        vals_t[...] = vals[...].T

    def either(half, body):
        @pl.when(half == 0)
        def _():
            body(half_len)

        @pl.when(half == 1)
        def _():
            body(2 * half_len)

    def attend(half):
        def block(i):
            args = (pairs, query, keys, vals_t, bias, seg_col, seg_row, mixed, mixed_t, log_sum)
            either(half, lambda length: attend_block(half * blocks + i, length, *args))

        loop(blocks, block)

    def out_rows(r, dst):
        dst[...] = dot_nn(mixed[r, :], wo[...]).astype(BF)

    def first_residual():
        exchange("a", None, 5)
        gain_two = value["two"]

        def body(i):
            r = tile(i, 32)
            rr = pl.ds(pl.multiple_of(y * half_len + t * quarter + i * 32, 32), 32)
            values = xg[rr, :].astype(F32) + total_of("a", r)
            y1[r, :] = values
            inverse = lax.rsqrt(jnp.mean(values * values, axis=-1, keepdims=True) + EPSILON)
            h2[rr, :] = (values * inverse * gain_two).astype(BF)

        loop(quarter // 32, body)
        row_sends.extend(spread_rows(h2, h2_idx))

    def gate(half, r):
        rows = h2[r, :]

        def cols(j):
            c = pl.ds(pl.multiple_of(half * part_h + j * 256, 256), 256)
            g = dot_nn(rows, wg[:, c])
            u = dot_nn(rows, wu[:, c])
            sg = 1.0 / (1.0 + jnp.exp(-g))
            gs = g * sg
            act_u[r, c] = gs.astype(BF)
            act_g[r, c] = (u * sg * (1.0 + g * (1.0 - sg))).astype(BF)
            act_m[r, c] = (gs * u).astype(BF)

        loop(part_h // 256, cols)

    def grad_cols(left, start, right, p, index):
        c = tile(index, 2 * db)
        for i in range(p.shape[2] // 256):
            r = slice(start + i * 256, start + (i + 1) * 256)
            both = dot_tn(left[:, r], right[:, c]).astype(BF)
            rows = slice(i * 256, (i + 1) * 256)
            p[0, index, rows, :] = both[:, 0:db]
            p[1, index, rows, :] = both[:, db : 2 * db]

    def grad_rows(left, right, units, p, index):
        c = tile(index, 2 * db)
        both = dot_tn(left[:, c], right[:, units]).astype(BF)
        p[0, index] = both[0:db, :]
        p[1, index] = both[db : 2 * db, :]

    def grad_down(part_of, p):
        loop(nz, lambda i: grad_cols(act_m, part_of * part_h, cg, p, i))

    def some_blocks(name, left, right, units, ks):
        p = grads[name][0]
        loop(len(ks), lambda i: grad_rows(left, right, units, p, z_from(ks[0] + i)))
        for k in ks:
            grad_send(name, k)

    def qkv_blocks(ks):
        def body(i):
            index = z_from(ks[0] + i)
            both = dot_tn(h1[:, tile(index, 2 * db)], grad_qkv[...]).astype(BF)
            for j, p in enumerate((p_q, p_k, p_v)):
                c = slice(j * heads_w, (j + 1) * heads_w)
                p[0, index] = both[0:db, c]
                p[1, index] = both[db : 2 * db, c]

        loop(len(ks), body)

    def hidden_back(half, r, dst):
        rows = cg[r, :]
        units = (first, second)[half]

        def cols(j):
            c = pl.ds(pl.multiple_of(half * part_h + j * 256, 256), 256)
            dm = dot_nt(rows, wd[c, :])
            act_g[r, c] = (dm * act_g[r, c].astype(F32)).astype(BF)
            act_u[r, c] = (dm * act_u[r, c].astype(F32)).astype(BF)

        loop(part_h // 256, cols)

        def back(j):
            c = tile(j, 512)
            total = dot_nt(act_g[r, units], wg[c, units]) + dot_nt(act_u[r, units], wu[c, units])
            if half == 0:
                ab[r, c] = total.astype(BF)
            else:
                dst[:, c] = (total + ab[r, c].astype(F32)).astype(BF)

        loop(width // 512, back)

    def second_residual():
        exchange("dh2", None, 5)
        gain_two = value["two"]

        def body(i, carry):
            r = tile(i, 32)
            rr = pl.ds(pl.multiple_of(y * half_len + t * quarter + i * 32, 32), 32)
            values = y1[r, :]
            inverse = lax.rsqrt(jnp.mean(values * values, axis=-1, keepdims=True) + EPSILON)
            normed = values * inverse
            grad = total_of("dh2", r)
            scaled = grad * gain_two
            mean = jnp.mean(scaled * normed, axis=-1, keepdims=True)
            full = cg[rr, :].astype(F32) + inverse * (scaled - normed * mean)
            final_rows[r, :] = full
            ab[rr, :] = full.astype(BF)
            return carry + jnp.sum(grad * normed, axis=0, keepdims=True)

        value["grad_two"] = lax.fori_loop(0, quarter // 32, body, jnp.zeros((1, width), F32))
        row_sends.extend(spread_rows(ab, ab_idx))

    def down_rows(r, dst):
        def cols(j):
            c = tile(j, 512)
            dst[:, c] = dot_nn(act_m[r, :], wd[:, c]).astype(BF)

        loop(width // 512, cols)

    def mixed_back(half):
        r = tile(half, half_len)
        grad_mixed[r, :] = dot_nt(ab[r, :], wo[...]).astype(BF)

    def clear_sums():
        grad_k[...] = jnp.zeros_like(grad_k)
        grad_v[...] = jnp.zeros_like(grad_v)

    def attend_back(half):
        def block(i):
            args = (
                pairs, query, keys, keys_t, vals, grad_mixed, bias, seg_col, seg_row, log_sum, grad_qkv, mixed_t, grad_k, grad_v,
            )
            either(half, lambda length: attend_back_block(half * blocks + i, length, *args))

        loop(blocks, block)

    def own_back():
        recv(ab.at[rows_of(y, 1 - t), :], ab_idx[0])
        clear_sums()
        mixed_back(y)

    def far_back():
        recv(ab.at[far_other, :], ab_idx[2])
        mixed_back(1 - y)

    def grad_out_all():
        loop(nz, lambda i: grad_cols(mixed, 0, ab, p_o, i))
        for k in range(1, nz + 1):
            grad_send("o", k)

    def sums_to_bf16():
        grad_qkv[:, heads_w : 2 * heads_w] = grad_k[...].astype(BF)
        grad_qkv[:, 2 * heads_w : 3 * heads_w] = grad_v[...].astype(BF)

    def hidden_one_back(r, dst):
        def cols(j):
            c = tile(j, 512)
            dst[:, c] = dot_nt(grad_qkv[r, :], wqkv[c, :]).astype(BF)

        loop(width // 512, cols)

    def finish_out():
        exchange("out", None, 5)

        def body(i):
            r = tile(i, 32)
            out[pl.ds(pl.multiple_of(t * quarter + i * 32, 32), 32), :] = (y1[r, :] + total_of("out", r)).astype(BF)

        loop(quarter // 32, body)
        send(out.at[my_rows, :], out.at[my_rows, :], c_dev, out_c)

    def finish_tokens():
        exchange("dh1", None, 5)
        gain_one = value["one"]

        def body(i, carry):
            r = tile(i, 32)
            rr = pl.ds(pl.multiple_of(y * half_len + t * quarter + i * 32, 32), 32)
            values = xg[rr, :].astype(F32)
            inverse = lax.rsqrt(jnp.mean(values * values, axis=-1, keepdims=True) + EPSILON)
            normed = values * inverse
            grad = total_of("dh1", r)
            scaled = grad * gain_one
            mean = jnp.mean(scaled * normed, axis=-1, keepdims=True)
            full = final_rows[r, :] + inverse * (scaled - normed * mean)
            g_tok[pl.ds(pl.multiple_of(t * quarter + i * 32, 32), 32), :] = full.astype(BF)
            return carry + jnp.sum(grad * normed, axis=0, keepdims=True)

        gain_one_grad = lax.fori_loop(0, quarter // 32, body, jnp.zeros((1, width), F32))
        for i in range(2 * nz):
            c = slice(i * db, (i + 1) * db)
            p_n[i % 2, i // 2] = jnp.concatenate(
                [gain_one_grad[:, c], value["grad_two"][:, c], jnp.zeros((6, db), F32)], axis=0
            )
        for k in range(1, nz + 1):
            grad_send("n", k)
        send(g_tok.at[my_rows, :], g_tok.at[my_rows, :], c_dev, gtok_c)

    def gains_core():
        send(f_n, c_n, c_dev, n_c)

    def gains_y():
        recv(c_n, n_c)
        y_n[0] = f_n[...] + c_n[...]
        send(y_n.at[0], y_n.at[1], y_dev, n_y)

    def gains_end():
        recv(y_n.at[1], n_y)
        o_gain[...] = y_n[0] + y_n[1]

    def finish():
        for name in out_idx:
            grad_done(name)
        recv(out.at[other_rows, :], out_c)
        recv(g_tok.at[other_rows, :], gtok_c)
        drain(list(sent))

    two = (1, 2), (3, 4)
    tasks = [
        send_tok,
        send_cot,
        gather_gains,
        lambda: core_forward(xg, tok_y, tok_c),
        lambda: core_forward(cg, cot_y, cot_c),
        lambda: (cot_local.wait(), recv(cg.at[far_other, :], cot_c)),
        segments,
        norm_own,
        norm_far,
        project,
        first_residual,
        lambda: row_sends.append(core_forward(h2, h2_idx[1], h2_idx[2])),
        lambda: recv(h2.at[rows_of(y, 1 - t), :], h2_idx[0]),
        lambda: recv(h2.at[far_other, :], h2_idx[2]),
        lambda: grad_down(0, p_d0),
        lambda: grad_down(1, p_d1),
        second_residual,
        lambda: row_sends.append(core_forward(ab, ab_idx[1], ab_idx[2])),
        own_back,
        far_back,
        grad_out_all,
        sums_to_bf16,
        finish_out,
        finish_tokens,
        gains_core,
        gains_y,
        gains_end,
        finish,
    ]
    all_rows = (own_rows, rows_of(y, 1 - t), far, far_other)
    tasks += [functools.partial(gate, half, r) for half in (0, 1) for r in all_rows]
    tasks += [functools.partial(hidden_back, 0, r, None) for r in all_rows]
    for i, units in enumerate((first, second)):
        tasks += [functools.partial(some_blocks, f"g{i}", h2, act_g, units, ks) for ks in two]
        tasks += [functools.partial(some_blocks, f"u{i}", h2, act_u, units, ks) for ks in two]
    tasks += [functools.partial(qkv_blocks, ks) for ks in two]
    tasks += [functools.partial(attend, half) for half in (1 - y, y)]
    tasks += [functools.partial(attend_back, half) for half in (y, 1 - y)]
    for name, compute in zip(kinds, (out_rows, down_rows, functools.partial(hidden_back, 1), hidden_one_back)):
        tasks += [functools.partial(exchange, name, compute, i) for i in range(5)]
    for name in names:
        tasks += [functools.partial(start_z, name), functools.partial(start_x, name), functools.partial(arrived, name)]
        tasks += [functools.partial(relay, name, k) for k in range(1, nz)]
        if names[name][2]:
            tasks += [functools.partial(relay_other, name, k) for k in range(nz)]
    for name in grads:
        if name in out_idx:
            tasks.append(functools.partial(grad_end, name))
        if grads[name][4]:
            tasks += [functools.partial(grad_step, name, 10 * c + k) for c in (0, 1) for k in range(2, nz + 1)]
        else:
            tasks += [functools.partial(grad_step, name, k) for k in range(1, nz + 1)]
    for name in ("d0", "d1", "q", "k", "v"):
        tasks += [functools.partial(grad_send, name, k) for k in ((1, 2) if grads[name][4] else range(1, nz + 1))]
    assert sorted(ORDER) == list(range(len(tasks)))
    for index in ORDER:
        tasks[index]()


def fused(nz, tokens, segment_ids, w_query, w_key, w_value, w_out, w_gate, w_up, w_down, gain_attn, gain_ffn, cotangent):
    half_len, _, width = tokens.shape
    length = 2 * half_len
    quarter = half_len // 2
    heads_w = w_query.shape[1] // 2
    hidden = w_gate.shape[1] // 2
    db = w_query.shape[0]
    heads = heads_w // HEAD_DIM
    gains = (gain_attn.reshape(1, db), gain_ffn.reshape(1, db))

    def vm(*shape, dtype=BF):
        return pltpu.VMEM(shape, dtype)

    shape_d, shape_g, shape_o, shape_q = (hidden // 2, db), (db, hidden // 2), (heads_w, db), (db, heads_w)
    shapes = (shape_d, shape_d, *[shape_g] * 4, shape_o, shape_q, shape_q, shape_q)
    ring_first = (True, *[False] * 9)
    scratch = [
        vm(length, width), vm(length, width), vm(1, length, dtype=I32), vm(2, 1, db), vm(2 * nz, 2, db, dtype=F32),
        vm(width, 3 * heads_w), vm(heads_w, width), vm(width, hidden), vm(width, hidden), vm(hidden, width),
        vm(length, width), vm(length, width), vm(length, width),
        vm(length, heads_w), vm(length, heads_w), vm(length, heads_w), vm(heads_w, length), vm(heads_w, length),
        vm(length, heads_w), vm(length, heads_w), vm(length, 3 * heads_w),
        vm(length, heads_w, dtype=F32), vm(length, heads_w, dtype=F32),
        vm(length, hidden), vm(length, hidden), vm(length, hidden),
        vm(quarter, width, dtype=F32), vm(length, BLOCK, dtype=F32), vm(heads_w, BLOCK, dtype=F32),
        vm(heads, 8, length, dtype=F32), vm(length, 128, dtype=I32),
        vm(4, quarter, width), vm(quarter, width), vm(2, 2, quarter, width), vm(2, quarter, width),
        vm(quarter, width, dtype=F32),
    ]
    scratch += [vm(2, nz, *shape) for shape in shapes]
    scratch += [vm(1 if first else nz, *shape) for shape, first in zip(shapes, ring_first)]
    scratch += [vm(2 if first else 1, nz - 1, *shape) for shape, first in zip(shapes, ring_first)]
    scratch += [
        vm(2, nz, 8, db, dtype=F32), vm(nz, 8, db, dtype=F32), vm(1, nz - 1, 8, db, dtype=F32), vm(8, db, dtype=F32),
        vm(8, db, dtype=F32), vm(2, 8, db, dtype=F32),
    ]
    scratch += [pltpu.SemaphoreType.DMA((SEMS[0],)), pltpu.SemaphoreType.DMA((SEMS[1],)), pltpu.SemaphoreType.DMA((SEMS[2],))]
    anywhere = pl.BlockSpec(memory_space=pl.ANY)
    weights = (w_query, w_key, w_value, w_out, w_gate, w_up, w_down)
    results_bytes = (9 << 19) - (1 << 16)
    results = pl.pallas_call(
        functools.partial(layer_kernel, nz),
        out_shape=[pltpu.VMEM((half_len, width), BF)] * 2
        + [pltpu.VMEM(item.shape, BF) for item in weights]
        + [pltpu.VMEM((8, db), F32)],
        in_specs=[anywhere] * 12,
        out_specs=[pl.BlockSpec(memory_space=pltpu.VMEM)] * 10,
        scratch_shapes=scratch,
        compiler_params=pltpu.CompilerParams(
            collective_id=0, has_side_effects=True, vmem_limit_bytes=VMEM_BYTES - results_bytes
        ),
        name="layer",
    )(tokens.reshape(half_len, width), cotangent.reshape(half_len, width), segment_ids, *gains, *weights)
    bodies = results[:9]
    wide = [jax.ShapeDtypeStruct(item.shape, BF if i < 2 else F32) for i, item in enumerate(bodies)]

    def widen(*refs):
        srcs, rows, dsts = refs[:9], refs[9], refs[10:21]
        finals, store_sems = refs[21:28], refs[28]
        stores = []

        def put(src, dst):
            stores.append(pltpu.make_async_copy(src, dst, store_sems.at[len(stores)]))
            stores[-1].start()

        for i in (0, 1):
            put(srcs[i], dsts[i])
            put(rows.at[i : i + 1, :], dsts[9 + i])
        for i in (*range(6, 9), *range(2, 6)):
            finals[i - 2][...] = srcs[i][...].astype(F32)
            put(finals[i - 2], dsts[i])
        for copy in stores:
            copy.wait()

    finals = pl.pallas_call(
        widen,
        out_shape=wide + [jax.ShapeDtypeStruct((1, db), F32)] * 2,
        in_specs=[pl.BlockSpec(memory_space=pltpu.VMEM)] * 10,
        out_specs=[anywhere] * 11,
        scratch_shapes=[vm(*item.shape, dtype=F32) for item in wide[2:]]
        + [pltpu.SemaphoreType.DMA((11,))],
        compiler_params=pltpu.CompilerParams(vmem_limit_bytes=16 << 20),
        name="widen",
    )(*results)
    shape = tokens.shape
    return (finals[0].reshape(shape), finals[1].reshape(shape), *finals[2:9], finals[9].reshape(db), finals[10].reshape(db))


def fits(mesh, tokens_shape):
    return mesh.shape["fsdp"] == 8 and mesh.shape["ctx"] == 2 and mesh.shape["tp"] == 2 and tokens_shape[1:] == (1, 1024)


def solution(mesh):
    def step(tokens, *rest):
        if fits(mesh, tokens.shape):
            return fused(mesh.shape["fsdp"] // 2, tokens, *rest)
        return local(tokens, *rest)

    return jax.shard_map(
        step,
        mesh=mesh,
        in_specs=(
            P("ctx", "fsdp", None),
            P("fsdp", "ctx"),
            P("fsdp", "tp"),
            P("fsdp", "tp"),
            P("fsdp", "tp"),
            P("tp", "fsdp"),
            P("fsdp", "tp"),
            P("fsdp", "tp"),
            P("tp", "fsdp"),
            P("fsdp"),
            P("fsdp"),
            P("ctx", "fsdp", None),
        ),
        out_specs=(
            P("ctx", "fsdp", None),
            P("ctx", "fsdp", None),
            P("fsdp", "tp"),
            P("fsdp", "tp"),
            P("fsdp", "tp"),
            P("tp", "fsdp"),
            P("fsdp", "tp"),
            P("fsdp", "tp"),
            P("tp", "fsdp"),
            P("fsdp"),
            P("fsdp"),
        ),
        check_vma=False,
    )
```
